32 devices in a mesh: dp: 16 (over z, y, core), branch: 2 (over x).
Axes of the slice: x: 2, y: 2, z: 4, core: 2. Of those that a mesh axis runs over, the one named last changes fastest.
Arguments:
- hidden: bfloat16 [24576, 768], P('dp'), may hold values from -6 to 6
- segment_ids: int32 [48, 512], P('dp'), may hold values from 0 to 3, never falling along the last dimension, each value on 1 to 256 neighbouring positions
- query_weight: bfloat16 [768, 384], replicated, may hold values from -0.21875 to 0.21875
- query_bias: bfloat16 [384], replicated, may hold values from -3 to 3
- key_weight: bfloat16 [768, 384], replicated, may hold values from -0.21875 to 0.21875
- value_weight: bfloat16 [768, 384], replicated, may hold values from -0.21875 to 0.21875
- value_bias: bfloat16 [384], replicated, may hold values from -3 to 3
- depthwise_weight: bfloat16 [9, 768], replicated, may hold values from -2 to 2
- pointwise_weight: bfloat16 [768, 384], replicated, may hold values from -0.21875 to 0.21875
- pointwise_bias: bfloat16 [384], replicated, may hold values from -3 to 3
- kernel_weight: bfloat16 [384, 54], replicated, may hold values from -0.3125 to 0.3125
- kernel_bias: bfloat16 [54], replicated, may hold values from -4 to 4
- conv_value_weight: bfloat16 [768, 384], replicated, may hold values from -0.21875 to 0.21875
- conv_value_bias: bfloat16 [384], replicated, may hold values from -3 to 3
- output_weight: bfloat16 [768, 768], replicated, may hold values from -0.75 to 0.75
- output_bias: bfloat16 [768], replicated, may hold values from -3 to 3
- norm1_gain: bfloat16 [768], replicated, may hold values from 0.25 to 1.75
- norm1_shift: bfloat16 [768], replicated, may hold values from -3 to 3
- ffn_in_weight: bfloat16 [2, 384, 1536], replicated, may hold values from -0.3125 to 0.3125
- ffn_in_bias: bfloat16 [3072], replicated, may hold values from -3 to 3
- ffn_out_weight: bfloat16 [2, 1536, 384], replicated, may hold values from -0.15625 to 0.15625
- ffn_out_bias: bfloat16 [768], replicated, may hold values from -3 to 3
- norm2_gain: bfloat16 [768], replicated, may hold values from 0.25 to 1.75
- norm2_shift: bfloat16 [768], replicated, may hold values from -3 to 3
- cotangent: bfloat16 [24576, 768], P(('dp', 'branch')), may hold values from -6 to 6
Outputs:
- layer_out: bfloat16 [24576, 768], P(('dp', 'branch'))
- input_grad: float32 [24576, 768], P(('dp', 'branch'))
- query_weight_grad: float32 [768, 384], P(('dp', 'branch'))
- query_bias_grad: float32 [384], replicated
- key_weight_grad: float32 [768, 384], P(('dp', 'branch'))
- value_weight_grad: float32 [768, 384], P(('dp', 'branch'))
- value_bias_grad: float32 [384], replicated
- depthwise_weight_grad: float32 [9, 768], P(None, ('dp', 'branch'))
- pointwise_weight_grad: float32 [768, 384], P(('dp', 'branch'))
- pointwise_bias_grad: float32 [384], replicated
- kernel_weight_grad: float32 [384, 54], replicated
- kernel_bias_grad: float32 [54], replicated
- conv_value_weight_grad: float32 [768, 384], P(('dp', 'branch'))
- conv_value_bias_grad: float32 [384], replicated
- output_weight_grad: float32 [768, 768], P(('dp', 'branch'))
- output_bias_grad: float32 [768], replicated
- norm1_gain_grad: float32 [768], replicated
- norm1_shift_grad: float32 [768], replicated
- ffn_in_weight_grad: float32 [2, 384, 1536], P(None, None, ('dp', 'branch'))
- ffn_in_bias_grad: float32 [3072], replicated
- ffn_out_weight_grad: float32 [2, 1536, 384], P(None, ('dp', 'branch'))
- ffn_out_bias_grad: float32 [768], replicated
- norm2_gain_grad: float32 [768], replicated
- norm2_shift_grad: float32 [768], replicated
The draws below stay inside these ranges and needn't reach their ends.
Inputs may be any that keep to these rules, and one draw needn't show every extreme that they name: `segment_ids`: within a packed row the ids never fall; a document holds at most 256 tokens.
All inputs are finite; a program needn't handle non-finite values.
Results may differ from the reference program's by a relative error of at most 0.015.
Values may be sent and summed in bfloat16 or wider, within the bound.
A program may use at most 192 MiB of HBM per device.

```python
import math
import jax
import jax.numpy as jnp
import numpy as np
from jax import lax

D = 768
HEADS = 6
HEAD_DIM = 64
KERNEL = 9
FF = 3072
GROUPS = 2
SEQ_LEN = 512
ROWS = 48
TOKENS = 24576


def levels(rng, shape, shards, least, largest):
    def one(position, blocks):
        steps = jax.random.uniform(jax.random.fold_in(jax.random.fold_in(rng, 6), position), (blocks,), jnp.float32, least / len(shards), largest / len(shards))
        return jnp.repeat(jnp.exp(steps), shape[position] // blocks).reshape((-1,) + (1,) * (len(shape) - position - 1))

    factor_of = one(*shards[0])
    for cut in shards[1:]:
        factor_of = factor_of * one(*cut)
    return factor_of


def length_profile(number_of, total, limit, slope):
    loads = [(1 << 20) // math.isqrt(rank ** slope) + 1 for rank in range(2, number_of + 1)]
    rest, counts = total - limit - (number_of - 1), [1] * (number_of - 1)
    while rest > 0:
        free = [i for i in range(number_of - 1) if counts[i] < limit]
        pool, left = sum([loads[i] for i in free]), rest
        for i in free:
            extra = min(limit - counts[i], max(1, left * loads[i] // pool), rest)
            counts[i] = counts[i] + extra
            rest = rest - extra
    return np.array([limit] + counts)


def ragged(own_key, number_of, total, limit, slope):
    if number_of == 2:
        one = jax.random.randint(own_key, (), max(1, total - limit), min(limit, total - 1) + 1)
        return jnp.stack([one, total - one])
    tallies = jnp.asarray(length_profile(number_of, total, limit, slope), jnp.int32)
    couples = (number_of - 1) // 2
    giver, sink = tallies[1:1 + 2 * couples:2], tallies[2:2 + 2 * couples:2]
    margin = jnp.minimum(giver - 1, limit - sink)
    passed = jax.random.randint(jax.random.fold_in(own_key, 1), (couples,), 0, 1 << 20) % (margin + 1)
    tallies = tallies.at[1:1 + 2 * couples:2].set(giver - passed).at[2:2 + 2 * couples:2].set(sink + passed)
    return tallies[jax.random.permutation(jax.random.fold_in(own_key, 2), number_of)]


def centred(stream_key, extent, spread, bound, split=(), dtype=jnp.bfloat16):
    values = jax.random.normal(stream_key, extent, jnp.float32) * spread
    if len(split) > 0:
        values = levels(stream_key, extent, split, -0.22, 0.18) * values
    return jnp.clip(values, min=-bound, max=bound).astype(dtype)


def setup_inputs(seed: int = 0) -> dict:
    splits = jax.random.split(jax.random.key(seed), 26)
    hidden = centred(splits[0], (TOKENS, D), 1.0, 6.0, ((0, 16),))
    segment_ids = jax.vmap(lambda own: jnp.searchsorted(jnp.cumsum(ragged(own, 4, SEQ_LEN, SEQ_LEN // 2, 2)), jnp.arange(SEQ_LEN), side="right"))(jax.random.split(splits[1], ROWS)).reshape((ROWS, SEQ_LEN)).astype(jnp.int32)
    query_weight = centred(splits[2], (D, HEADS * HEAD_DIM), D ** -0.5, 0.21875)
    query_bias = centred(splits[3], (HEADS * HEAD_DIM,), 0.5, 3.0)
    key_weight = centred(splits[4], (D, HEADS * HEAD_DIM), D ** -0.5, 0.21875)
    value_weight = centred(splits[5], (D, HEADS * HEAD_DIM), D ** -0.5, 0.21875)
    value_bias = centred(splits[6], (HEADS * HEAD_DIM,), 0.5, 3.0)
    depthwise_weight = centred(splits[7], (KERNEL, D), KERNEL ** -0.5, 2.0)
    pointwise_weight = centred(splits[8], (D, HEADS * HEAD_DIM), D ** -0.5, 0.21875)
    pointwise_bias = centred(splits[9], (HEADS * HEAD_DIM,), 0.5, 3.0)
    kernel_weight = centred(splits[10], (HEADS * HEAD_DIM, HEADS * KERNEL), (HEADS * HEAD_DIM) ** -0.5, 0.3125)
    kernel_bias = centred(splits[11], (HEADS * KERNEL,), 1.0, 4.0)
    conv_value_weight = centred(splits[12], (D, HEADS * HEAD_DIM), D ** -0.5, 0.21875)
    conv_value_bias = centred(splits[13], (HEADS * HEAD_DIM,), 0.5, 3.0)
    output_weight = centred(splits[14], (D, D), 64 ** -0.5, 0.75)
    output_bias = centred(splits[15], (D,), 0.5, 3.0)
    norm1_gain = jnp.clip(1.0 + 0.15 * jax.random.normal(splits[16], (D,), jnp.float32), 0.25, 1.75).astype(jnp.bfloat16)
    norm1_shift = centred(splits[17], (D,), 0.5, 3.0)
    ffn_in_weight = centred(splits[18], (GROUPS, D // GROUPS, FF // GROUPS), (D // GROUPS) ** -0.5, 0.3125)
    ffn_in_bias = centred(splits[19], (FF,), 0.5, 3.0)
    ffn_out_weight = centred(splits[20], (GROUPS, FF // GROUPS, D // GROUPS), (FF // GROUPS) ** -0.5, 0.15625)
    ffn_out_bias = centred(splits[21], (D,), 0.5, 3.0)
    norm2_gain = jnp.clip(1.0 + 0.15 * jax.random.normal(splits[22], (D,), jnp.float32), 0.25, 1.75).astype(jnp.bfloat16)
    norm2_shift = centred(splits[23], (D,), 0.5, 3.0)
    cotangent = centred(splits[24], (TOKENS, D), 1.0, 6.0, ((0, 32),))
    return dict(hidden=hidden, segment_ids=segment_ids, query_weight=query_weight, query_bias=query_bias, key_weight=key_weight, value_weight=value_weight, value_bias=value_bias, depthwise_weight=depthwise_weight, pointwise_weight=pointwise_weight, pointwise_bias=pointwise_bias, kernel_weight=kernel_weight, kernel_bias=kernel_bias, conv_value_weight=conv_value_weight, conv_value_bias=conv_value_bias, output_weight=output_weight, output_bias=output_bias, norm1_gain=norm1_gain, norm1_shift=norm1_shift, ffn_in_weight=ffn_in_weight, ffn_in_bias=ffn_in_bias, ffn_out_weight=ffn_out_weight, ffn_out_bias=ffn_out_bias, norm2_gain=norm2_gain, norm2_shift=norm2_shift, cotangent=cotangent)


@jax.custom_vjp
def low(v):
    return lax.optimization_barrier(v.astype(jnp.bfloat16)).astype(jnp.float32)

@jax.custom_vjp
def low_back(v):
    return v

def low_keep(v):
    return (low(v), None)

def low_pass(kept, grad):
    return (grad,)

def back_keep(v):
    return (v, None)

def back_low(kept, grad):
    return (low(grad),)
low.defvjp(low_keep, low_pass)
low_back.defvjp(back_keep, back_low)
precise = lax.Precision.HIGHEST
norm_eps = 1e-12

def matmul(first_op, second_op):
    return jnp.dot(first_op, second_op, precision=precise)

def layer_norm(values, gain, shift):
    average = lax.optimization_barrier(jnp.mean(values, axis=-1, keepdims=True))
    centered = values - average
    variance = lax.optimization_barrier(jnp.mean(centered * centered, axis=-1, keepdims=True))
    return centered * lax.rsqrt(variance + norm_eps) * gain + shift

def grouped(values, weight):
    groups, inner_width, outer_width = weight.shape
    pieces = values.reshape(values.shape[0], groups, inner_width)
    result = jnp.einsum('ngi,gio->ngo', pieces, weight, precision=precise)
    return result.reshape(values.shape[0], groups * outer_width)

def tap_masks(segments):
    reach = KERNEL // 2
    length = segments.shape[1]
    padded = jnp.pad(segments, ((0, 0), (reach, reach)), constant_values=-1)
    return [(padded[:, j:j + length] == segments).astype(jnp.float32) for j in range(KERNEL)]

def forward(hidden, segments, params):
    query_weight, query_bias, key_weight, value_weight, value_bias, depthwise_weight, pointwise_weight, pointwise_bias, kernel_weight, kernel_bias, conv_value_weight, conv_value_bias, output_weight, output_bias, norm1_gain, norm1_shift, ffn_in_weight, ffn_in_bias, ffn_out_weight, ffn_out_bias, norm2_gain, norm2_shift = params
    row_count, length = segments.shape
    token_count = row_count * length
    reach = KERNEL // 2
    head_shape = (row_count, length, HEADS, HEAD_DIM)
    query_pre = matmul(hidden, query_weight) + query_bias
    query_attn = low(low_back(query_pre))
    query_conv = low_back(query_pre)
    keys_low = low(low_back(matmul(hidden, key_weight)))
    values_low = low(low_back(matmul(hidden, value_weight) + value_bias))
    scores = jnp.einsum('rqhd,rkhd->rhqk', query_attn.reshape(head_shape), keys_low.reshape(head_shape), precision=precise)
    scores = low_back(scores * HEAD_DIM ** (-0.5))
    same_segment = segments[:, :, None] == segments[:, None, :]
    attn_probs = jax.nn.softmax(jnp.where(same_segment[:, None], scores, -1e+30), axis=-1)
    context = jnp.einsum('rhqk,rkhd->rqhd', low(attn_probs), values_low.reshape(head_shape), precision=precise)
    context = low(low_back(context.reshape(token_count, HEADS * HEAD_DIM)))
    tap_list = tap_masks(segments)
    padded_grid = jnp.pad(hidden.reshape(row_count, length, -1), ((0, 0), (reach, reach), (0, 0)))
    depthwise = sum((depthwise_weight[j] * padded_grid[:, j:j + length] * tap_list[j][:, :, None] for j in range(KERNEL)))
    depth_low = low(depthwise.reshape(token_count, -1))
    key_conv = low_back(matmul(depth_low, pointwise_weight) + pointwise_bias)
    conv_attn = low(low_back(key_conv * query_conv))
    kernel_logits = low_back(matmul(conv_attn, kernel_weight) + kernel_bias)
    conv_kernel = jax.nn.softmax(kernel_logits.reshape(row_count, length, HEADS, KERNEL), axis=-1)
    conv_values = low_back(matmul(hidden, conv_value_weight) + conv_value_bias)
    value_grid = jnp.pad(conv_values.reshape(head_shape), ((0, 0), (reach, reach), (0, 0), (0, 0)))
    conv_out = sum((conv_kernel[..., j, None] * value_grid[:, j:j + length] * tap_list[j][:, :, None, None] for j in range(KERNEL)))
    conv_out = low(low_back(conv_out.reshape(token_count, HEADS * HEAD_DIM)))
    joined = jnp.concatenate([context, conv_out], axis=-1)
    attn_out = low_back(matmul(joined, output_weight) + output_bias)
    normed = layer_norm(hidden + attn_out, norm1_gain, norm1_shift)
    inner_act = low_back(grouped(low(normed), ffn_in_weight) + ffn_in_bias)
    activated = low(jax.nn.gelu(inner_act, approximate=False))
    outer_act = low_back(grouped(activated, ffn_out_weight) + ffn_out_bias)
    return layer_norm(normed + outer_act, norm2_gain, norm2_shift)

def reference(hidden, segment_ids, query_weight, query_bias, key_weight, value_weight, value_bias, depthwise_weight, pointwise_weight, pointwise_bias, kernel_weight, kernel_bias, conv_value_weight, conv_value_bias, output_weight, output_bias, norm1_gain, norm1_shift, ffn_in_weight, ffn_in_bias, ffn_out_weight, ffn_out_bias, norm2_gain, norm2_shift, cotangent):
    params = tuple((item.astype(jnp.float32) for item in (query_weight, query_bias, key_weight, value_weight, value_bias, depthwise_weight, pointwise_weight, pointwise_bias, kernel_weight, kernel_bias, conv_value_weight, conv_value_bias, output_weight, output_bias, norm1_gain, norm1_shift, ffn_in_weight, ffn_in_bias, ffn_out_weight, ffn_out_bias, norm2_gain, norm2_shift)))
    per_block = math.gcd(ROWS, max(1, 4096 // SEQ_LEN))
    blocks = ROWS // per_block
    span = per_block * SEQ_LEN
    hidden_blocks = hidden.astype(jnp.float32).reshape(blocks, span, D)
    segment_blocks = segment_ids.reshape(blocks, per_block, SEQ_LEN)
    cotangent_blocks = cotangent.astype(jnp.float32).reshape(blocks, span, D)

    def one_block(totals, inputs):
        hidden_block, segment_block, cotangent_block = inputs
        result, pullback = jax.vjp(lambda state, weights: forward(state, segment_block, weights), hidden_block, params)
        block_input_grad, param_grads = pullback(cotangent_block)
        totals = tuple((first + second for first, second in zip(totals, param_grads)))
        return (totals, (result.astype(jnp.bfloat16), block_input_grad))
    zeros = tuple((jnp.zeros_like(item) for item in params))
    totals, (outputs, input_grads) = lax.scan(one_block, zeros, (hidden_blocks, segment_blocks, cotangent_blocks))
    grad_qw, grad_qb, grad_kw, grad_vw, grad_vb, grad_dw, grad_pw, grad_pb, grad_kern_w, grad_kern_b, grad_cvw, grad_cvb, grad_ow, grad_ob, grad_g1, grad_n1, grad_w1, grad_b1, grad_w2, grad_b2, grad_g2, grad_n2 = totals
    return (outputs.reshape(TOKENS, D), input_grads.reshape(TOKENS, D), grad_qw, grad_qb, grad_kw, grad_vw, grad_vb, grad_dw, grad_pw, grad_pb, grad_kern_w, grad_kern_b, grad_cvw, grad_cvb, grad_ow, grad_ob, grad_g1, grad_n1, grad_w1, grad_b1, grad_w2, grad_b2, grad_g2, grad_n2)
```

```python
import functools
import math

import jax
import jax.numpy as jnp
from jax import lax
from jax.experimental import pallas as pl
from jax.experimental.pallas import tpu as pltpu
from jax.sharding import PartitionSpec as P

MESH = pl.DeviceIdType.MESH
CHUNK = 48

def comm_plan(dp_size):
    bits = int(math.log2(dp_size)) + 1
    extra = max(0, bits - 5)
    return bits, extra

def orders(bits, extra):
    halving = list(range(extra, bits))
    first = [1] if 1 in halving else []
    rest = [b for b in halving if b not in first]
    if len(rest) >= 4:
        a = [rest[0], rest[2], rest[1]] + rest[3:]
        b = [rest[1], rest[2], rest[0]] + rest[3:]
    else:
        a, b = rest, rest[::-1]
    ex = list(range(extra))
    return (first + a), (first + b), ex

def comm_kernel(dp_size, rows, g_ref, s_ref, out_ref, sout_ref, rb, srb, erb, send, recv, ssend, srecv, esend, erecv):
    bits, extra = comm_plan(dp_size)
    order_a, order_b, ex = orders(bits, extra)
    nh = len(order_a)
    dp = lax.axis_index("dp")
    br = lax.axis_index("branch")
    my = [br] + [lax.rem(lax.div(dp, 1 << (k - 1)), 2) for k in range(1, bits)]

    def partner(k):
        if k == 0:
            return (dp, 1 - br)
        return (dp + (1 << (k - 1)) * (1 - 2 * my[k]), br)

    barrier = pltpu.get_barrier_semaphore()
    for k in range(bits):
        pl.semaphore_signal(barrier, inc=1, device_id=partner(k), device_id_type=MESH)
    pl.semaphore_wait(barrier, bits)

    n_chunks = rows // CHUNK

    def axis_of(k):
        return bits - 1 - k

    pending = {}

    def start(c, s, order):
        fixed = {k: my[k] for k in order[:s]}
        k = order[s]
        fixed[k] = 1 - my[k]
        left = nh - 1 - s
        off = sum(1 << (nh - 1 - t) for t in range(s))
        free = [i for i in range(nh) if (bits - 1 - i) not in fixed]
        copies = []
        total = 1 << left
        for u in range(total):
            idx = []
            pos = 0
            for i in range(nh):
                kk = bits - 1 - i
                if kk in fixed:
                    idx.append(fixed[kk])
                else:
                    idx.append((u >> (left - 1 - pos)) & 1)
                    pos += 1
            cp = pltpu.make_async_remote_copy(
                src_ref=g_ref.at[tuple(idx) + (pl.ds(c * CHUNK, CHUNK),)],
                dst_ref=rb.at[c, off + u],
                send_sem=send.at[c, s], recv_sem=recv.at[c, s],
                device_id=partner(k), device_id_type=MESH)
            cp.start()
        whole = pltpu.make_async_remote_copy(
            src_ref=rb.at[c, pl.ds(off, total)], dst_ref=rb.at[c, pl.ds(off, total)],
            send_sem=send.at[c, s], recv_sem=recv.at[c, s],
            device_id=partner(k), device_id_type=MESH)
        pending[(c, s)] = whole

    def add(c, s, order):
        pending[(c, s)].wait_recv()
        left = nh - 1 - s
        off = sum(1 << (nh - 1 - t) for t in range(s))
        fixed = {k: my[k] for k in order[:s + 1]}
        for u in range(1 << left):
            idx = []
            pos = 0
            for i in range(nh):
                kk = bits - 1 - i
                if kk in fixed:
                    idx.append(fixed[kk])
                else:
                    idx.append((u >> (left - 1 - pos)) & 1)
                    pos += 1
            at = tuple(idx) + (pl.ds(c * CHUNK, CHUNK),)
            tot = g_ref[at].astype(jnp.float32) + rb[c, off + u].astype(jnp.float32)
            if s == nh - 1:
                out_ref[pl.ds(c * CHUNK, CHUNK), :] = tot
            else:
                g_ref[at] = tot.astype(g_ref.dtype)

    def small_start(s, k):
        cp = pltpu.make_async_remote_copy(
            src_ref=sout_ref, dst_ref=srb.at[s], send_sem=ssend.at[s], recv_sem=srecv.at[s],
            device_id=partner(k), device_id_type=MESH)
        cp.start()
        pending[("s", s)] = cp

    sout_ref[...] = s_ref[...]
    small_order = order_a + ex
    half = n_chunks // 2
    for w in range(half + nh):
        for p in range(half - 1, -1, -1):
            s = w - p
            for col, order in ((0, order_a), (1, order_b)):
                c = 2 * p + col
                if 1 <= s <= nh:
                    add(c, s - 1, order)
                if 0 <= s < nh:
                    start(c, s, order)
        if w >= 1 and w <= bits:
            pending[("s", w - 1)].wait()
            sout_ref[...] = sout_ref[...] + srb[w - 1]
        if w < bits:
            small_start(w, small_order[w])
    for w in range(half + nh, bits + 1):
        pending[("s", w - 1)].wait()
        sout_ref[...] = sout_ref[...] + srb[w - 1]
        if w < bits:
            small_start(w, small_order[w])
    for i, k in enumerate(ex):
        cp = pltpu.make_async_remote_copy(
            src_ref=out_ref, dst_ref=erb.at[i], send_sem=esend.at[i], recv_sem=erecv.at[i],
            device_id=partner(k), device_id_type=MESH)
        cp.start()
        cp.wait()
        out_ref[...] = out_ref[...] + erb[i]
    for c in range(n_chunks):
        for s in range(nh):
            pending[(c, s)].wait_send()

def comm_call(dp_size, g, s):
    bits, extra = comm_plan(dp_size)
    nh = bits - extra
    rows = g.shape[-2]
    n_chunks = rows // CHUNK
    gg = g.reshape((2,) * nh + g.shape[-2:])
    vm = pl.BlockSpec(memory_space=pltpu.VMEM)
    return pl.pallas_call(
        functools.partial(comm_kernel, dp_size, rows),
        out_shape=(jax.ShapeDtypeStruct((rows, g.shape[-1]), jnp.float32),
                   jax.ShapeDtypeStruct(s.shape, jnp.float32)),
        in_specs=[vm, vm], out_specs=(vm, vm),
        scratch_shapes=[
            pltpu.VMEM((n_chunks, (1 << nh) - 1, CHUNK, g.shape[-1]), jnp.bfloat16),
            pltpu.VMEM((bits,) + s.shape, jnp.float32),
            pltpu.VMEM((max(extra, 1), rows if extra else 8, g.shape[-1]), jnp.float32),
            pltpu.SemaphoreType.DMA((n_chunks, nh)),
            pltpu.SemaphoreType.DMA((n_chunks, nh)),
            pltpu.SemaphoreType.DMA((bits,)),
            pltpu.SemaphoreType.DMA((bits,)),
            pltpu.SemaphoreType.DMA((max(extra, 1),)),
            pltpu.SemaphoreType.DMA((max(extra, 1),)),
        ],
        compiler_params=pltpu.CompilerParams(collective_id=0, has_side_effects=True, vmem_limit_bytes=60 << 20),
        name="grad_reduce",
    )(gg, s)

D = 768
HEADS = 6
HEAD_DIM = 64
KERNEL = 9


norm_eps = 1e-12
lowered = jnp.bfloat16


def matmul(first_op, second_op):
    return jnp.dot(first_op, second_op, preferred_element_type=jnp.float32)


def matmul_left(first_op, second_op):
    return lax.dot_general(
        first_op, second_op, (((0,), (0,)), ((), ())), preferred_element_type=jnp.float32
    )


def matmul_right(first_op, second_op):
    return lax.dot_general(
        first_op, second_op, (((1,), (1,)), ((), ())), preferred_element_type=jnp.float32
    )


def column_sums(values):
    return jnp.sum(values.astype(jnp.float32), axis=0)


def layer_norm(values, gain, shift):
    average = jnp.mean(values, axis=-1, keepdims=True)
    centered = values - average
    variance = jnp.mean(centered * centered, axis=-1, keepdims=True)
    return centered * lax.rsqrt(variance + norm_eps) * gain + shift


def gelu_exact(values):
    return jax.nn.gelu(values, approximate=False)


def grouped_forward(values, weight):
    groups, inner_width, outer_width = weight.shape
    pieces = values.reshape(values.shape[0], groups, inner_width)
    result = jnp.einsum("ngi,gio->ngo", pieces, weight, preferred_element_type=jnp.float32)
    return result.reshape(values.shape[0], groups * outer_width)


def grouped_input_grad(grads, weight):
    groups, inner_width, outer_width = weight.shape
    pieces = grads.reshape(grads.shape[0], groups, outer_width)
    result = jnp.einsum("ngo,gio->ngi", pieces, weight, preferred_element_type=jnp.float32)
    return result.reshape(grads.shape[0], groups * inner_width)


def tap_masks(segments):
    reach = KERNEL // 2
    length = segments.shape[1]
    padded = jnp.pad(segments, ((0, 0), (reach, reach)), constant_values=-1)
    return [(padded[:, j : j + length] == segments).astype(jnp.float32) for j in range(KERNEL)]


def spread_back(terms, length):
    reach = KERNEL // 2
    pad_spec = ((0, 0), (reach, reach)) + ((0, 0),) * (terms[0].ndim - 2)
    return sum(
        (
            jnp.pad(terms[j], pad_spec)[:, 2 * reach - j : 2 * reach - j + length]
            for j in range(KERNEL)
        )
    )


def attention_inputs(hidden, head_shape, weights):
    query_weight, query_bias, key_weight, value_weight, value_bias = weights
    queries = (matmul(hidden, query_weight) + query_bias).astype(lowered).reshape(head_shape)
    keys_low = matmul(hidden, key_weight).astype(lowered).reshape(head_shape)
    values_low = (matmul(hidden, value_weight) + value_bias).astype(lowered).reshape(head_shape)
    return (queries, keys_low, values_low)


def masked_scores(query_seq, key_seq, segment_seq):
    scores = jnp.einsum(
        "qhd,khd->hqk", query_seq, key_seq, preferred_element_type=jnp.float32
    ) * HEAD_DIM ** (-0.5)
    same_segment = segment_seq[:, None] == segment_seq[None, :]
    return jnp.where(same_segment[None], scores, -1e30)


def attention_forward(hidden, segments, weights):
    row_count, length = segments.shape
    head_shape = (row_count, length, HEADS, HEAD_DIM)
    queries, keys_low, values_low = attention_inputs(hidden, head_shape, weights)

    def per_sequence(inputs):
        query_seq, key_seq, value_seq, segment_seq = inputs
        scores = masked_scores(query_seq, key_seq, segment_seq)
        row_peak = jnp.max(scores, axis=-1, keepdims=True)
        exponent = jnp.exp(scores - row_peak)
        row_sum = jnp.sum(exponent, axis=-1, keepdims=True)
        probs_low = (exponent / row_sum).astype(lowered)
        context = jnp.einsum(
            "hqk,khd->qhd", probs_low, value_seq, preferred_element_type=jnp.float32
        )
        return (context.astype(lowered), (row_peak + jnp.log(row_sum))[..., 0])

    context, log_sums = lax.map(per_sequence, (queries, keys_low, values_low, segments))
    return (context.reshape(row_count * length, HEADS * HEAD_DIM), log_sums)


def attention_backward(hidden, segments, weights, log_sums, context_grad):
    query_weight, query_bias, key_weight, value_weight, value_bias = weights
    row_count, length = segments.shape
    token_count = row_count * length
    head_shape = (row_count, length, HEADS, HEAD_DIM)
    queries, keys_low, values_low = attention_inputs(hidden, head_shape, weights)
    scale = HEAD_DIM ** (-0.5)

    def per_sequence(inputs):
        query_seq, key_seq, value_seq, segment_seq, log_seq, grad_seq = inputs
        scores = masked_scores(query_seq, key_seq, segment_seq)
        attn_probs = jnp.exp(scores - log_seq[..., None])
        probs_low = attn_probs.astype(lowered)
        value_grad = jnp.einsum(
            "hqk,qhd->khd", probs_low, grad_seq, preferred_element_type=jnp.float32
        )
        prob_grad = jnp.einsum(
            "qhd,khd->hqk", grad_seq, value_seq, preferred_element_type=jnp.float32
        )
        score_grad = attn_probs * (
            prob_grad - jnp.sum(prob_grad * attn_probs, axis=-1, keepdims=True)
        )
        score_low = score_grad.astype(lowered)
        query_grad = (
            jnp.einsum("hqk,khd->qhd", score_low, key_seq, preferred_element_type=jnp.float32)
            * scale
        )
        key_grad = (
            jnp.einsum("hqk,qhd->khd", score_low, query_seq, preferred_element_type=jnp.float32)
            * scale
        )
        return (query_grad.astype(lowered), key_grad.astype(lowered), value_grad.astype(lowered))

    grad_heads = context_grad.reshape(head_shape)
    query_low, key_low, value_low = lax.map(
        per_sequence, (queries, keys_low, values_low, segments, log_sums, grad_heads)
    )
    width = HEADS * HEAD_DIM
    query_low = query_low.reshape(token_count, width)
    key_low = key_low.reshape(token_count, width)
    value_low = value_low.reshape(token_count, width)
    input_part = (
        matmul_right(query_low, query_weight)
        + matmul_right(key_low, key_weight)
        + matmul_right(value_low, value_weight)
    )
    zero_wide = jnp.zeros((D, width), jnp.float32)
    zero_vector = jnp.zeros((width,), jnp.float32)
    big_grads = (
        matmul_left(hidden, query_low),
        matmul_left(hidden, key_low),
        matmul_left(hidden, value_low),
        jnp.zeros((D, KERNEL), jnp.float32),
        zero_wide,
        zero_wide,
    )
    small_grads = (
        column_sums(query_low),
        column_sums(value_low),
        zero_vector,
        jnp.zeros((width, HEADS * KERNEL), jnp.float32),
        jnp.zeros((HEADS * KERNEL,), jnp.float32),
        zero_vector,
    )
    return (input_part, big_grads, small_grads)


def conv_pieces(hidden, segments, weights):
    (
        query_weight,
        query_bias,
        depthwise_weight,
        pointwise_weight,
        pointwise_bias,
        kernel_weight,
        kernel_bias,
        conv_value_weight,
        conv_value_bias,
    ) = weights
    row_count, length = segments.shape
    token_count = row_count * length
    reach = KERNEL // 2
    tap_list = tap_masks(segments)
    padded_grid = jnp.pad(hidden.reshape(row_count, length, D), ((0, 0), (reach, reach), (0, 0)))
    depthwise = sum(
        (
            depthwise_weight[j].astype(jnp.float32)
            * padded_grid[:, j : j + length]
            * tap_list[j][:, :, None]
            for j in range(KERNEL)
        )
    )
    depth_low = depthwise.reshape(token_count, D).astype(lowered)
    query_pre = matmul(hidden, query_weight) + query_bias
    key_conv = matmul(depth_low, pointwise_weight) + pointwise_bias
    conv_attn = (key_conv * query_pre).astype(lowered)
    kernel_logits = matmul(conv_attn, kernel_weight) + kernel_bias
    conv_kernel = jax.nn.softmax(kernel_logits.reshape(row_count, length, HEADS, KERNEL), axis=-1)
    conv_values = (matmul(hidden, conv_value_weight) + conv_value_bias).reshape(
        row_count, length, HEADS, HEAD_DIM
    )
    value_grid = jnp.pad(conv_values, ((0, 0), (reach, reach), (0, 0), (0, 0)))
    conv_out = sum(
        (
            conv_kernel[..., j, None]
            * value_grid[:, j : j + length]
            * tap_list[j][:, :, None, None]
            for j in range(KERNEL)
        )
    )
    return (
        tap_list,
        padded_grid,
        depth_low,
        query_pre,
        key_conv,
        conv_attn,
        conv_kernel,
        value_grid,
        conv_out,
    )


def conv_forward(hidden, segments, weights):
    row_count, length = segments.shape
    conv_out = conv_pieces(hidden, segments, weights)[-1]
    return (
        conv_out.reshape(row_count * length, HEADS * HEAD_DIM).astype(lowered),
        jnp.zeros((row_count, HEADS, length), jnp.float32),
    )


def conv_backward(hidden, segments, weights, conv_grad):
    (
        query_weight,
        query_bias,
        depthwise_weight,
        pointwise_weight,
        pointwise_bias,
        kernel_weight,
        kernel_bias,
        conv_value_weight,
        conv_value_bias,
    ) = weights
    row_count, length = segments.shape
    token_count = row_count * length
    width = HEADS * HEAD_DIM
    (
        tap_list,
        padded_grid,
        depth_low,
        query_pre,
        key_conv,
        conv_attn,
        conv_kernel,
        value_grid,
        conv_out,
    ) = conv_pieces(hidden, segments, weights)
    upstream = conv_grad.astype(jnp.float32).reshape(row_count, length, HEADS, HEAD_DIM)
    kernel_grad = jnp.stack(
        [
            jnp.sum(upstream * value_grid[:, j : j + length], axis=-1) * tap_list[j][:, :, None]
            for j in range(KERNEL)
        ],
        axis=-1,
    )
    value_terms = [
        conv_kernel[..., j, None] * tap_list[j][:, :, None, None] * upstream for j in range(KERNEL)
    ]
    conv_value_low = spread_back(value_terms, length).reshape(token_count, width).astype(lowered)
    logit_grad = conv_kernel * (
        kernel_grad - jnp.sum(kernel_grad * conv_kernel, axis=-1, keepdims=True)
    )
    logit_low = logit_grad.reshape(token_count, HEADS * KERNEL).astype(lowered)
    span_low = matmul_right(logit_low, kernel_weight).astype(lowered)
    span_full = span_low.astype(jnp.float32)
    key_conv_low = (span_full * query_pre).astype(lowered)
    query_conv_low = (span_full * key_conv).astype(lowered)
    depth_grad = matmul_right(key_conv_low, pointwise_weight).reshape(row_count, length, D)
    depthwise_grad = jnp.stack(
        [
            jnp.sum(
                padded_grid[:, j : j + length] * tap_list[j][:, :, None] * depth_grad, axis=(0, 1)
            )
            for j in range(KERNEL)
        ],
        axis=-1,
    )
    depth_terms = [
        depthwise_weight[j].astype(jnp.float32) * tap_list[j][:, :, None] * depth_grad
        for j in range(KERNEL)
    ]
    input_part = (
        matmul_right(query_conv_low, query_weight)
        + matmul_right(conv_value_low, conv_value_weight)
        + spread_back(depth_terms, length).reshape(token_count, D)
    )
    zero_wide = jnp.zeros((D, width), jnp.float32)
    big_grads = (
        matmul_left(hidden, query_conv_low),
        zero_wide,
        zero_wide,
        depthwise_grad,
        matmul_left(depth_low, key_conv_low),
        matmul_left(hidden, conv_value_low),
    )
    small_grads = (
        column_sums(query_conv_low),
        jnp.zeros((width,), jnp.float32),
        column_sums(key_conv_low),
        matmul_left(conv_attn, logit_low),
        column_sums(logit_low),
        column_sums(conv_value_low),
    )
    return (input_part, big_grads, small_grads)


def local(
    hidden,
    segment_ids,
    query_weight,
    query_bias,
    key_weight,
    value_weight,
    value_bias,
    depthwise_weight,
    pointwise_weight,
    pointwise_bias,
    kernel_weight,
    kernel_bias,
    conv_value_weight,
    conv_value_bias,
    output_weight,
    output_bias,
    norm1_gain,
    norm1_shift,
    ffn_in_weight,
    ffn_in_bias,
    ffn_out_weight,
    ffn_out_bias,
    norm2_gain,
    norm2_shift,
    cotangent,
):
    branch_index = lax.axis_index("branch")
    attend_weights = (query_weight, query_bias, key_weight, value_weight, value_bias)
    conv_weights = (
        query_weight,
        query_bias,
        depthwise_weight,
        pointwise_weight,
        pointwise_bias,
        kernel_weight,
        kernel_bias,
        conv_value_weight,
        conv_value_bias,
    )
    context, log_sums = lax.cond(
        branch_index == 0,
        lambda operands: attention_forward(operands[0], operands[1], attend_weights),
        lambda operands: conv_forward(operands[0], operands[1], conv_weights),
        (hidden, segment_ids),
    )
    joined = lax.all_to_all(context, "branch", split_axis=0, concat_axis=1, tiled=True)
    own_count = joined.shape[0]
    own_hidden = lax.dynamic_slice_in_dim(hidden, branch_index * own_count, own_count, 0)
    residual = own_hidden.astype(jnp.float32) + matmul(joined, output_weight) + output_bias
    normed, norm1_back = jax.vjp(
        layer_norm, residual, norm1_gain.astype(jnp.float32), norm1_shift.astype(jnp.float32)
    )
    normed_low = normed.astype(lowered)
    inner_act = grouped_forward(normed_low, ffn_in_weight) + ffn_in_bias
    activated, gelu_back = jax.vjp(gelu_exact, inner_act)
    active_low = activated.astype(lowered)
    summed = normed + grouped_forward(active_low, ffn_out_weight) + ffn_out_bias
    result, norm2_back = jax.vjp(
        layer_norm, summed, norm2_gain.astype(jnp.float32), norm2_shift.astype(jnp.float32)
    )
    layer_out = result.astype(lowered)
    sum_grad, gain2_grad, shift2_grad = norm2_back(cotangent.astype(jnp.float32))
    outer_low = sum_grad.astype(lowered)
    groups = ffn_in_weight.shape[0]
    active_pieces = active_low.reshape(own_count, groups, -1)
    outer_pieces = outer_low.reshape(own_count, groups, -1)
    ffn_out_grad = jnp.einsum(
        "ngi,ngo->igo", active_pieces, outer_pieces, preferred_element_type=jnp.float32
    )
    (inner_grad,) = gelu_back(grouped_input_grad(outer_low, ffn_out_weight))
    inner_low = inner_grad.astype(lowered)
    normed_pieces = normed_low.reshape(own_count, groups, -1)
    inner_pieces = inner_low.reshape(own_count, groups, -1)
    ffn_in_grad = jnp.einsum(
        "ngi,ngo->ogi", normed_pieces, inner_pieces, preferred_element_type=jnp.float32
    )
    normed_grad = sum_grad + grouped_input_grad(inner_low, ffn_in_weight)
    residual_grad, gain1_grad, shift1_grad = norm1_back(normed_grad)
    attn_low = residual_grad.astype(lowered)
    output_weight_grad = matmul_left(joined, attn_low)
    joined_grad = matmul_right(attn_low, output_weight).astype(lowered)
    context_grad = lax.all_to_all(joined_grad, "branch", split_axis=1, concat_axis=0, tiled=True)
    input_part, big_grads, branch_small = lax.cond(
        branch_index == 0,
        lambda operands: attention_backward(
            operands[0], operands[1], attend_weights, operands[2], operands[3]
        ),
        lambda operands: conv_backward(operands[0], operands[1], conv_weights, operands[3]),
        (hidden, segment_ids, log_sums, context_grad),
    )
    input_grad = (
        lax.psum_scatter(
            input_part.astype(jnp.bfloat16), "branch", scatter_dimension=0, tiled=True
        ).astype(jnp.float32)
        + residual_grad
    )
    dp_size = lax.axis_size("dp")
    units = 32
    q_g, k_g, v_g, depth_g, p_g, cv_g = big_grads
    unit_parts = [
        jnp.transpose(ffn_out_grad.reshape(units, -1, groups, D // groups), (0, 2, 1, 3)).reshape(units, -1, 384),
        jnp.transpose(ffn_in_grad.reshape(units, -1, groups, D // groups), (0, 2, 1, 3)).reshape(units, -1, 384),
        output_weight_grad[:, :384].reshape(units, -1, 384),
        output_weight_grad[:, 384:].reshape(units, -1, 384),
    ] + [x.reshape(units, -1, 384) for x in (q_g, k_g, v_g, p_g, cv_g)] + [
        jnp.pad(depth_g, ((0, 0), (0, 384 - KERNEL))).reshape(units, -1, 384)
    ]
    packed = jnp.concatenate([x.astype(lowered) for x in unit_parts], axis=1)
    small_terms = branch_small + (
        column_sums(attn_low),
        gain1_grad,
        shift1_grad,
        column_sums(inner_low),
        column_sums(outer_low),
        gain2_grad,
        shift2_grad,
    )
    flat = [jnp.transpose(x).reshape(-1) for x in small_terms]
    sizes = [x.shape[0] for x in flat]
    total = sum(sizes)
    small = jnp.pad(jnp.concatenate(flat), (0, 96 * 384 - total)).reshape(96, 384)
    out_sum, small_sum = comm_call(dp_size, packed, small)
    device = lax.axis_index("dp") * 2 + branch_index
    share = 2 * dp_size // units

    def piece(start, rows):
        n = rows // share
        return lax.dynamic_slice_in_dim(out_sum, start + lax.rem(device, share) * n, n, 0)

    ffn_out_w_grad = jnp.stack([piece(0, 48), piece(48, 48)])
    ffn_in_w_grad = jnp.stack([piece(96, 48), piece(144, 48)])
    out_w_grad = jnp.concatenate([piece(192, 24), piece(216, 24)], axis=1)
    query_w_grad, key_w_grad, value_w_grad, point_w_grad, conv_w_grad = [
        piece(240 + 24 * i, 24) for i in range(5)
    ]
    depth_w_grad = piece(360, 24)[:, :KERNEL]
    small_flat = small_sum.reshape(-1)
    parts, at = [], 0
    for n in sizes:
        parts.append(small_flat[at : at + n])
        at += n
    (
        query_b_grad,
        value_b_grad,
        point_b_grad,
        kern_w_grad,
        kern_b_grad,
        conv_b_grad,
        out_b_grad,
        gain_one,
        shift_one,
        ffn_in_b_grad,
        ffn_out_b_grad,
        gain_two,
        shift_two,
    ) = parts
    kern_w_grad = jnp.transpose(kern_w_grad.reshape(HEADS * KERNEL, HEADS * HEAD_DIM))
    return (
        layer_out,
        input_grad,
        query_w_grad,
        query_b_grad,
        key_w_grad,
        value_w_grad,
        value_b_grad,
        jnp.transpose(depth_w_grad),
        point_w_grad,
        point_b_grad,
        kern_w_grad,
        kern_b_grad,
        conv_w_grad,
        conv_b_grad,
        out_w_grad,
        out_b_grad,
        gain_one,
        shift_one,
        jnp.transpose(ffn_in_w_grad, (0, 2, 1)),
        ffn_in_b_grad,
        ffn_out_w_grad,
        ffn_out_b_grad,
        gain_two,
        shift_two,
    )


def solution(mesh):
    in_specs = (
        P("dp", None),
        P("dp", None),
        P(),
        P(),
        P(),
        P(),
        P(),
        P(),
        P(),
        P(),
        P(),
        P(),
        P(),
        P(),
        P(),
        P(),
        P(),
        P(),
        P(),
        P(),
        P(),
        P(),
        P(),
        P(),
        P(("dp", "branch"), None),
    )
    out_specs = (
        P(("dp", "branch"), None),
        P(("dp", "branch"), None),
        P(("dp", "branch"), None),
        P(),
        P(("dp", "branch"), None),
        P(("dp", "branch"), None),
        P(),
        P(None, ("dp", "branch")),
        P(("dp", "branch"), None),
        P(),
        P(),
        P(),
        P(("dp", "branch"), None),
        P(),
        P(("dp", "branch"), None),
        P(),
        P(),
        P(),
        P(None, None, ("dp", "branch")),
        P(),
        P(None, ("dp", "branch"), None),
        P(),
        P(),
        P(),
    )
    return jax.shard_map(local, mesh=mesh, in_specs=in_specs, out_specs=out_specs, check_vma=False)
```

```python
import functools
import math

import jax
import jax.numpy as jnp
from jax import lax
from jax.experimental import pallas as pl
from jax.experimental.pallas import tpu as pltpu
from jax.sharding import PartitionSpec as P

HEADS = 6
HEAD_DIM = 64
KERNEL = 9
WIDTH = HEADS * HEAD_DIM
D = 768
TILE = 256
PAD = 8
NEG = -1e30
norm_eps = 1e-12
low_type = jnp.bfloat16
f32 = jnp.float32

VEC_SIZES = (
    ("query_bias", 384), ("value_bias", 384), ("pointwise_bias", 384), ("conv_value_bias", 384),
    ("output_bias", 768), ("norm1_gain", 768), ("norm1_shift", 768), ("ffn_in_bias", 3072),
    ("ffn_out_bias", 768), ("norm2_gain", 768), ("norm2_shift", 768), ("kernel_bias", 128),
)
VEC_AT = {}
_at = 0
for _name, _size in VEC_SIZES:
    VEC_AT[_name] = (_at, _size)
    _at += _size
VEC_TOTAL = _at


def vec(vecs_ref, name):
    at, size = VEC_AT[name]
    return vecs_ref[0:1, at : at + size]


def mm(a, b):
    return jnp.dot(a, b, preferred_element_type=f32)


def mm_nt(a, b):
    return lax.dot_general(a, b, (((1,), (1,)), ((), ())), preferred_element_type=f32)


def mm_tn(a, b):
    return lax.dot_general(a, b, (((0,), (0,)), ((), ())), preferred_element_type=f32)


def tap_permutation():
    row = lax.broadcasted_iota(jnp.int32, (72, 54), 0)
    col = lax.broadcasted_iota(jnp.int32, (72, 54), 1)
    head = lax.rem(row, 8)
    return jnp.where((head * 9 + lax.div(row, 8) == col) & (head < HEADS), 1.0, 0.0)


def head_spread(j):
    row = lax.broadcasted_iota(jnp.int32, (72, WIDTH), 0)
    col = lax.broadcasted_iota(jnp.int32, (72, WIDTH), 1)
    return jnp.where(row == j * 8 + lax.div(col, HEAD_DIM), 1.0, 0.0).astype(low_type)


def tap_spread():
    row = lax.broadcasted_iota(jnp.int32, (72, KERNEL * 128), 0)
    col = lax.broadcasted_iota(jnp.int32, (72, KERNEL * 128), 1)
    return jnp.where(row == lax.div(col, 128) * 8, 1.0, 0.0).astype(low_type)


def aligned(start, size):
    return pl.ds(pl.multiple_of(start, size), size)


def half_rows(block, odd):
    zero = jnp.zeros((HEAD_DIM, block.shape[1]), block.dtype)
    kept = block[HEAD_DIM:] if odd else block[:HEAD_DIM]
    return jnp.concatenate([zero, kept] if odd else [kept, zero], axis=0)


def half_lanes(block, odd):
    lane = lax.broadcasted_iota(jnp.int32, block.shape, 1)
    keep = (lane >= HEAD_DIM) if odd else (lane < HEAD_DIM)
    return jnp.where(keep, block, jnp.zeros_like(block))


def shifted(pad_ref, c, start, j, size):
    return pad_ref[c, pl.ds(start + (PAD - 4 + j), size), :]


def depth_conv(pad_ref, mask_ref, weight, start, out, flip):
    for lo in range(0, TILE, 64):
        for c in range(D // 128):
            total = None
            for j in range(KERNEL):
                w = weight[KERNEL - 1 - j if flip else j][:, c * 128 : c * 128 + 128]
                term = shifted(pad_ref, c, start + lo, j, 64) * w
                if j != KERNEL // 2:
                    term = term * mask_ref[lo : lo + 64, j * 128 : j * 128 + 128]
                total = term if total is None else total + term
            out(c, lo, total)


def span_conv(pad_ref, taps, start):
    totals = [None] * (WIDTH // 128)
    for j in range(KERNEL):
        spread = mm(taps, head_spread(j))
        for c in range(WIDTH // 128):
            term = spread[:, c * 128 : c * 128 + 128] * shifted(pad_ref, c, start, j, TILE)
            totals[c] = term if totals[c] is None else totals[c] + term
    return jnp.concatenate(totals, axis=1)


def taps_softmax(logits):
    parts = [logits[j * 8 : j * 8 + 8] for j in range(KERNEL)]
    peak = functools.reduce(jnp.maximum, parts)
    parts = [jnp.exp(x - peak) for x in parts]
    scale = 1.0 / functools.reduce(jnp.add, parts)
    return jnp.concatenate([x * scale for x in parts], axis=0)


def mix_kernel(
    hidden, segments, query_w, key_w, value_w, point_w, conv_w, depth_w, kernel_w, vecs,
    joined, q_out, k_out, v_out, probs, conv_pad, taps_out, tap_mask, query_pre, key_conv, depth_low, conv_attn,
    x_pad, v_t, ctx_t, bias, seg_rows, mask_cols,
):
    b = lax.axis_index("branch")
    base = b * 512
    segs = segments[...].astype(f32)
    row0 = jnp.where(b == 0, segs[0:1], segs[1:2])
    row1 = jnp.where(b == 0, segs[1:2], segs[2:3])
    seg_rows[0:1, :] = row0
    seg_rows[1:2, :] = row1
    seg_t = jnp.transpose(jnp.concatenate([row0, row1] * 4, axis=0))
    both = jnp.concatenate([row0, row1 + 1024.0], axis=1)
    both = jnp.broadcast_to(both, (8, 1024))
    for j in range(KERNEL):
        moved = both if j == 4 else pltpu.roll(both, (4 - j) % 1024, 1)
        tap_mask[j * 8 : j * 8 + 8, :] = jnp.where(moved == both, 1.0, 0.0)
    for c in range(D // 128):
        x_pad[c, 0:PAD, :] = jnp.zeros((PAD, 128), f32)
        x_pad[c, 1024 + PAD : 1024 + 2 * PAD, :] = jnp.zeros((PAD, 128), f32)
    for c in range(WIDTH // 128):
        conv_pad[c, 0:PAD, :] = jnp.zeros((PAD, 128), f32)
        conv_pad[c, 1024 + PAD : 1024 + 2 * PAD, :] = jnp.zeros((PAD, 128), f32)
    taps_out[...] = jnp.zeros_like(taps_out)

    def project(e, carry):
        x = hidden[aligned(base + e * TILE, TILE), :]
        rows = aligned(e * TILE, TILE)
        k_out[rows, :] = mm(x, key_w[...]).astype(low_type)
        v = mm(x, value_w[...]) + vec(vecs, "value_bias")
        v_out[rows, :] = v.astype(low_type)
        v_t[:, rows] = jnp.transpose(v).astype(low_type)
        cv = mm(x, conv_w[...]) + vec(vecs, "conv_value_bias")
        place = pl.ds(pl.multiple_of(e * TILE + PAD, 8), TILE)
        for c in range(WIDTH // 128):
            conv_pad[c, place, :] = cv[:, c * 128 : c * 128 + 128]
        for c in range(D // 128):
            x_pad[c, place, :] = x[:, c * 128 : c * 128 + 128].astype(f32)
        return carry

    lax.fori_loop(0, 4, project, 0)
    kernel_rows = mm_nt(tap_permutation().astype(low_type), kernel_w[...]).astype(low_type)
    kernel_bias = jnp.sum(tap_permutation() * vec(vecs, "kernel_bias")[:, :54], axis=1, keepdims=True)
    depth_weights = [depth_w[j : j + 1, :].astype(f32) for j in range(KERNEL)]

    def own(i, carry):
        e = b + i
        rows = aligned(i * TILE, TILE)
        ext = aligned(e * TILE, TILE)
        x = hidden[aligned(base + e * TILE, TILE), :]
        q_pre = mm(x, query_w[...]) + vec(vecs, "query_bias")
        query_pre[rows, :] = q_pre
        q = q_pre.astype(low_type).astype(f32) * 0.125
        q_out[rows, :] = q.astype(low_type)
        q_t = jnp.transpose(q).astype(low_type)
        row = lax.div(e, 2)
        keys = aligned(row * 512, 512)
        seg_q = jnp.where(row == 0, seg_rows[0:1, :], seg_rows[1:2, :])
        seg_q = jnp.where(lax.rem(e, 2) == 0, seg_q[:, :TILE], seg_q[:, TILE:])
        seg_k = jnp.where(row == 0, seg_t[:, 0:1], seg_t[:, 1:2])
        bias[...] = jnp.where(seg_k == seg_q, 0.0, NEG)
        for h in range(HEADS):
            p = h // 2
            k_pair = k_out[keys, p * 128 : p * 128 + 128]
            scores = mm(k_pair, half_rows(q_t[p * 128 : p * 128 + 128], h % 2)) + bias[...]
            peak = jnp.max(scores, axis=0, keepdims=True)
            weight = jnp.exp(scores - peak)
            weight = (weight * (1.0 / jnp.sum(weight, axis=0, keepdims=True))).astype(low_type)
            probs[i * HEADS + h] = weight
            ctx_t[h * HEAD_DIM : (h + 1) * HEAD_DIM, :] = mm(v_t[h * HEAD_DIM : (h + 1) * HEAD_DIM, keys], weight)
        joined[rows, 0:WIDTH] = jnp.transpose(ctx_t[...]).astype(low_type)

        masks = tap_mask[:, ext]
        mask_cols[...] = mm(jnp.transpose(masks).astype(low_type), tap_spread())

        def keep(c, lo, value):
            at = pl.ds(pl.multiple_of(i * TILE + lo, 64), 64)
            depth_low[at, c * 128 : c * 128 + 128] = value.astype(low_type)

        depth_conv(x_pad, mask_cols, depth_weights, e * TILE, keep, False)
        kc = mm(depth_low[rows, :], point_w[...]) + vec(vecs, "pointwise_bias")
        key_conv[rows, :] = kc
        attn = (kc * q_pre).astype(low_type)
        conv_attn[rows, :] = attn
        taps = taps_softmax(mm_nt(kernel_rows, attn) + kernel_bias)
        taps_out[:, ext] = taps
        spread = span_conv(conv_pad, jnp.transpose(taps * masks).astype(low_type), e * TILE)
        joined[rows, WIDTH : 2 * WIDTH] = spread.astype(low_type)
        return carry

    lax.fori_loop(0, 3, own, 0)


VM = pl.BlockSpec(memory_space=pltpu.VMEM)


def mix_call(hidden, segments, query_w, key_w, value_w, point_w, conv_w, depth_w, kernel_w, vecs):
    shape = jax.ShapeDtypeStruct
    outs = (
        shape((768, 768), low_type), shape((768, WIDTH), low_type), shape((1024, WIDTH), low_type),
        shape((1024, WIDTH), low_type), shape((18, 512, TILE), low_type), shape((3, 1024 + 2 * PAD, 128), f32),
        shape((72, 1024), f32), shape((72, 1024), f32), shape((768, WIDTH), f32), shape((768, WIDTH), f32),
        shape((768, D), low_type), shape((768, WIDTH), low_type),
    )
    return pl.pallas_call(
        mix_kernel, out_shape=outs, in_specs=[VM] * 10, out_specs=(VM,) * len(outs),
        scratch_shapes=[
            pltpu.VMEM((6, 1024 + 2 * PAD, 128), f32), pltpu.VMEM((WIDTH, 1024), low_type),
            pltpu.VMEM((WIDTH, TILE), f32), pltpu.VMEM((512, TILE), f32), pltpu.VMEM((8, 512), f32),
            pltpu.VMEM((TILE, KERNEL * 128), f32),
        ],
        compiler_params=pltpu.CompilerParams(vmem_limit_bytes=60 << 20),
        name="mix_forward",
    )(hidden, segments, query_w, key_w, value_w, point_w, conv_w, depth_w, kernel_w, vecs)


SMALL2 = (("output_bias", 2), ("norm1_gain", 2), ("norm1_shift", 2), ("ffn_in_bias", 8), ("ffn_out_bias", 2), ("norm2_gain", 2), ("norm2_shift", 2))


def fold_rows(values):
    return jnp.sum(values.reshape(values.shape[0] // 8, 8, values.shape[1]), axis=0)


def normalize(values):
    centered = values - jnp.mean(values, axis=1, keepdims=True)
    scale = lax.rsqrt(jnp.mean(centered * centered, axis=1, keepdims=True) + norm_eps)
    return centered * scale, scale


def norm_back(grad, unit, scale, gain):
    e = grad * gain
    return (e - jnp.mean(e, axis=1, keepdims=True) - unit * jnp.mean(e * unit, axis=1, keepdims=True)) * scale


def write_small(small, row, total):
    line = jnp.sum(total, axis=0, keepdims=True)
    for k in range(line.shape[1] // 384):
        small[row + k : row + k + 1, :] = line[:, k * 384 : k * 384 + 384]


def ffn_kernel(
    hidden, joined, cotangent, out_w, in_w, ffo_w, vecs,
    layer_out, residual_grad, joined_grad, units, small,
    active, inner, normed_low, outer_low, attn_low, slope, total, unit1, sums, sums_in,
):
    b = lax.axis_index("branch")
    sums[...] = jnp.zeros_like(sums)
    sums_in[...] = jnp.zeros_like(sums_in)

    def block(i, carry):
        rows = aligned(i * TILE, TILE)
        x = hidden[aligned(b * 768 + i * TILE, TILE), :].astype(f32)
        n1, scale1 = normalize(x + mm(joined[rows, :], out_w[...]) + vec(vecs, "output_bias"))
        unit1[...] = n1
        normed = n1 * vec(vecs, "norm1_gain") + vec(vecs, "norm1_shift")
        normed_low[rows, :] = normed.astype(low_type)
        total[...] = normed + vec(vecs, "ffn_out_bias")

        def forward(c, carry):
            g, part = lax.div(c, 2), lax.rem(c, 2)
            lanes = pl.ds(pl.multiple_of(g * 384, 128), 384)
            wide = pl.ds(pl.multiple_of(part * 768, 128), 768)
            here = pl.ds(pl.multiple_of(c * 768, 128), 768)
            at = pl.ds(pl.multiple_of(VEC_AT["ffn_in_bias"][0] + c * 768, 128), 768)
            z = mm(normed_low[rows, lanes], in_w[g, :, wide]) + vecs[0:1, at]
            phi = 0.5 + 0.5 * lax.erf(z * (0.5**0.5))
            act = (z * phi).astype(low_type)
            active[rows, here] = act
            slope[:, here] = phi + z * jnp.exp(-0.5 * z * z) * ((2.0 * math.pi) ** -0.5)
            total[:, lanes] += mm(act, ffo_w[g, pl.ds(pl.multiple_of(part * 768, 128), 768), :])
            return carry

        lax.fori_loop(0, 4, forward, 0)
        n2, scale2 = normalize(total[...])
        layer_out[rows, :] = (n2 * vec(vecs, "norm2_gain") + vec(vecs, "norm2_shift")).astype(low_type)
        grad = cotangent[rows, :].astype(f32)
        sums[5] += fold_rows(grad * n2)
        sums[6] += fold_rows(grad)
        sum_grad = norm_back(grad, n2, scale2, vec(vecs, "norm2_gain"))
        outer = sum_grad.astype(low_type)
        outer_low[rows, :] = outer
        sums[4] += fold_rows(outer.astype(f32))
        total[...] = sum_grad

        def backward(c, carry):
            g, part = lax.div(c, 2), lax.rem(c, 2)
            lanes = pl.ds(pl.multiple_of(g * 384, 128), 384)
            wide = pl.ds(pl.multiple_of(part * 768, 128), 768)
            here = pl.ds(pl.multiple_of(c * 768, 128), 768)
            grad_in = mm_nt(outer_low[rows, lanes], ffo_w[g, wide, :]) * slope[:, here]
            grad_low = grad_in.astype(low_type)
            inner[rows, here] = grad_low
            sums_in[:, here] += fold_rows(grad_low.astype(f32))
            total[:, lanes] += mm_nt(grad_low, in_w[g, :, wide])
            return carry

        lax.fori_loop(0, 4, backward, 0)
        normed_grad = total[...]
        n1 = unit1[...]
        sums[1] += fold_rows(normed_grad * n1)
        sums[2] += fold_rows(normed_grad)
        grad1 = norm_back(normed_grad, n1, scale1, vec(vecs, "norm1_gain"))
        residual_grad[rows, :] = grad1
        attn = grad1.astype(low_type)
        attn_low[rows, :] = attn
        sums[0] += fold_rows(attn.astype(f32))
        joined_grad[rows, :] = mm_nt(attn, out_w[...]).astype(low_type)
        return carry

    lax.fori_loop(0, 3, block, 0)

    for g in range(2):
        lanes = slice(g * 384, g * 384 + 384)

        def weights(m, carry, g=g, lanes=lanes):
            wide = pl.ds(pl.multiple_of(g * 1536 + m * 384, 128), 384)
            group = pl.ds(m * 8, 8)
            grad_out = mm_tn(active[:, wide], outer_low[:, lanes])
            units[group, g * 48 : g * 48 + 48, :] = grad_out.reshape(8, 48, 384).astype(low_type)
            grad_in = mm_tn(inner[:, wide], normed_low[:, lanes])
            units[group, 96 + g * 48 : 144 + g * 48, :] = grad_in.reshape(8, 48, 384).astype(low_type)
            return carry

        lax.fori_loop(0, 4, weights, 0)
    for m in range(2):
        grad_w = mm_tn(joined[:, m * 384 : m * 384 + 384], attn_low[...])
        halves = [grad_w[:, :384].reshape(16, 24, 384), grad_w[:, 384:].reshape(16, 24, 384)]
        units[m * 16 : m * 16 + 16, 192:240, :] = jnp.concatenate(halves, axis=1).astype(low_type)
    small[...] = jnp.zeros_like(small)
    row = 0
    for k, (name, count) in enumerate(SMALL2):
        if name == "ffn_in_bias":
            write_small(small, row, sums_in[...])
        else:
            write_small(small, row, sums[k])
        row += count


def ffn_call(hidden, joined, cotangent, out_w, in_w, ffo_w, vecs):
    shape = jax.ShapeDtypeStruct
    outs = (
        shape((768, D), low_type), shape((768, D), f32), shape((768, D), low_type),
        shape((32, 240, 384), low_type), shape((32, 384), f32),
    )
    return pl.pallas_call(
        ffn_kernel, out_shape=outs, in_specs=[VM] * 7, out_specs=(VM,) * len(outs),
        scratch_shapes=[
            pltpu.VMEM((768, 3072), low_type), pltpu.VMEM((768, 3072), low_type),
            pltpu.VMEM((768, D), low_type), pltpu.VMEM((768, D), low_type), pltpu.VMEM((768, D), low_type),
            pltpu.VMEM((TILE, 3072), f32), pltpu.VMEM((TILE, D), f32), pltpu.VMEM((TILE, D), f32),
            pltpu.VMEM((7, 8, D), f32), pltpu.VMEM((8, 3072), f32),
        ],
        compiler_params=pltpu.CompilerParams(vmem_limit_bytes=60 << 20),
        name="ffn",
    )(hidden, joined, cotangent, out_w, in_w, ffo_w, vecs)


def back_kernel(
    hidden, joined_grad, residual_grad, q_in, k_in, v_in, probs, conv_pad, taps, tap_mask, query_pre, key_conv, depth_low,
    conv_attn, query_w, key_w, value_w, point_w, conv_w, depth_w, kernel_w,
    grad_own, grad_other, units, small,
    dk_acc, dv_acc, k_t, dq_low, kvc, key_conv_low, dg_pad, cg_pad, x_pad, mask_cols, dw_acc, dq_t, kernel_acc, bias_acc, moved_taps, part,
    sums,
):
    b = lax.axis_index("branch")
    base = b * 512
    for ref in (dk_acc, dv_acc, dg_pad, cg_pad, dw_acc, kernel_acc, bias_acc, sums):
        ref[...] = jnp.zeros_like(ref)
    for c in range(D // 128):
        x_pad[c, 0:PAD, :] = jnp.zeros((PAD, 128), f32)
        x_pad[c, 1024 + PAD : 1024 + 2 * PAD, :] = jnp.zeros((PAD, 128), f32)

    def prepare(e, carry):
        rows = aligned(e * TILE, TILE)
        k_t[:, rows] = jnp.transpose(k_in[rows, :].astype(f32)).astype(low_type)
        x = hidden[aligned(base + e * TILE, TILE), :]
        place = pl.ds(pl.multiple_of(e * TILE + PAD, 8), TILE)
        for c in range(D // 128):
            x_pad[c, place, :] = x[:, c * 128 : c * 128 + 128].astype(f32)
        return carry

    lax.fori_loop(0, 4, prepare, 0)
    kernel_rows = mm_nt(tap_permutation().astype(low_type), kernel_w[...]).astype(low_type)
    depth_weights = [depth_w[j : j + 1, :].astype(f32) for j in range(KERNEL)]
    head_rows = head_spread(0)[:8]
    moved = []
    for j in range(KERNEL):
        rows = taps[(8 - j) * 8 : (8 - j) * 8 + 8, :]
        rows = rows if j == 4 else pltpu.roll(rows, (4 - j) % 1024, 1)
        moved.append(rows * tap_mask[j * 8 : j * 8 + 8, :])
    moved_taps[...] = jnp.transpose(jnp.concatenate(moved, axis=0)).astype(low_type)

    def own(i, carry):
        e = b + i
        rows = aligned(i * TILE, TILE)
        ext = aligned(e * TILE, TILE)
        place = pl.ds(pl.multiple_of(e * TILE + PAD, 8), TILE)
        keys = aligned(lax.div(e, 2) * 512, 512)
        d_ctx = joined_grad[rows, 0:WIDTH]
        d_ctx_t = jnp.transpose(d_ctx.astype(f32)).astype(low_type)
        for p in range(HEADS // 2):
            lanes = slice(p * 128, p * 128 + 128)
            v_pair = v_in[keys, lanes]
            q_pair = q_in[rows, lanes]
            d_pair = d_ctx[:, lanes]
            scores, weights = [], []
            for odd in range(2):
                h = 2 * p + odd
                weight = probs[i * HEADS + h]
                prob_grad = mm(v_pair, half_rows(d_ctx_t[lanes], odd))
                wide = weight.astype(f32)
                term = wide * prob_grad
                score = (term - wide * jnp.sum(term, axis=0, keepdims=True)).astype(low_type)
                dq_t[h * HEAD_DIM : (h + 1) * HEAD_DIM, :] = mm(k_t[h * HEAD_DIM : (h + 1) * HEAD_DIM, keys], score)
                scores.append(score)
                weights.append(weight)
            q_both = jnp.concatenate([half_lanes(q_pair, 0), half_lanes(q_pair, 1)], axis=0)
            d_both = jnp.concatenate([half_lanes(d_pair, 0), half_lanes(d_pair, 1)], axis=0)
            dk_acc[keys, lanes] += mm(jnp.concatenate(scores, axis=1), q_both)
            dv_acc[keys, lanes] += mm(jnp.concatenate(weights, axis=1), d_both)
        query_low = (jnp.transpose(dq_t[...]) * 0.125).astype(low_type)

        grad = joined_grad[rows, WIDTH : 2 * WIDTH].astype(f32)
        for c in range(WIDTH // 128):
            cg_pad[c, place, :] = grad[:, c * 128 : c * 128 + 128]
        grads = []
        for j in range(KERNEL):
            pieces = [
                (grad[:, c * 128 : c * 128 + 128] * shifted(conv_pad, c, e * TILE, j, TILE)).astype(low_type)
                for c in range(WIDTH // 128)
            ]
            grads.append(mm_nt(head_rows, jnp.concatenate(pieces, axis=1)) * tap_mask[j * 8 : j * 8 + 8, ext])
        kept = taps[:, ext]
        level = functools.reduce(jnp.add, [grads[j] * kept[j * 8 : j * 8 + 8] for j in range(KERNEL)])
        logit = kept * jnp.concatenate([x - level for x in grads], axis=0)
        logit_low = logit.astype(low_type)
        logit_wide = logit_low.astype(f32)
        kernel_acc[...] += mm(logit_low, conv_attn[rows, :])
        bias_acc[...] += logit_wide[:, :128] + logit_wide[:, 128:]
        span = mm(jnp.transpose(logit_wide).astype(low_type), kernel_rows).astype(low_type).astype(f32)
        point_low = (span * query_pre[rows, :]).astype(low_type)
        query_conv = (span * key_conv[rows, :]).astype(low_type)
        key_conv_low[rows, :] = point_low
        sums[2] += fold_rows(point_low.astype(f32))
        both = query_low.astype(f32) + query_conv.astype(f32)
        sums[0] += fold_rows(both)
        dq_low[rows, :] = both.astype(low_type)
        d_depth = mm_nt(point_low, point_w[...])
        for c in range(D // 128):
            dg_pad[c, place, :] = d_depth[:, c * 128 : c * 128 + 128]
        mask_cols[...] = mm(jnp.transpose(tap_mask[:, ext]).astype(low_type), tap_spread())
        for c in range(D // 128):
            totals = [None] * KERNEL
            for lo in range(0, TILE, 64):
                grad_rows = dg_pad[c, pl.ds(e * TILE + (PAD + lo), 64), :]
                for j in range(KERNEL):
                    term = shifted(x_pad, c, e * TILE + lo, j, 64) * grad_rows
                    if j != KERNEL // 2:
                        term = term * mask_cols[lo : lo + 64, j * 128 : j * 128 + 128]
                    term = fold_rows(term)
                    totals[j] = term if lo == 0 else totals[j] + term
            for j in range(KERNEL):
                dw_acc[j, :, c * 128 : c * 128 + 128] += totals[j]
        return carry

    lax.fori_loop(0, 3, own, 0)

    def spread(e):
        ext = aligned(e * TILE, TILE)
        dk = dk_acc[ext, :].astype(low_type)
        dv = dv_acc[ext, :].astype(low_type)
        dc = span_conv(cg_pad, moved_taps[ext, :], e * TILE).astype(low_type)
        kvc[ext, 0:WIDTH] = dk
        kvc[ext, WIDTH : 2 * WIDTH] = dv
        kvc[ext, 2 * WIDTH : 3 * WIDTH] = dc
        sums[1] += fold_rows(dv.astype(f32))
        sums[3] += fold_rows(dc.astype(f32))
        mask_cols[...] = mm(jnp.transpose(tap_mask[:, ext]).astype(low_type), tap_spread())

        def keep(c, lo, value):
            part[lo : lo + 64, c * 128 : c * 128 + 128] = value

        depth_conv(dg_pad, mask_cols, depth_weights, e * TILE, keep, True)
        return part[...] + mm_nt(dk, key_w[...]) + mm_nt(dv, value_w[...]) + mm_nt(dc, conv_w[...])

    def finish(i, carry):
        rows = aligned(i * TILE, TILE)
        grad_own[rows, :] = spread(b + i) + mm_nt(dq_low[rows, :], query_w[...]) + residual_grad[rows, :]
        return carry

    lax.fori_loop(0, 3, finish, 0)
    grad_other[...] = spread(3 * (1 - b)).astype(low_type)

    depth_total = jnp.sum(dw_acc[...], axis=1)
    depth_t = jnp.transpose(jnp.concatenate([depth_total, jnp.zeros((128 - KERNEL, D), f32)], axis=0))
    for m in range(2):
        lanes = slice(m * 384, m * 384 + 384)
        group = slice(m * 16, m * 16 + 16)
        grad_kvc = mm_tn(hidden[aligned(base, 512), lanes], kvc[0:512, :]) + mm_tn(hidden[aligned(base + 512, 512), lanes], kvc[512:1024, :])
        grad_q = mm_tn(hidden[pl.ds(pl.multiple_of(b * 768, 256), 768), lanes], dq_low[...])
        grad_p = mm_tn(depth_low[:, lanes], key_conv_low[...])
        grad_d = jnp.concatenate([depth_t[lanes], jnp.zeros((384, 256), f32)], axis=1)
        pieces = [grad_q] + [grad_kvc[:, k * WIDTH : (k + 1) * WIDTH] for k in range(3)] + [grad_p, grad_d]
        pieces = [x.reshape(16, 24, 384) for x in pieces]
        for k in range(3):
            units[group, k * 48 : k * 48 + 48, :] = jnp.concatenate(pieces[2 * k : 2 * k + 2], axis=1).astype(low_type)
    small[...] = jnp.zeros_like(small)
    small[0:72, :] = kernel_acc[...]
    for k in range(4):
        small[72 + k : 73 + k, :] = jnp.sum(sums[k], axis=0, keepdims=True)
    column = jnp.concatenate([bias_acc[...], jnp.zeros((56, 128), f32)], axis=0)
    small[76:77, 0:128] = jnp.sum(jnp.transpose(column), axis=0, keepdims=True)


def back_call(hidden, joined_grad, residual_grad, saved, weights):
    shape = jax.ShapeDtypeStruct
    outs = (shape((768, D), f32), shape((256, D), low_type), shape((32, 144, 384), low_type), shape((96, 384), f32))
    operands = (hidden, joined_grad, residual_grad) + tuple(saved) + tuple(weights)
    ext = 1024 + 2 * PAD
    return pl.pallas_call(
        back_kernel, out_shape=outs, in_specs=[VM] * len(operands), out_specs=(VM,) * len(outs),
        scratch_shapes=[
            pltpu.VMEM((1024, WIDTH), f32), pltpu.VMEM((1024, WIDTH), f32), pltpu.VMEM((WIDTH, 1024), low_type),
            pltpu.VMEM((768, WIDTH), low_type), pltpu.VMEM((1024, 3 * WIDTH), low_type), pltpu.VMEM((768, WIDTH), low_type),
            pltpu.VMEM((6, ext, 128), f32), pltpu.VMEM((3, ext, 128), f32), pltpu.VMEM((6, ext, 128), f32),
            pltpu.VMEM((TILE, KERNEL * 128), f32), pltpu.VMEM((KERNEL, 8, D), f32), pltpu.VMEM((WIDTH, TILE), f32),
            pltpu.VMEM((72, WIDTH), f32), pltpu.VMEM((72, 128), f32), pltpu.VMEM((1024, 72), low_type), pltpu.VMEM((TILE, D), f32),
            pltpu.VMEM((4, 8, WIDTH), f32),
        ],
        compiler_params=pltpu.CompilerParams(vmem_limit_bytes=60 << 20),
        name="mix_backward",
    )(*operands)


MESH = pl.DeviceIdType.MESH
CHUNK = 48


def comm_orders(bits, extra):
    halving = list(range(extra, bits))
    first = [1] if 1 in halving else []
    rest = [k for k in halving if k not in first]
    a = [rest[0], rest[2], rest[1]] + rest[3:]
    b = [rest[1], rest[2], rest[0]] + rest[3:]
    return first + a, first + b


def comm_kernel(dp_size, g2, g3, s2, s3, other, out, s_out, got, rb, srb, erb, send, recv, ssend, srecv, esend, erecv, osem):
    bits = int(math.log2(dp_size)) + 1
    extra = max(0, bits - 5)
    orders = comm_orders(bits, extra)
    nh = bits - extra
    dp = lax.axis_index("dp")
    br = lax.axis_index("branch")
    my = [br] + [lax.rem(lax.div(dp, 1 << (k - 1)), 2) for k in range(1, bits)]
    chunks2 = g2.shape[-2] // CHUNK
    n_chunks = chunks2 + g3.shape[-2] // CHUNK

    def partner(k):
        if k == 0:
            return (dp, 1 - br)
        return (dp + (1 << (k - 1)) * (1 - 2 * my[k]), br)

    barrier = pltpu.get_barrier_semaphore()
    for k in range(bits):
        pl.semaphore_signal(barrier, inc=1, device_id=partner(k), device_id_type=MESH)
    pl.semaphore_wait(barrier, bits)

    def copy(src, dst, ssem, rsem, k):
        return pltpu.make_async_remote_copy(
            src_ref=src, dst_ref=dst, send_sem=ssem, recv_sem=rsem, device_id=partner(k), device_id_type=MESH
        )

    def offset(s):
        return sum(1 << (nh - 1 - t) for t in range(s))

    def source(c):
        return (g2, c * CHUNK) if c < chunks2 else (g3, (c - chunks2) * CHUNK)

    def place(u, free, fixed):
        names = sorted(free + list(fixed), reverse=True)
        index, at = 0, len(free) - 1
        for k in names:
            if k in fixed:
                value = fixed[k]
            else:
                value = (u >> at) & 1
                at -= 1
            index = index * 2 + value
        return index

    waits = {}

    def free_bits(order, s):
        return sorted(set(order[s:]), reverse=True)

    def start(c, s, order):
        k = order[s]
        free = free_bits(order, s + 1)
        count = 1 << len(free)
        for u in range(count):
            at = place(u, free, {k: 1 - my[k]})
            if s == 0:
                ref, row = source(c)
                src = ref.at[at, pl.ds(row, CHUNK)]
            else:
                src = rb.at[c, offset(s - 1) + at]
            copy(src, rb.at[c, offset(s) + u], send.at[c, s], recv.at[c, s], k).start()
        whole = rb.at[c, pl.ds(offset(s), count)]
        waits[(c, s)] = copy(whole, whole, send.at[c, s], recv.at[c, s], k)

    def add(c, s, order):
        waits[(c, s)].wait_recv()
        k = order[s]
        free = free_bits(order, s + 1)
        for u in range(1 << len(free)):
            at = place(u, free, {k: my[k]})
            if s == 0:
                ref, row = source(c)
                mine = ref[at, row : row + CHUNK, :]
            else:
                mine = rb[c, offset(s - 1) + at]
            total = mine.astype(jnp.float32) + rb[c, offset(s) + u].astype(jnp.float32)
            if s == nh - 1:
                out[c * CHUNK : (c + 1) * CHUNK, :] = total
            else:
                rb[c, offset(s) + u] = total.astype(rb.dtype)

    small_order = orders[0] + list(range(extra))

    def small_start(s):
        cp = copy(s_out, srb.at[s], ssend.at[s], srecv.at[s], small_order[s])
        cp.start()
        waits[("s", s)] = cp

    def small_add(s):
        waits[("s", s)].wait()
        s_out[...] = s_out[...] + srb[s]

    other_copy = copy(other, got, osem.at[0], osem.at[1], 0)
    other_copy.start()
    s_out[0 : s3.shape[0], :] = s3[...]
    s_out[s3.shape[0] :, :] = s2[...]
    half = n_chunks // 2
    for w in range(max(half + nh, bits + 1)):
        for p in range(half - 1, -1, -1):
            s = w - p
            for c, order in ((2 * p, orders[0]), (2 * p + 1, orders[1])):
                if 1 <= s <= nh:
                    add(c, s - 1, order)
                if 0 <= s < nh:
                    start(c, s, order)
        if 1 <= w <= bits:
            small_add(w - 1)
        if w < bits:
            small_start(w)
    for k in range(extra):
        cp = copy(out, erb.at[k], esend.at[k], erecv.at[k], k)
        cp.start()
        cp.wait()
        out[...] = out[...] + erb[k]
    for c in range(n_chunks):
        for s in range(nh):
            waits[(c, s)].wait_send()
    other_copy.wait()


def comm_call(dp_size, g2, g3, s2, s3, other):
    bits = int(math.log2(dp_size)) + 1
    extra = max(0, bits - 5)
    nh = bits - extra
    rows = g2.shape[1] + g3.shape[1]
    n_chunks = rows // CHUNK
    shape = jax.ShapeDtypeStruct
    small_shape = (s2.shape[0] + s3.shape[0], 384)
    dma = pltpu.SemaphoreType.DMA
    return pl.pallas_call(
        functools.partial(comm_kernel, dp_size),
        out_shape=(shape((rows, 384), jnp.float32), shape(small_shape, jnp.float32), shape(other.shape, other.dtype)),
        in_specs=[VM] * 5,
        out_specs=(VM, VM, VM),
        scratch_shapes=[
            pltpu.VMEM((n_chunks, (1 << nh) - 1, CHUNK, 384), jnp.bfloat16),
            pltpu.VMEM((bits,) + small_shape, jnp.float32),
            pltpu.VMEM((max(extra, 1), rows if extra else 8, 384), jnp.float32),
            dma((n_chunks, nh)), dma((n_chunks, nh)), dma((bits,)), dma((bits,)),
            dma((max(extra, 1),)), dma((max(extra, 1),)), dma((2,)),
        ],
        compiler_params=pltpu.CompilerParams(collective_id=0, has_side_effects=True, vmem_limit_bytes=60 << 20),
        name="grad_reduce",
    )(g2, g3, s2, s3, other)


def local(
    hidden, segment_ids, query_weight, query_bias, key_weight, value_weight, value_bias, depthwise_weight,
    pointwise_weight, pointwise_bias, kernel_weight, kernel_bias, conv_value_weight, conv_value_bias, output_weight,
    output_bias, norm1_gain, norm1_shift, ffn_in_weight, ffn_in_bias, ffn_out_weight, ffn_out_bias, norm2_gain,
    norm2_shift, cotangent,
):
    dp_size = lax.axis_size("dp")
    branch = lax.axis_index("branch")
    named = dict(
        query_bias=query_bias, value_bias=value_bias, pointwise_bias=pointwise_bias, conv_value_bias=conv_value_bias,
        output_bias=output_bias, norm1_gain=norm1_gain, norm1_shift=norm1_shift, ffn_in_bias=ffn_in_bias,
        ffn_out_bias=ffn_out_bias, norm2_gain=norm2_gain, norm2_shift=norm2_shift,
        kernel_bias=jnp.pad(kernel_bias, (0, 128 - kernel_bias.shape[0])),
    )
    vecs = jnp.concatenate([named[name] for name, _ in VEC_SIZES]).astype(f32).reshape(1, VEC_TOTAL)
    joined, *saved = mix_call(
        hidden, segment_ids, query_weight, key_weight, value_weight, pointwise_weight, conv_value_weight,
        depthwise_weight, kernel_weight, vecs,
    )
    layer_out, residual_grad, joined_grad, units2, small2 = ffn_call(
        hidden, joined, cotangent, output_weight, ffn_in_weight, ffn_out_weight, vecs
    )
    grad_own, grad_other, units3, small3 = back_call(
        hidden, joined_grad, residual_grad, saved,
        (query_weight, key_weight, value_weight, pointwise_weight, conv_value_weight, depthwise_weight, kernel_weight),
    )
    out_sum, small_sum, got = comm_call(dp_size, units2, units3, small2, small3, grad_other)
    start = (1 - branch) * 512
    block = lax.dynamic_slice_in_dim(grad_own, start, 256, 0) + got.astype(f32)
    input_grad = lax.dynamic_update_slice_in_dim(grad_own, block, start, 0)
    share = 2 * dp_size // 32
    device = lax.axis_index("dp") * 2 + branch

    def piece(start, rows):
        n = rows // share
        return lax.dynamic_slice_in_dim(out_sum, start + lax.rem(device, share) * n, n, 0)

    def small(row, size):
        return small_sum[row : row + -(-size // 384)].reshape(-1)[:size]

    kern_w = jnp.transpose(small_sum[:72].reshape(9, 8, 384)[:, :6], (2, 1, 0)).reshape(384, 54)
    kern_b = jnp.transpose(small_sum[76, :72].reshape(9, 8)[:, :6]).reshape(54)
    in_g = jnp.stack([piece(96, 48), piece(144, 48)])
    return (
        layer_out,
        input_grad,
        piece(240, 24),
        small(72, 384),
        piece(264, 24),
        piece(288, 24),
        small(73, 384),
        jnp.transpose(piece(360, 24)[:, :KERNEL]),
        piece(336, 24),
        small(74, 384),
        kern_w,
        kern_b,
        piece(312, 24),
        small(75, 384),
        jnp.concatenate([piece(192, 24), piece(216, 24)], axis=1),
        small(96, 768),
        small(98, 768),
        small(100, 768),
        jnp.transpose(in_g, (0, 2, 1)),
        small(102, 3072),
        jnp.stack([piece(0, 48), piece(48, 48)]),
        small(110, 768),
        small(112, 768),
        small(114, 768),
    )


def solution(mesh):
    tokens, copied = P(("dp", "branch"), None), P()
    in_specs = (P("dp", None), P("dp", None)) + (copied,) * 22 + (tokens,)
    out_specs = (
        tokens, tokens, tokens, copied, tokens, tokens, copied, P(None, ("dp", "branch")), tokens, copied, copied, copied,
        tokens, copied, tokens, copied, copied, copied, P(None, None, ("dp", "branch")), copied,
        P(None, ("dp", "branch"), None), copied, copied, copied,
    )
    return jax.shard_map(local, mesh=mesh, in_specs=in_specs, out_specs=out_specs, check_vma=False)
```

```python
import functools
import math

import jax
import jax.numpy as jnp
from jax import lax
from jax.experimental import pallas as pl
from jax.experimental.pallas import tpu as pltpu
from jax.sharding import PartitionSpec as P

HEADS = 6
HEAD_DIM = 64
KERNEL = 9
WIDTH = HEADS * HEAD_DIM
D = 768
TILE = 256
PAD = 8
NEG = -1e30
norm_eps = 1e-12
low_type = jnp.bfloat16
f32 = jnp.float32

VEC_SIZES = (
    ("query_bias", 384), ("value_bias", 384), ("pointwise_bias", 384), ("conv_value_bias", 384),
    ("output_bias", 768), ("norm1_gain", 768), ("norm1_shift", 768), ("ffn_in_bias", 3072),
    ("ffn_out_bias", 768), ("norm2_gain", 768), ("norm2_shift", 768), ("kernel_bias", 128),
)
VEC_AT = {}
_at = 0
for _name, _size in VEC_SIZES:
    VEC_AT[_name] = (_at, _size)
    _at += _size
VEC_TOTAL = _at


def vec(vecs_ref, name):
    at, size = VEC_AT[name]
    return vecs_ref[0:1, at : at + size]


def load_vecs(vecs, names, refs):
    for name, ref in zip(names, refs):
        at, size = VEC_AT[name]
        if name == "kernel_bias":
            size = ref.shape[0]
        vecs[0:1, at : at + size] = ref[...].astype(f32).reshape(1, size)


MIX_VECS = ("query_bias", "value_bias", "pointwise_bias", "conv_value_bias", "kernel_bias")
FFN_VECS = ("output_bias", "norm1_gain", "norm1_shift", "ffn_in_bias", "ffn_out_bias", "norm2_gain", "norm2_shift")


def mm(a, b):
    return jnp.dot(a, b, preferred_element_type=f32)


def mm_nt(a, b):
    return lax.dot_general(a, b, (((1,), (1,)), ((), ())), preferred_element_type=f32)


def mm_tn(a, b):
    return lax.dot_general(a, b, (((0,), (0,)), ((), ())), preferred_element_type=f32)


def tap_permutation():
    row = lax.broadcasted_iota(jnp.int32, (72, 54), 0)
    col = lax.broadcasted_iota(jnp.int32, (72, 54), 1)
    head = lax.rem(row, 8)
    return jnp.where((head * 9 + lax.div(row, 8) == col) & (head < HEADS), 1.0, 0.0)


def head_spread(j):
    row = lax.broadcasted_iota(jnp.int32, (72, WIDTH), 0)
    col = lax.broadcasted_iota(jnp.int32, (72, WIDTH), 1)
    return jnp.where(row == j * 8 + lax.div(col, HEAD_DIM), 1.0, 0.0).astype(low_type)


def tap_spread():
    row = lax.broadcasted_iota(jnp.int32, (72, KERNEL * 128), 0)
    col = lax.broadcasted_iota(jnp.int32, (72, KERNEL * 128), 1)
    return jnp.where(row == lax.div(col, 128) * 8, 1.0, 0.0).astype(low_type)


def aligned(start, size):
    return pl.ds(pl.multiple_of(start, size), size)


def half_rows(block, odd):
    zero = jnp.zeros((HEAD_DIM, block.shape[1]), block.dtype)
    kept = block[HEAD_DIM:] if odd else block[:HEAD_DIM]
    return jnp.concatenate([zero, kept] if odd else [kept, zero], axis=0)


def half_lanes(block, odd):
    lane = lax.broadcasted_iota(jnp.int32, block.shape, 1)
    keep = (lane >= HEAD_DIM) if odd else (lane < HEAD_DIM)
    return jnp.where(keep, block, jnp.zeros_like(block))


def shifted(pad_ref, c, start, j, size):
    return pad_ref[c, pl.ds(start + (PAD - 4 + j), size), :]


def depth_conv(pad_ref, mask_ref, weight, start, out, flip):
    for lo in range(0, TILE, 64):
        for c in range(D // 128):
            total = None
            for j in range(KERNEL):
                w = weight[KERNEL - 1 - j if flip else j][:, c * 128 : c * 128 + 128]
                term = shifted(pad_ref, c, start + lo, j, 64) * w
                if j != KERNEL // 2:
                    term = term * mask_ref[lo : lo + 64, j * 128 : j * 128 + 128]
                total = term if total is None else total + term
            out(c, lo, total)


def span_conv(pad_ref, taps, start):
    totals = [None] * (WIDTH // 128)
    for j in range(KERNEL):
        spread = mm(taps, head_spread(j))
        for c in range(WIDTH // 128):
            term = spread[:, c * 128 : c * 128 + 128] * shifted(pad_ref, c, start, j, TILE)
            totals[c] = term if totals[c] is None else totals[c] + term
    return jnp.concatenate(totals, axis=1)


def taps_softmax(logits):
    parts = [logits[j * 8 : j * 8 + 8] for j in range(KERNEL)]
    peak = functools.reduce(jnp.maximum, parts)
    parts = [jnp.exp(x - peak) for x in parts]
    scale = 1.0 / functools.reduce(jnp.add, parts)
    return jnp.concatenate([x * scale for x in parts], axis=0)


def mix_kernel(
    hidden, segments, query_w, key_w, value_w, point_w, conv_w, depth_w, kernel_w,
    vec0, vec1, vec2, vec3, vec4, joined, q_out, k_out, v_out, probs, conv_pad, taps_out, tap_mask, query_pre, key_conv, depth_low, conv_attn,
    x_pad, v_t, ctx_t, bias, seg_rows, mask_cols, vecs,
):
    load_vecs(vecs, MIX_VECS, (vec0, vec1, vec2, vec3, vec4))
    b = lax.axis_index("branch")
    base = b * 512
    segs = segments[...].astype(f32)
    row0 = jnp.where(b == 0, segs[0:1], segs[1:2])
    row1 = jnp.where(b == 0, segs[1:2], segs[2:3])
    seg_rows[0:1, :] = row0
    seg_rows[1:2, :] = row1
    seg_t = jnp.transpose(jnp.concatenate([row0, row1] * 4, axis=0))
    both = jnp.concatenate([row0, row1 + 1024.0], axis=1)
    both = jnp.broadcast_to(both, (8, 1024))
    for j in range(KERNEL):
        moved = both if j == 4 else pltpu.roll(both, (4 - j) % 1024, 1)
        tap_mask[j * 8 : j * 8 + 8, :] = jnp.where(moved == both, 1.0, 0.0)
    for c in range(D // 128):
        x_pad[c, 0:PAD, :] = jnp.zeros((PAD, 128), f32)
        x_pad[c, 1024 + PAD : 1024 + 2 * PAD, :] = jnp.zeros((PAD, 128), f32)
    for c in range(WIDTH // 128):
        conv_pad[c, 0:PAD, :] = jnp.zeros((PAD, 128), f32)
        conv_pad[c, 1024 + PAD : 1024 + 2 * PAD, :] = jnp.zeros((PAD, 128), f32)
    taps_out[...] = jnp.zeros_like(taps_out)

    def project(e, carry):
        x = hidden[aligned(base + e * TILE, TILE), :]
        rows = aligned(e * TILE, TILE)
        k_out[rows, :] = mm(x, key_w[...]).astype(low_type)
        v = mm(x, value_w[...]) + vec(vecs, "value_bias")
        v_out[rows, :] = v.astype(low_type)
        v_t[:, rows] = jnp.transpose(v).astype(low_type)
        cv = mm(x, conv_w[...]) + vec(vecs, "conv_value_bias")
        place = pl.ds(pl.multiple_of(e * TILE + PAD, 8), TILE)
        for c in range(WIDTH // 128):
            conv_pad[c, place, :] = cv[:, c * 128 : c * 128 + 128]
        for c in range(D // 128):
            x_pad[c, place, :] = x[:, c * 128 : c * 128 + 128].astype(f32)
        return carry

    lax.fori_loop(0, 4, project, 0)
    kernel_rows = mm(tap_permutation().astype(low_type), kernel_w[...]).astype(low_type)
    kernel_bias = jnp.sum(tap_permutation() * vec(vecs, "kernel_bias")[:, :54], axis=1, keepdims=True)
    depth_weights = [depth_w[j : j + 1, :].astype(f32) for j in range(KERNEL)]

    def own(i, carry):
        e = b + i
        rows = aligned(i * TILE, TILE)
        ext = aligned(e * TILE, TILE)
        x = hidden[aligned(base + e * TILE, TILE), :]
        q_pre = mm(x, query_w[...]) + vec(vecs, "query_bias")
        query_pre[rows, :] = q_pre
        q = q_pre.astype(low_type).astype(f32) * 0.125
        q_out[rows, :] = q.astype(low_type)
        q_t = jnp.transpose(q).astype(low_type)
        row = lax.div(e, 2)
        keys = aligned(row * 512, 512)
        seg_q = jnp.where(row == 0, seg_rows[0:1, :], seg_rows[1:2, :])
        seg_q = jnp.where(lax.rem(e, 2) == 0, seg_q[:, :TILE], seg_q[:, TILE:])
        seg_k = jnp.where(row == 0, seg_t[:, 0:1], seg_t[:, 1:2])
        bias[...] = jnp.where(seg_k == seg_q, 0.0, NEG)
        for h in range(HEADS):
            p = h // 2
            k_pair = k_out[keys, p * 128 : p * 128 + 128]
            scores = mm(k_pair, half_rows(q_t[p * 128 : p * 128 + 128], h % 2)) + bias[...]
            peak = jnp.max(scores, axis=0, keepdims=True)
            weight = jnp.exp(scores - peak)
            weight = (weight * (1.0 / jnp.sum(weight, axis=0, keepdims=True))).astype(low_type)
            probs[i * HEADS + h] = weight
            ctx_t[h * HEAD_DIM : (h + 1) * HEAD_DIM, :] = mm(v_t[h * HEAD_DIM : (h + 1) * HEAD_DIM, keys], weight)
        joined[rows, 0:WIDTH] = jnp.transpose(ctx_t[...]).astype(low_type)

        masks = tap_mask[:, ext]
        mask_cols[...] = mm(jnp.transpose(masks).astype(low_type), tap_spread())

        def keep(c, lo, value):
            at = pl.ds(pl.multiple_of(i * TILE + lo, 64), 64)
            depth_low[at, c * 128 : c * 128 + 128] = value.astype(low_type)

        depth_conv(x_pad, mask_cols, depth_weights, e * TILE, keep, False)
        kc = mm(depth_low[rows, :], point_w[...]) + vec(vecs, "pointwise_bias")
        key_conv[rows, :] = kc
        attn = (kc * q_pre).astype(low_type)
        conv_attn[rows, :] = attn
        taps = taps_softmax(mm_nt(kernel_rows, attn) + kernel_bias)
        taps_out[:, ext] = taps
        spread = span_conv(conv_pad, jnp.transpose(taps * masks).astype(low_type), e * TILE)
        joined[rows, WIDTH : 2 * WIDTH] = spread.astype(low_type)
        return carry

    lax.fori_loop(0, 3, own, 0)


VM = pl.BlockSpec(memory_space=pltpu.VMEM)


def mix_call(*operands):
    shape = jax.ShapeDtypeStruct
    outs = (
        shape((768, 768), low_type), shape((768, WIDTH), low_type), shape((1024, WIDTH), low_type),
        shape((1024, WIDTH), low_type), shape((18, 512, TILE), low_type), shape((3, 1024 + 2 * PAD, 128), f32),
        shape((72, 1024), f32), shape((72, 1024), f32), shape((768, WIDTH), f32), shape((768, WIDTH), f32),
        shape((768, D), low_type), shape((768, WIDTH), low_type),
    )
    return pl.pallas_call(
        mix_kernel, out_shape=outs, in_specs=[VM] * len(operands), out_specs=(VM,) * len(outs),
        scratch_shapes=[
            pltpu.VMEM((6, 1024 + 2 * PAD, 128), f32), pltpu.VMEM((WIDTH, 1024), low_type),
            pltpu.VMEM((WIDTH, TILE), f32), pltpu.VMEM((512, TILE), f32), pltpu.VMEM((8, 512), f32),
            pltpu.VMEM((TILE, KERNEL * 128), f32), pltpu.VMEM((1, VEC_TOTAL), f32),
        ],
        compiler_params=pltpu.CompilerParams(vmem_limit_bytes=60 << 20),
        name="mix_forward",
    )(*operands)


SMALL2 = (("output_bias", 2), ("norm1_gain", 2), ("norm1_shift", 2), ("ffn_in_bias", 8), ("ffn_out_bias", 2), ("norm2_gain", 2), ("norm2_shift", 2))


def fold_rows(values):
    return jnp.sum(values.reshape(values.shape[0] // 8, 8, values.shape[1]), axis=0)


def normalize(values):
    centered = values - jnp.mean(values, axis=1, keepdims=True)
    scale = lax.rsqrt(jnp.mean(centered * centered, axis=1, keepdims=True) + norm_eps)
    return centered * scale, scale


def norm_back(grad, unit, scale, gain):
    e = grad * gain
    return (e - jnp.mean(e, axis=1, keepdims=True) - unit * jnp.mean(e * unit, axis=1, keepdims=True)) * scale


def write_small(small, row, total):
    line = jnp.sum(total, axis=0, keepdims=True)
    for k in range(line.shape[1] // 384):
        small[row + k : row + k + 1, :] = line[:, k * 384 : k * 384 + 384]


def ffn_kernel(
    hidden, joined, cotangent, out_w, in_w, ffo_w,
    vec0, vec1, vec2, vec3, vec4, vec5, vec6,
    layer_out, residual_grad, joined_grad, units, small,
    active, inner, normed_low, outer_low, attn_low, slope, total, unit1, sums, sums_in, vecs,
):
    load_vecs(vecs, FFN_VECS, (vec0, vec1, vec2, vec3, vec4, vec5, vec6))
    b = lax.axis_index("branch")
    sums[...] = jnp.zeros_like(sums)
    sums_in[...] = jnp.zeros_like(sums_in)

    def block(i, carry):
        rows = aligned(i * TILE, TILE)
        x = hidden[aligned(b * 768 + i * TILE, TILE), :].astype(f32)
        n1, scale1 = normalize(x + mm(joined[rows, :], out_w[...]) + vec(vecs, "output_bias"))
        unit1[...] = n1
        normed = n1 * vec(vecs, "norm1_gain") + vec(vecs, "norm1_shift")
        normed_low[rows, :] = normed.astype(low_type)
        total[...] = normed + vec(vecs, "ffn_out_bias")

        def forward(c, carry):
            g, part = lax.div(c, 2), lax.rem(c, 2)
            lanes = pl.ds(pl.multiple_of(g * 384, 128), 384)
            wide = pl.ds(pl.multiple_of(part * 768, 128), 768)
            here = pl.ds(pl.multiple_of(c * 768, 128), 768)
            at = pl.ds(pl.multiple_of(VEC_AT["ffn_in_bias"][0] + c * 768, 128), 768)
            z = mm(normed_low[rows, lanes], in_w[g, :, wide]) + vecs[0:1, at]
            phi = 0.5 + 0.5 * lax.erf(z * (0.5**0.5))
            act = (z * phi).astype(low_type)
            active[rows, here] = act
            slope[:, here] = phi + z * jnp.exp(-0.5 * z * z) * ((2.0 * math.pi) ** -0.5)
            total[:, lanes] += mm(act, ffo_w[g, pl.ds(pl.multiple_of(part * 768, 128), 768), :])
            return carry

        lax.fori_loop(0, 4, forward, 0)
        n2, scale2 = normalize(total[...])
        layer_out[rows, :] = (n2 * vec(vecs, "norm2_gain") + vec(vecs, "norm2_shift")).astype(low_type)
        grad = cotangent[rows, :].astype(f32)
        sums[5] += fold_rows(grad * n2)
        sums[6] += fold_rows(grad)
        sum_grad = norm_back(grad, n2, scale2, vec(vecs, "norm2_gain"))
        outer = sum_grad.astype(low_type)
        outer_low[rows, :] = outer
        sums[4] += fold_rows(outer.astype(f32))
        total[...] = sum_grad

        def backward(c, carry):
            g, part = lax.div(c, 2), lax.rem(c, 2)
            lanes = pl.ds(pl.multiple_of(g * 384, 128), 384)
            wide = pl.ds(pl.multiple_of(part * 768, 128), 768)
            here = pl.ds(pl.multiple_of(c * 768, 128), 768)
            grad_in = mm_nt(outer_low[rows, lanes], ffo_w[g, wide, :]) * slope[:, here]
            grad_low = grad_in.astype(low_type)
            inner[rows, here] = grad_low
            sums_in[:, here] += fold_rows(grad_low.astype(f32))
            total[:, lanes] += mm_nt(grad_low, in_w[g, :, wide])
            return carry

        lax.fori_loop(0, 4, backward, 0)
        normed_grad = total[...]
        n1 = unit1[...]
        sums[1] += fold_rows(normed_grad * n1)
        sums[2] += fold_rows(normed_grad)
        grad1 = norm_back(normed_grad, n1, scale1, vec(vecs, "norm1_gain"))
        residual_grad[rows, :] = grad1
        attn = grad1.astype(low_type)
        attn_low[rows, :] = attn
        sums[0] += fold_rows(attn.astype(f32))
        joined_grad[rows, :] = mm_nt(attn, out_w[...]).astype(low_type)
        return carry

    lax.fori_loop(0, 3, block, 0)

    for g in range(2):
        lanes = slice(g * 384, g * 384 + 384)

        def weights(m, carry, g=g, lanes=lanes):
            wide = pl.ds(pl.multiple_of(g * 1536 + m * 384, 128), 384)
            group = pl.ds(m * 8, 8)
            grad_out = mm_tn(active[:, wide], outer_low[:, lanes])
            units[group, g * 48 : g * 48 + 48, :] = grad_out.reshape(8, 48, 384).astype(low_type)
            grad_in = mm_tn(inner[:, wide], normed_low[:, lanes])
            units[group, 96 + g * 48 : 144 + g * 48, :] = grad_in.reshape(8, 48, 384).astype(low_type)
            return carry

        lax.fori_loop(0, 4, weights, 0)
    for m in range(2):
        grad_w = mm_tn(joined[:, m * 384 : m * 384 + 384], attn_low[...])
        halves = [grad_w[:, :384].reshape(16, 24, 384), grad_w[:, 384:].reshape(16, 24, 384)]
        units[m * 16 : m * 16 + 16, 192:240, :] = jnp.concatenate(halves, axis=1).astype(low_type)
    small[...] = jnp.zeros_like(small)
    row = 0
    for k, (name, count) in enumerate(SMALL2):
        if name == "ffn_in_bias":
            write_small(small, row, sums_in[...])
        else:
            write_small(small, row, sums[k])
        row += count


def ffn_call(*operands):
    shape = jax.ShapeDtypeStruct
    outs = (
        shape((768, D), low_type), shape((768, D), f32), shape((768, D), low_type),
        shape((32, 240, 384), low_type), shape((32, 384), f32),
    )
    return pl.pallas_call(
        ffn_kernel, out_shape=outs, in_specs=[VM] * len(operands), out_specs=(VM,) * len(outs),
        scratch_shapes=[
            pltpu.VMEM((768, 3072), low_type), pltpu.VMEM((768, 3072), low_type),
            pltpu.VMEM((768, D), low_type), pltpu.VMEM((768, D), low_type), pltpu.VMEM((768, D), low_type),
            pltpu.VMEM((TILE, 3072), f32), pltpu.VMEM((TILE, D), f32), pltpu.VMEM((TILE, D), f32),
            pltpu.VMEM((7, 8, D), f32), pltpu.VMEM((8, 3072), f32), pltpu.VMEM((1, VEC_TOTAL), f32),
        ],
        compiler_params=pltpu.CompilerParams(vmem_limit_bytes=60 << 20),
        name="ffn",
    )(*operands)


def back_kernel(
    hidden, joined_grad, residual_grad, q_in, k_in, v_in, probs, conv_pad, taps, tap_mask, query_pre, key_conv, depth_low,
    conv_attn, query_w, key_w, value_w, point_w, conv_w, depth_w, kernel_w,
    grad_own, grad_other, units, small,
    dk_acc, dv_acc, k_t, dq_low, kvc, key_conv_low, dg_pad, cg_pad, x_pad, mask_cols, dw_acc, dq_t, kernel_acc, bias_acc, moved_taps, part,
    sums,
):
    b = lax.axis_index("branch")
    base = b * 512
    for ref in (dk_acc, dv_acc, dg_pad, cg_pad, dw_acc, kernel_acc, bias_acc, sums):
        ref[...] = jnp.zeros_like(ref)
    for c in range(D // 128):
        x_pad[c, 0:PAD, :] = jnp.zeros((PAD, 128), f32)
        x_pad[c, 1024 + PAD : 1024 + 2 * PAD, :] = jnp.zeros((PAD, 128), f32)

    def prepare(e, carry):
        rows = aligned(e * TILE, TILE)
        k_t[:, rows] = jnp.transpose(k_in[rows, :].astype(f32)).astype(low_type)
        x = hidden[aligned(base + e * TILE, TILE), :]
        place = pl.ds(pl.multiple_of(e * TILE + PAD, 8), TILE)
        for c in range(D // 128):
            x_pad[c, place, :] = x[:, c * 128 : c * 128 + 128].astype(f32)
        return carry

    lax.fori_loop(0, 4, prepare, 0)
    kernel_rows = mm(tap_permutation().astype(low_type), kernel_w[...]).astype(low_type)
    depth_weights = [depth_w[j : j + 1, :].astype(f32) for j in range(KERNEL)]
    head_rows = head_spread(0)[:8]
    moved = []
    for j in range(KERNEL):
        rows = taps[(8 - j) * 8 : (8 - j) * 8 + 8, :]
        rows = rows if j == 4 else pltpu.roll(rows, (4 - j) % 1024, 1)
        moved.append(rows * tap_mask[j * 8 : j * 8 + 8, :])
    moved_taps[...] = jnp.transpose(jnp.concatenate(moved, axis=0)).astype(low_type)

    def own(i, carry):
        e = b + i
        rows = aligned(i * TILE, TILE)
        ext = aligned(e * TILE, TILE)
        place = pl.ds(pl.multiple_of(e * TILE + PAD, 8), TILE)
        keys = aligned(lax.div(e, 2) * 512, 512)
        d_ctx = joined_grad[rows, 0:WIDTH]
        d_ctx_t = jnp.transpose(d_ctx.astype(f32)).astype(low_type)
        for p in range(HEADS // 2):
            lanes = slice(p * 128, p * 128 + 128)
            v_pair = v_in[keys, lanes]
            q_pair = q_in[rows, lanes]
            d_pair = d_ctx[:, lanes]
            scores, weights = [], []
            for odd in range(2):
                h = 2 * p + odd
                weight = probs[i * HEADS + h]
                prob_grad = mm(v_pair, half_rows(d_ctx_t[lanes], odd))
                wide = weight.astype(f32)
                term = wide * prob_grad
                score = (term - wide * jnp.sum(term, axis=0, keepdims=True)).astype(low_type)
                dq_t[h * HEAD_DIM : (h + 1) * HEAD_DIM, :] = mm(k_t[h * HEAD_DIM : (h + 1) * HEAD_DIM, keys], score)
                scores.append(score)
                weights.append(weight)
            q_both = jnp.concatenate([half_lanes(q_pair, 0), half_lanes(q_pair, 1)], axis=0)
            d_both = jnp.concatenate([half_lanes(d_pair, 0), half_lanes(d_pair, 1)], axis=0)
            dk_acc[keys, lanes] += mm(jnp.concatenate(scores, axis=1), q_both)
            dv_acc[keys, lanes] += mm(jnp.concatenate(weights, axis=1), d_both)
        query_low = (jnp.transpose(dq_t[...]) * 0.125).astype(low_type)

        grad = joined_grad[rows, WIDTH : 2 * WIDTH].astype(f32)
        for c in range(WIDTH // 128):
            cg_pad[c, place, :] = grad[:, c * 128 : c * 128 + 128]
        grads = []
        for j in range(KERNEL):
            pieces = [
                (grad[:, c * 128 : c * 128 + 128] * shifted(conv_pad, c, e * TILE, j, TILE)).astype(low_type)
                for c in range(WIDTH // 128)
            ]
            grads.append(mm_nt(head_rows, jnp.concatenate(pieces, axis=1)) * tap_mask[j * 8 : j * 8 + 8, ext])
        kept = taps[:, ext]
        level = functools.reduce(jnp.add, [grads[j] * kept[j * 8 : j * 8 + 8] for j in range(KERNEL)])
        logit = kept * jnp.concatenate([x - level for x in grads], axis=0)
        logit_low = logit.astype(low_type)
        logit_wide = logit_low.astype(f32)
        kernel_acc[...] += mm(logit_low, conv_attn[rows, :])
        bias_acc[...] += logit_wide[:, :128] + logit_wide[:, 128:]
        span = mm(jnp.transpose(logit_wide).astype(low_type), kernel_rows).astype(low_type).astype(f32)
        point_low = (span * query_pre[rows, :]).astype(low_type)
        query_conv = (span * key_conv[rows, :]).astype(low_type)
        key_conv_low[rows, :] = point_low
        sums[2] += fold_rows(point_low.astype(f32))
        both = query_low.astype(f32) + query_conv.astype(f32)
        sums[0] += fold_rows(both)
        dq_low[rows, :] = both.astype(low_type)
        d_depth = mm_nt(point_low, point_w[...])
        for c in range(D // 128):
            dg_pad[c, place, :] = d_depth[:, c * 128 : c * 128 + 128]
        mask_cols[...] = mm(jnp.transpose(tap_mask[:, ext]).astype(low_type), tap_spread())
        for c in range(D // 128):
            totals = [None] * KERNEL
            for lo in range(0, TILE, 64):
                grad_rows = dg_pad[c, pl.ds(e * TILE + (PAD + lo), 64), :]
                for j in range(KERNEL):
                    term = shifted(x_pad, c, e * TILE + lo, j, 64) * grad_rows
                    if j != KERNEL // 2:
                        term = term * mask_cols[lo : lo + 64, j * 128 : j * 128 + 128]
                    term = fold_rows(term)
                    totals[j] = term if lo == 0 else totals[j] + term
            for j in range(KERNEL):
                dw_acc[j, :, c * 128 : c * 128 + 128] += totals[j]
        return carry

    lax.fori_loop(0, 3, own, 0)

    def spread(e):
        ext = aligned(e * TILE, TILE)
        dk = dk_acc[ext, :].astype(low_type)
        dv = dv_acc[ext, :].astype(low_type)
        dc = span_conv(cg_pad, moved_taps[ext, :], e * TILE).astype(low_type)
        kvc[ext, 0:WIDTH] = dk
        kvc[ext, WIDTH : 2 * WIDTH] = dv
        kvc[ext, 2 * WIDTH : 3 * WIDTH] = dc
        sums[1] += fold_rows(dv.astype(f32))
        sums[3] += fold_rows(dc.astype(f32))
        mask_cols[...] = mm(jnp.transpose(tap_mask[:, ext]).astype(low_type), tap_spread())

        def keep(c, lo, value):
            part[lo : lo + 64, c * 128 : c * 128 + 128] = value

        depth_conv(dg_pad, mask_cols, depth_weights, e * TILE, keep, True)
        return part[...] + mm_nt(dk, key_w[...]) + mm_nt(dv, value_w[...]) + mm_nt(dc, conv_w[...])

    def finish(i, carry):
        rows = aligned(i * TILE, TILE)
        grad_own[rows, :] = spread(b + i) + mm_nt(dq_low[rows, :], query_w[...]) + residual_grad[rows, :]
        return carry

    lax.fori_loop(0, 3, finish, 0)
    grad_other[...] = spread(3 * (1 - b)).astype(low_type)

    depth_total = jnp.sum(dw_acc[...], axis=1)
    depth_t = jnp.transpose(jnp.concatenate([depth_total, jnp.zeros((128 - KERNEL, D), f32)], axis=0))
    for m in range(2):
        lanes = slice(m * 384, m * 384 + 384)
        group = slice(m * 16, m * 16 + 16)
        grad_kvc = mm_tn(hidden[aligned(base, 512), lanes], kvc[0:512, :]) + mm_tn(hidden[aligned(base + 512, 512), lanes], kvc[512:1024, :])
        grad_q = mm_tn(hidden[pl.ds(pl.multiple_of(b * 768, 256), 768), lanes], dq_low[...])
        grad_p = mm_tn(depth_low[:, lanes], key_conv_low[...])
        grad_d = jnp.concatenate([depth_t[lanes], jnp.zeros((384, 256), f32)], axis=1)
        pieces = [grad_q] + [grad_kvc[:, k * WIDTH : (k + 1) * WIDTH] for k in range(3)] + [grad_p, grad_d]
        pieces = [x.reshape(16, 24, 384) for x in pieces]
        for k in range(3):
            units[group, k * 48 : k * 48 + 48, :] = jnp.concatenate(pieces[2 * k : 2 * k + 2], axis=1).astype(low_type)
    small[...] = jnp.zeros_like(small)
    small[0:72, :] = kernel_acc[...]
    for k in range(4):
        small[72 + k : 73 + k, :] = jnp.sum(sums[k], axis=0, keepdims=True)
    column = jnp.concatenate([bias_acc[...], jnp.zeros((56, 128), f32)], axis=0)
    small[76:77, 0:128] = jnp.sum(jnp.transpose(column), axis=0, keepdims=True)


def back_call(hidden, joined_grad, residual_grad, saved, weights):
    shape = jax.ShapeDtypeStruct
    outs = (shape((768, D), f32), shape((256, D), low_type), shape((32, 144, 384), low_type), shape((96, 384), f32))
    operands = (hidden, joined_grad, residual_grad) + tuple(saved) + tuple(weights)
    ext = 1024 + 2 * PAD
    return pl.pallas_call(
        back_kernel, out_shape=outs, in_specs=[VM] * len(operands), out_specs=(VM,) * len(outs),
        scratch_shapes=[
            pltpu.VMEM((1024, WIDTH), f32), pltpu.VMEM((1024, WIDTH), f32), pltpu.VMEM((WIDTH, 1024), low_type),
            pltpu.VMEM((768, WIDTH), low_type), pltpu.VMEM((1024, 3 * WIDTH), low_type), pltpu.VMEM((768, WIDTH), low_type),
            pltpu.VMEM((6, ext, 128), f32), pltpu.VMEM((3, ext, 128), f32), pltpu.VMEM((6, ext, 128), f32),
            pltpu.VMEM((TILE, KERNEL * 128), f32), pltpu.VMEM((KERNEL, 8, D), f32), pltpu.VMEM((WIDTH, TILE), f32),
            pltpu.VMEM((72, WIDTH), f32), pltpu.VMEM((72, 128), f32), pltpu.VMEM((1024, 72), low_type), pltpu.VMEM((TILE, D), f32),
            pltpu.VMEM((4, 8, WIDTH), f32),
        ],
        compiler_params=pltpu.CompilerParams(vmem_limit_bytes=60 << 20),
        name="mix_backward",
    )(*operands)


MESH = pl.DeviceIdType.MESH
CHUNK = 48


def comm_orders(bits, extra):
    halving = list(range(extra, bits))
    first = [1] if 1 in halving else []
    rest = [k for k in halving if k not in first]
    a = [rest[0], rest[2], rest[1]] + rest[3:]
    b = [rest[1], rest[2], rest[0]] + rest[3:]
    return first + a, first + b


def comm_kernel(dp_size, g2, g3, s2, s3, other, out, s_out, got, rb, srb, erb, send, recv, ssend, srecv, esend, erecv, osem):
    bits = int(math.log2(dp_size)) + 1
    extra = max(0, bits - 5)
    orders = comm_orders(bits, extra)
    nh = bits - extra
    dp = lax.axis_index("dp")
    br = lax.axis_index("branch")
    my = [br] + [lax.rem(lax.div(dp, 1 << (k - 1)), 2) for k in range(1, bits)]
    chunks2 = g2.shape[-2] // CHUNK
    n_chunks = chunks2 + g3.shape[-2] // CHUNK

    def partner(k):
        if k == 0:
            return (dp, 1 - br)
        return (dp + (1 << (k - 1)) * (1 - 2 * my[k]), br)

    barrier = pltpu.get_barrier_semaphore()
    for k in range(bits):
        pl.semaphore_signal(barrier, inc=1, device_id=partner(k), device_id_type=MESH)
    pl.semaphore_wait(barrier, bits)

    def copy(src, dst, ssem, rsem, k):
        return pltpu.make_async_remote_copy(
            src_ref=src, dst_ref=dst, send_sem=ssem, recv_sem=rsem, device_id=partner(k), device_id_type=MESH
        )

    def offset(s):
        return sum(1 << (nh - 1 - t) for t in range(s))

    def source(c):
        return (g2, c * CHUNK) if c < chunks2 else (g3, (c - chunks2) * CHUNK)

    def place(u, free, fixed):
        names = sorted(free + list(fixed), reverse=True)
        index, at = 0, len(free) - 1
        for k in names:
            if k in fixed:
                value = fixed[k]
            else:
                value = (u >> at) & 1
                at -= 1
            index = index * 2 + value
        return index

    waits = {}

    def free_bits(order, s):
        return sorted(set(order[s:]), reverse=True)

    def start(c, s, order):
        k = order[s]
        free = free_bits(order, s + 1)
        count = 1 << len(free)
        for u in range(count):
            at = place(u, free, {k: 1 - my[k]})
            if s == 0:
                ref, row = source(c)
                src = ref.at[at, pl.ds(row, CHUNK)]
            else:
                src = rb.at[c, offset(s - 1) + at]
            copy(src, rb.at[c, offset(s) + u], send.at[c, s], recv.at[c, s], k).start()
        whole = rb.at[c, pl.ds(offset(s), count)]
        waits[(c, s)] = copy(whole, whole, send.at[c, s], recv.at[c, s], k)

    def add(c, s, order):
        waits[(c, s)].wait_recv()
        k = order[s]
        free = free_bits(order, s + 1)
        for u in range(1 << len(free)):
            at = place(u, free, {k: my[k]})
            if s == 0:
                ref, row = source(c)
                mine = ref[at, row : row + CHUNK, :]
            else:
                mine = rb[c, offset(s - 1) + at]
            total = mine.astype(jnp.float32) + rb[c, offset(s) + u].astype(jnp.float32)
            if s == nh - 1:
                out[c * CHUNK : (c + 1) * CHUNK, :] = total
            else:
                rb[c, offset(s) + u] = total.astype(rb.dtype)

    small_order = orders[0] + list(range(extra))

    def small_start(s):
        cp = copy(s_out, srb.at[s], ssend.at[s], srecv.at[s], small_order[s])
        cp.start()
        waits[("s", s)] = cp

    def small_add(s):
        waits[("s", s)].wait()
        s_out[...] = s_out[...] + srb[s]

    other_copy = copy(other, got, osem.at[0], osem.at[1], 0)
    other_copy.start()
    s_out[0 : s3.shape[0], :] = s3[...]
    s_out[s3.shape[0] :, :] = s2[...]
    half = n_chunks // 2
    for w in range(max(half + nh, bits + 1)):
        for p in range(half - 1, -1, -1):
            s = w - p
            for c, order in ((2 * p, orders[0]), (2 * p + 1, orders[1])):
                if 1 <= s <= nh:
                    add(c, s - 1, order)
                if 0 <= s < nh:
                    start(c, s, order)
        if 1 <= w <= bits:
            small_add(w - 1)
        if w < bits:
            small_start(w)
    for k in range(extra):
        cp = copy(out, erb.at[k], esend.at[k], erecv.at[k], k)
        cp.start()
        cp.wait()
        out[...] = out[...] + erb[k]
    for c in range(n_chunks):
        for s in range(nh):
            waits[(c, s)].wait_send()
    other_copy.wait()


def comm_call(dp_size, g2, g3, s2, s3, other):
    bits = int(math.log2(dp_size)) + 1
    extra = max(0, bits - 5)
    nh = bits - extra
    rows = g2.shape[1] + g3.shape[1]
    n_chunks = rows // CHUNK
    shape = jax.ShapeDtypeStruct
    small_shape = (s2.shape[0] + s3.shape[0], 384)
    dma = pltpu.SemaphoreType.DMA
    return pl.pallas_call(
        functools.partial(comm_kernel, dp_size),
        out_shape=(shape((rows, 384), jnp.float32), shape(small_shape, jnp.float32), shape(other.shape, other.dtype)),
        in_specs=[VM] * 5,
        out_specs=(VM, VM, VM),
        scratch_shapes=[
            pltpu.VMEM((n_chunks, (1 << nh) - 1, CHUNK, 384), jnp.bfloat16),
            pltpu.VMEM((bits,) + small_shape, jnp.float32),
            pltpu.VMEM((max(extra, 1), rows if extra else 8, 384), jnp.float32),
            dma((n_chunks, nh)), dma((n_chunks, nh)), dma((bits,)), dma((bits,)),
            dma((max(extra, 1),)), dma((max(extra, 1),)), dma((2,)),
        ],
        compiler_params=pltpu.CompilerParams(collective_id=0, has_side_effects=True, vmem_limit_bytes=60 << 20),
        name="grad_reduce",
    )(g2, g3, s2, s3, other)


def exact_columns(table, rows):
    return lax.dot_general(table, rows, (((0,), (0,)), ((), ())), precision=lax.Precision.HIGHEST, preferred_element_type=f32)


FINAL_SMALL = (
    ("query_b", 72, 384), ("value_b", 73, 384), ("point_b", 74, 384), ("conv_b", 75, 384), ("out_b", 96, 768), ("gain1", 98, 768),
    ("shift1", 100, 768), ("in_b", 102, 3072), ("ffo_b", 110, 768), ("gain2", 112, 768), ("shift2", 114, 768),
)


def final_kernel(
    grad_own, got, total, small,
    input_grad, query_w, key_w, value_w, depth_w, point_w, kernel_w, kernel_b, conv_w, out_w, in_w, ffo_w, *vectors,
):
    b = lax.axis_index("branch")
    input_grad[...] = grad_own[...]
    rows = aligned((1 - b) * 512, 256)
    input_grad[rows, :] = grad_own[rows, :] + got[...].astype(f32)
    for ref, row in ((query_w, 240), (key_w, 264), (value_w, 288), (conv_w, 312), (point_w, 336)):
        ref[...] = total[row : row + 24, :]
    ffo_w[0] = total[0:48, :]
    ffo_w[1] = total[48:96, :]
    out_w[:, 0:384] = total[192:216, :]
    out_w[:, 384:768] = total[216:240, :]
    in_w[0] = total[96:144, :]
    in_w[1] = total[144:192, :]
    depth = jnp.concatenate([total[360:384, 0:128], jnp.zeros((104, 128), f32)], axis=0)
    depth_w[...] = jnp.transpose(depth)[0:KERNEL, 0:24]
    table = tap_permutation()
    kernel_w[...] = exact_columns(table, small[0:72, :])
    column = jnp.transpose(jnp.concatenate([small[76:77, 0:128]] * 128, axis=0))[0:72, :]
    kernel_b[...] = jnp.sum(column[:, 0:54] * table, axis=0, keepdims=True).reshape(54)
    for ref, (_, row, size) in zip(vectors, FINAL_SMALL):
        ref[...] = jnp.concatenate([small[row + k : row + k + 1, :] for k in range(size // 384)], axis=1).reshape(size)


def final_call(grad_own, got, total, small):
    shape = lambda *s: jax.ShapeDtypeStruct(s, f32)
    outs = (
        shape(768, D), shape(24, 384), shape(24, 384), shape(24, 384), shape(KERNEL, 24), shape(24, 384), shape(54, 384), shape(54),
        shape(24, 384), shape(24, 768), shape(2, 48, 384), shape(2, 48, 384),
    ) + tuple(shape(size) for _, _, size in FINAL_SMALL)
    return pl.pallas_call(
        final_kernel, out_shape=outs, in_specs=[VM] * 4, out_specs=(VM,) * len(outs),
        compiler_params=pltpu.CompilerParams(vmem_limit_bytes=32 << 20), name="finish",
    )(grad_own, got, total, small)


def local(
    hidden, segment_ids, query_weight, query_bias, key_weight, value_weight, value_bias, depthwise_weight,
    pointwise_weight, pointwise_bias, kernel_weight, kernel_bias, conv_value_weight, conv_value_bias, output_weight,
    output_bias, norm1_gain, norm1_shift, ffn_in_weight, ffn_in_bias, ffn_out_weight, ffn_out_bias, norm2_gain,
    norm2_shift, cotangent,
):
    dp_size = lax.axis_size("dp")
    branch = lax.axis_index("branch")
    kernel_rows = jnp.transpose(kernel_weight)
    joined, *saved = mix_call(
        hidden, segment_ids, query_weight, key_weight, value_weight, pointwise_weight, conv_value_weight,
        depthwise_weight, kernel_rows, query_bias, value_bias, pointwise_bias, conv_value_bias, kernel_bias,
    )
    layer_out, residual_grad, joined_grad, units2, small2 = ffn_call(
        hidden, joined, cotangent, output_weight, ffn_in_weight, ffn_out_weight, output_bias, norm1_gain, norm1_shift,
        ffn_in_bias, ffn_out_bias, norm2_gain, norm2_shift,
    )
    grad_own, grad_other, units3, small3 = back_call(
        hidden, joined_grad, residual_grad, saved,
        (query_weight, key_weight, value_weight, pointwise_weight, conv_value_weight, depthwise_weight, kernel_rows),
    )
    out_sum, small_sum, got = comm_call(dp_size, units2, units3, small2, small3, grad_other)
    share = 2 * dp_size // 32
    if share == 1:
        (
            input_grad, query_w, key_w, value_w, depth_w, point_w, kernel_w, kernel_b, conv_w, out_w, in_w, ffo_w,
            query_b, value_b, point_b, conv_b, out_b, gain1, shift1, in_b, ffo_b, gain2, shift2,
        ) = final_call(grad_own, got, out_sum, small_sum)
        return (
            layer_out, input_grad, query_w, query_b, key_w, value_w, value_b, depth_w, point_w, point_b, jnp.transpose(kernel_w),
            kernel_b, conv_w, conv_b, out_w, out_b, gain1, shift1, jnp.transpose(in_w, (0, 2, 1)), in_b, ffo_w, ffo_b, gain2, shift2,
        )
    start = (1 - branch) * 512
    block = lax.dynamic_slice_in_dim(grad_own, start, 256, 0) + got.astype(f32)
    input_grad = lax.dynamic_update_slice_in_dim(grad_own, block, start, 0)
    device = lax.axis_index("dp") * 2 + branch

    def piece(start, rows):
        n = rows // share
        return lax.dynamic_slice_in_dim(out_sum, start + lax.rem(device, share) * n, n, 0)

    def small(row, size):
        return small_sum[row : row + -(-size // 384)].reshape(-1)[:size]

    kern_w = jnp.transpose(small_sum[:72].reshape(9, 8, 384)[:, :6], (2, 1, 0)).reshape(384, 54)
    kern_b = jnp.transpose(small_sum[76, :72].reshape(9, 8)[:, :6]).reshape(54)
    in_g = jnp.stack([piece(96, 48), piece(144, 48)])
    return (
        layer_out,
        input_grad,
        piece(240, 24),
        small(72, 384),
        piece(264, 24),
        piece(288, 24),
        small(73, 384),
        jnp.transpose(piece(360, 24)[:, :KERNEL]),
        piece(336, 24),
        small(74, 384),
        kern_w,
        kern_b,
        piece(312, 24),
        small(75, 384),
        jnp.concatenate([piece(192, 24), piece(216, 24)], axis=1),
        small(96, 768),
        small(98, 768),
        small(100, 768),
        jnp.transpose(in_g, (0, 2, 1)),
        small(102, 3072),
        jnp.stack([piece(0, 48), piece(48, 48)]),
        small(110, 768),
        small(112, 768),
        small(114, 768),
    )


def solution(mesh):
    tokens, copied = P(("dp", "branch"), None), P()
    in_specs = (P("dp", None), P("dp", None)) + (copied,) * 22 + (tokens,)
    out_specs = (
        tokens, tokens, tokens, copied, tokens, tokens, copied, P(None, ("dp", "branch")), tokens, copied, copied, copied,
        tokens, copied, tokens, copied, copied, copied, P(None, None, ("dp", "branch")), copied,
        P(None, ("dp", "branch"), None), copied, copied, copied,
    )
    return jax.shard_map(local, mesh=mesh, in_specs=in_specs, out_specs=out_specs, check_vma=False)
```

```python
import functools
import math

import jax
import jax.numpy as jnp
from jax import lax
from jax.experimental import pallas as pl
from jax.experimental.pallas import tpu as pltpu
from jax.sharding import PartitionSpec as P

HEADS = 6
HEAD_DIM = 64
KERNEL = 9
WIDTH = HEADS * HEAD_DIM
D = 768
TILE = 256
PAD = 8
NEG = -1e30
norm_eps = 1e-12
low_type = jnp.bfloat16
f32 = jnp.float32

VEC_SIZES = (
    ("query_bias", 384), ("value_bias", 384), ("pointwise_bias", 384), ("conv_value_bias", 384),
    ("output_bias", 768), ("norm1_gain", 768), ("norm1_shift", 768), ("ffn_in_bias", 3072),
    ("ffn_out_bias", 768), ("norm2_gain", 768), ("norm2_shift", 768), ("kernel_bias", 128),
)
VEC_AT = {}
_at = 0
for _name, _size in VEC_SIZES:
    VEC_AT[_name] = (_at, _size)
    _at += _size
VEC_TOTAL = _at


def vec(vecs_ref, name):
    at, size = VEC_AT[name]
    return vecs_ref[0:1, at : at + size]


def load_vecs(vecs, names, refs):
    for name, ref in zip(names, refs):
        at, size = VEC_AT[name]
        if name == "kernel_bias":
            size = ref.shape[0]
        vecs[0:1, at : at + size] = ref[...].astype(f32).reshape(1, size)


MIX_VECS = ("query_bias", "value_bias", "pointwise_bias", "conv_value_bias", "kernel_bias")
FFN_VECS = ("output_bias", "norm1_gain", "norm1_shift", "ffn_in_bias", "ffn_out_bias", "norm2_gain", "norm2_shift")


def mm(a, b):
    return jnp.dot(a, b, preferred_element_type=f32)


def mm_nt(a, b):
    return lax.dot_general(a, b, (((1,), (1,)), ((), ())), preferred_element_type=f32)


def mm_tn(a, b):
    return lax.dot_general(a, b, (((0,), (0,)), ((), ())), preferred_element_type=f32)


def tap_permutation():
    row = lax.broadcasted_iota(jnp.int32, (72, 54), 0)
    col = lax.broadcasted_iota(jnp.int32, (72, 54), 1)
    head = lax.rem(row, 8)
    return jnp.where((head * 9 + lax.div(row, 8) == col) & (head < HEADS), 1.0, 0.0)


def head_spread(j):
    row = lax.broadcasted_iota(jnp.int32, (72, WIDTH), 0)
    col = lax.broadcasted_iota(jnp.int32, (72, WIDTH), 1)
    return jnp.where(row == j * 8 + lax.div(col, HEAD_DIM), 1.0, 0.0).astype(low_type)


def tap_spread():
    row = lax.broadcasted_iota(jnp.int32, (72, KERNEL * 128), 0)
    col = lax.broadcasted_iota(jnp.int32, (72, KERNEL * 128), 1)
    return jnp.where(row == lax.div(col, 128) * 8, 1.0, 0.0).astype(low_type)


def aligned(start, size):
    return pl.ds(pl.multiple_of(start, size), size)


def half_rows(block, odd):
    zero = jnp.zeros((HEAD_DIM, block.shape[1]), block.dtype)
    kept = block[HEAD_DIM:] if odd else block[:HEAD_DIM]
    return jnp.concatenate([zero, kept] if odd else [kept, zero], axis=0)


def half_lanes(block, odd):
    lane = lax.broadcasted_iota(jnp.int32, block.shape, 1)
    keep = (lane >= HEAD_DIM) if odd else (lane < HEAD_DIM)
    return jnp.where(keep, block, jnp.zeros_like(block))


def shifted(pad_ref, c, start, j, size):
    return pad_ref[c, pl.ds(start + (PAD - 4 + j), size), :]


def depth_conv(pad_ref, mask_ref, weight, start, out, flip):
    for lo in range(0, TILE, 64):
        for c in range(D // 128):
            total = None
            for j in range(KERNEL):
                w = weight[KERNEL - 1 - j if flip else j][:, c * 128 : c * 128 + 128]
                term = shifted(pad_ref, c, start + lo, j, 64) * w
                if j != KERNEL // 2:
                    term = term * mask_ref[lo : lo + 64, j * 128 : j * 128 + 128]
                total = term if total is None else total + term
            out(c, lo, total)


def span_conv(pad_ref, taps, start):
    totals = [None] * (WIDTH // 128)
    for j in range(KERNEL):
        spread = mm(taps, head_spread(j))
        for c in range(WIDTH // 128):
            term = spread[:, c * 128 : c * 128 + 128] * shifted(pad_ref, c, start, j, TILE)
            totals[c] = term if totals[c] is None else totals[c] + term
    return jnp.concatenate(totals, axis=1)


def taps_softmax(logits):
    parts = [logits[j * 8 : j * 8 + 8] for j in range(KERNEL)]
    peak = functools.reduce(jnp.maximum, parts)
    parts = [jnp.exp(x - peak) for x in parts]
    scale = 1.0 / functools.reduce(jnp.add, parts)
    return jnp.concatenate([x * scale for x in parts], axis=0)


def mix_kernel(
    hidden, segments, query_w, key_w, value_w, point_w, conv_w, depth_w, kernel_w,
    vec0, vec1, vec2, vec3, vec4, joined, q_out, k_out, v_out, probs, conv_pad, taps_out, tap_mask, query_pre, key_conv, depth_low, conv_attn,
    x_pad, v_t, ctx_t, bias, seg_rows, mask_cols, vecs,
):
    load_vecs(vecs, MIX_VECS, (vec0, vec1, vec2, vec3, vec4))
    b = lax.axis_index("branch")
    base = b * 512
    segs = segments[...].astype(f32)
    row0 = jnp.where(b == 0, segs[0:1], segs[1:2])
    row1 = jnp.where(b == 0, segs[1:2], segs[2:3])
    seg_rows[0:1, :] = row0
    seg_rows[1:2, :] = row1
    seg_t = jnp.transpose(jnp.concatenate([row0, row1] * 4, axis=0))
    both = jnp.concatenate([row0, row1 + 1024.0], axis=1)
    both = jnp.broadcast_to(both, (8, 1024))
    for j in range(KERNEL):
        moved = both if j == 4 else pltpu.roll(both, (4 - j) % 1024, 1)
        tap_mask[j * 8 : j * 8 + 8, :] = jnp.where(moved == both, 1.0, 0.0)
    for c in range(D // 128):
        x_pad[c, 0:PAD, :] = jnp.zeros((PAD, 128), f32)
        x_pad[c, 1024 + PAD : 1024 + 2 * PAD, :] = jnp.zeros((PAD, 128), f32)
    for c in range(WIDTH // 128):
        conv_pad[c, 0:PAD, :] = jnp.zeros((PAD, 128), f32)
        conv_pad[c, 1024 + PAD : 1024 + 2 * PAD, :] = jnp.zeros((PAD, 128), f32)
    taps_out[...] = jnp.zeros_like(taps_out)

    def project(e, carry):
        x = hidden[aligned(base + e * TILE, TILE), :]
        rows = aligned(e * TILE, TILE)
        k_out[rows, :] = mm(x, key_w[...]).astype(low_type)
        v = mm(x, value_w[...]) + vec(vecs, "value_bias")
        v_out[rows, :] = v.astype(low_type)
        v_t[:, rows] = jnp.transpose(v).astype(low_type)
        cv = mm(x, conv_w[...]) + vec(vecs, "conv_value_bias")
        place = pl.ds(pl.multiple_of(e * TILE + PAD, 8), TILE)
        for c in range(WIDTH // 128):
            conv_pad[c, place, :] = cv[:, c * 128 : c * 128 + 128]
        for c in range(D // 128):
            x_pad[c, place, :] = x[:, c * 128 : c * 128 + 128].astype(f32)
        return carry

    lax.fori_loop(0, 4, project, 0)
    kernel_rows = mm(tap_permutation().astype(low_type), kernel_w[...]).astype(low_type)
    kernel_bias = jnp.sum(tap_permutation() * vec(vecs, "kernel_bias")[:, :54], axis=1, keepdims=True)
    depth_weights = [depth_w[j : j + 1, :].astype(f32) for j in range(KERNEL)]

    def own(i, carry):
        e = b + i
        rows = aligned(i * TILE, TILE)
        ext = aligned(e * TILE, TILE)
        x = hidden[aligned(base + e * TILE, TILE), :]
        q_pre = mm(x, query_w[...]) + vec(vecs, "query_bias")
        query_pre[rows, :] = q_pre.astype(low_type)
        q = q_pre.astype(low_type).astype(f32) * 0.125
        q_out[rows, :] = q.astype(low_type)
        q_t = jnp.transpose(q).astype(low_type)
        row = lax.div(e, 2)
        keys = aligned(row * 512, 512)
        seg_q = jnp.where(row == 0, seg_rows[0:1, :], seg_rows[1:2, :])
        seg_q = jnp.where(lax.rem(e, 2) == 0, seg_q[:, :TILE], seg_q[:, TILE:])
        seg_k = jnp.where(row == 0, seg_t[:, 0:1], seg_t[:, 1:2])
        bias[...] = jnp.where(seg_k == seg_q, 0.0, NEG)
        for h in range(HEADS):
            p = h // 2
            k_pair = k_out[keys, p * 128 : p * 128 + 128]
            scores = mm(k_pair, half_rows(q_t[p * 128 : p * 128 + 128], h % 2)) + bias[...]
            peak = jnp.max(scores, axis=0, keepdims=True)
            weight = jnp.exp(scores - peak)
            weight = (weight * (1.0 / jnp.sum(weight, axis=0, keepdims=True))).astype(low_type)
            probs[i * HEADS + h] = weight
            ctx_t[h * HEAD_DIM : (h + 1) * HEAD_DIM, :] = mm(v_t[h * HEAD_DIM : (h + 1) * HEAD_DIM, keys], weight)
        joined[rows, 0:WIDTH] = jnp.transpose(ctx_t[...]).astype(low_type)

        masks = tap_mask[:, ext]
        mask_cols[...] = mm(jnp.transpose(masks).astype(low_type), tap_spread())

        def keep(c, lo, value):
            at = pl.ds(pl.multiple_of(i * TILE + lo, 64), 64)
            depth_low[at, c * 128 : c * 128 + 128] = value.astype(low_type)

        depth_conv(x_pad, mask_cols, depth_weights, e * TILE, keep, False)
        kc = mm(depth_low[rows, :], point_w[...]) + vec(vecs, "pointwise_bias")
        key_conv[rows, :] = kc.astype(low_type)
        attn = (kc * q_pre).astype(low_type)
        conv_attn[rows, :] = attn
        taps = taps_softmax(mm_nt(kernel_rows, attn) + kernel_bias)
        taps_out[:, ext] = taps
        spread = span_conv(conv_pad, jnp.transpose(taps * masks).astype(low_type), e * TILE)
        joined[rows, WIDTH : 2 * WIDTH] = spread.astype(low_type)
        return carry

    lax.fori_loop(0, 3, own, 0)


VM = pl.BlockSpec(memory_space=pltpu.VMEM)


def mix_call(*operands):
    shape = jax.ShapeDtypeStruct
    outs = (
        shape((768, 768), low_type), shape((768, WIDTH), low_type), shape((1024, WIDTH), low_type),
        shape((1024, WIDTH), low_type), shape((18, 512, TILE), low_type), shape((3, 1024 + 2 * PAD, 128), f32),
        shape((72, 1024), f32), shape((72, 1024), f32), shape((768, WIDTH), low_type), shape((768, WIDTH), low_type),
        shape((768, D), low_type), shape((768, WIDTH), low_type),
    )
    return pl.pallas_call(
        mix_kernel, out_shape=outs, in_specs=[VM] * len(operands), out_specs=(VM,) * len(outs),
        scratch_shapes=[
            pltpu.VMEM((6, 1024 + 2 * PAD, 128), f32), pltpu.VMEM((WIDTH, 1024), low_type),
            pltpu.VMEM((WIDTH, TILE), f32), pltpu.VMEM((512, TILE), f32), pltpu.VMEM((8, 512), f32),
            pltpu.VMEM((TILE, KERNEL * 128), f32), pltpu.VMEM((1, VEC_TOTAL), f32),
        ],
        compiler_params=pltpu.CompilerParams(vmem_limit_bytes=60 << 20),
        name="mix_forward",
    )(*operands)


SMALL2 = (("output_bias", 2), ("norm1_gain", 2), ("norm1_shift", 2), ("ffn_in_bias", 8), ("ffn_out_bias", 2), ("norm2_gain", 2), ("norm2_shift", 2))


def fold_rows(values):
    return jnp.sum(values.reshape(values.shape[0] // 8, 8, values.shape[1]), axis=0)


def normalize(values):
    centered = values - jnp.mean(values, axis=1, keepdims=True)
    scale = lax.rsqrt(jnp.mean(centered * centered, axis=1, keepdims=True) + norm_eps)
    return centered * scale, scale


def norm_back(grad, unit, scale, gain):
    e = grad * gain
    return (e - jnp.mean(e, axis=1, keepdims=True) - unit * jnp.mean(e * unit, axis=1, keepdims=True)) * scale


def write_small(small, row, total):
    line = jnp.sum(total, axis=0, keepdims=True)
    for k in range(line.shape[1] // 384):
        small[row + k : row + k + 1, :] = line[:, k * 384 : k * 384 + 384]


def ffn_kernel(
    hidden, joined, cotangent, out_w, in_w, ffo_w,
    vec0, vec1, vec2, vec3, vec4, vec5, vec6,
    layer_out, residual_grad, joined_grad, units, small,
    active, inner, normed_low, outer_low, attn_low, slope, total, unit1, sums, sums_in, vecs,
):
    load_vecs(vecs, FFN_VECS, (vec0, vec1, vec2, vec3, vec4, vec5, vec6))
    b = lax.axis_index("branch")
    sums[...] = jnp.zeros_like(sums)
    sums_in[...] = jnp.zeros_like(sums_in)

    def block(i, carry):
        rows = aligned(i * TILE, TILE)
        x = hidden[aligned(b * 768 + i * TILE, TILE), :].astype(f32)
        n1, scale1 = normalize(x + mm(joined[rows, :], out_w[...]) + vec(vecs, "output_bias"))
        unit1[...] = n1
        normed = n1 * vec(vecs, "norm1_gain") + vec(vecs, "norm1_shift")
        normed_low[rows, :] = normed.astype(low_type)
        total[...] = normed + vec(vecs, "ffn_out_bias")

        def forward(c, carry):
            g, part = lax.div(c, 2), lax.rem(c, 2)
            lanes = pl.ds(pl.multiple_of(g * 384, 128), 384)
            wide = pl.ds(pl.multiple_of(part * 768, 128), 768)
            here = pl.ds(pl.multiple_of(c * 768, 128), 768)
            at = pl.ds(pl.multiple_of(VEC_AT["ffn_in_bias"][0] + c * 768, 128), 768)
            z = mm(normed_low[rows, lanes], in_w[g, :, wide]) + vecs[0:1, at]
            phi = 0.5 + 0.5 * lax.erf(z * (0.5**0.5))
            act = (z * phi).astype(low_type)
            active[rows, here] = act
            slope[:, here] = phi + z * jnp.exp(-0.5 * z * z) * ((2.0 * math.pi) ** -0.5)
            total[:, lanes] += mm(act, ffo_w[g, pl.ds(pl.multiple_of(part * 768, 128), 768), :])
            return carry

        lax.fori_loop(0, 4, forward, 0)
        n2, scale2 = normalize(total[...])
        layer_out[rows, :] = (n2 * vec(vecs, "norm2_gain") + vec(vecs, "norm2_shift")).astype(low_type)
        grad = cotangent[rows, :].astype(f32)
        sums[5] += fold_rows(grad * n2)
        sums[6] += fold_rows(grad)
        sum_grad = norm_back(grad, n2, scale2, vec(vecs, "norm2_gain"))
        outer = sum_grad.astype(low_type)
        outer_low[rows, :] = outer
        sums[4] += fold_rows(outer.astype(f32))
        total[...] = sum_grad

        def backward(c, carry):
            g, part = lax.div(c, 2), lax.rem(c, 2)
            lanes = pl.ds(pl.multiple_of(g * 384, 128), 384)
            wide = pl.ds(pl.multiple_of(part * 768, 128), 768)
            here = pl.ds(pl.multiple_of(c * 768, 128), 768)
            grad_in = mm_nt(outer_low[rows, lanes], ffo_w[g, wide, :]) * slope[:, here]
            grad_low = grad_in.astype(low_type)
            inner[rows, here] = grad_low
            sums_in[:, here] += fold_rows(grad_low.astype(f32))
            total[:, lanes] += mm_nt(grad_low, in_w[g, :, wide])
            return carry

        lax.fori_loop(0, 4, backward, 0)
        normed_grad = total[...]
        n1 = unit1[...]
        sums[1] += fold_rows(normed_grad * n1)
        sums[2] += fold_rows(normed_grad)
        grad1 = norm_back(normed_grad, n1, scale1, vec(vecs, "norm1_gain"))
        residual_grad[rows, :] = grad1
        attn = grad1.astype(low_type)
        attn_low[rows, :] = attn
        sums[0] += fold_rows(attn.astype(f32))
        joined_grad[rows, :] = mm_nt(attn, out_w[...]).astype(low_type)
        return carry

    lax.fori_loop(0, 3, block, 0)

    for g in range(2):
        lanes = slice(g * 384, g * 384 + 384)

        def weights(m, carry, g=g, lanes=lanes):
            wide = pl.ds(pl.multiple_of(g * 1536 + m * 384, 128), 384)
            group = pl.ds(m * 8, 8)
            grad_out = mm_tn(active[:, wide], outer_low[:, lanes])
            units[group, g * 48 : g * 48 + 48, :] = grad_out.reshape(8, 48, 384).astype(low_type)
            grad_in = mm_tn(inner[:, wide], normed_low[:, lanes])
            units[group, 96 + g * 48 : 144 + g * 48, :] = grad_in.reshape(8, 48, 384).astype(low_type)
            return carry

        lax.fori_loop(0, 4, weights, 0)
    for m in range(2):
        grad_w = mm_tn(joined[:, m * 384 : m * 384 + 384], attn_low[...])
        halves = [grad_w[:, :384].reshape(16, 24, 384), grad_w[:, 384:].reshape(16, 24, 384)]
        units[m * 16 : m * 16 + 16, 192:240, :] = jnp.concatenate(halves, axis=1).astype(low_type)
    small[...] = jnp.zeros_like(small)
    row = 0
    for k, (name, count) in enumerate(SMALL2):
        if name == "ffn_in_bias":
            write_small(small, row, sums_in[...])
        else:
            write_small(small, row, sums[k])
        row += count


def ffn_call(*operands):
    shape = jax.ShapeDtypeStruct
    outs = (
        shape((768, D), low_type), shape((768, D), f32), shape((768, D), low_type),
        shape((32, 240, 384), low_type), shape((32, 384), f32),
    )
    return pl.pallas_call(
        ffn_kernel, out_shape=outs, in_specs=[VM] * len(operands), out_specs=(VM,) * len(outs),
        scratch_shapes=[
            pltpu.VMEM((768, 3072), low_type), pltpu.VMEM((768, 3072), low_type),
            pltpu.VMEM((768, D), low_type), pltpu.VMEM((768, D), low_type), pltpu.VMEM((768, D), low_type),
            pltpu.VMEM((TILE, 3072), f32), pltpu.VMEM((TILE, D), f32), pltpu.VMEM((TILE, D), f32),
            pltpu.VMEM((7, 8, D), f32), pltpu.VMEM((8, 3072), f32), pltpu.VMEM((1, VEC_TOTAL), f32),
        ],
        compiler_params=pltpu.CompilerParams(vmem_limit_bytes=60 << 20),
        name="ffn",
    )(*operands)


MESH = pl.DeviceIdType.MESH
CHUNK = 48


class Reducer:
    def __init__(self, dp_size, sources, kept, kept_sem, buffer, out, send, recv):
        self.bits = int(math.log2(dp_size)) + 1
        self.extra = max(0, self.bits - 5)
        self.nh = self.bits - self.extra
        self.dp = lax.axis_index("dp")
        self.br = lax.axis_index("branch")
        self.my = [self.br] + [lax.rem(lax.div(self.dp, 1 << (k - 1)), 2) for k in range(1, self.bits)]
        self.kept, self.kept_sem = kept, kept_sem
        self.buffer, self.out, self.send, self.recv = buffer, out, send, recv
        self.sources = [(ref, row) for ref in sources for row in range(0, ref.shape[1], CHUNK)]
        halving = list(range(self.extra, self.bits))
        first = [1] if 1 in halving else []
        r = [k for k in halving if k not in first]
        turns = [(0, 2, 1), (1, 2, 0), (0, 2, 1), (1, 2, 0), (2, 0, 1), (0, 2, 1), (1, 0, 2), (2, 1, 0)]
        self.orders = [first + [r[t] for t in turn] + r[3:] for turn in turns]

    def enter(self):
        barrier = pltpu.get_barrier_semaphore()
        for k in range(self.bits):
            pl.semaphore_signal(barrier, inc=1, device_id=self.partner(k), device_id_type=MESH)
        pl.semaphore_wait(barrier, self.bits)

    def partner(self, k):
        if k == 0:
            return (self.dp, 1 - self.br)
        return (self.dp + (1 << (k - 1)) * (1 - 2 * self.my[k]), self.br)

    def copy(self, src, dst, ssem, rsem, k):
        return pltpu.make_async_remote_copy(
            src_ref=src, dst_ref=dst, send_sem=ssem, recv_sem=rsem, device_id=self.partner(k), device_id_type=MESH
        )

    def offset(self, s):
        return sum(1 << (self.nh - 1 - t) for t in range(s))

    def place(self, u, free, fixed, value):
        index, at = 0, len(free) - 1
        for k in sorted(free + [fixed], reverse=True):
            if k == fixed:
                index = index * 2 + value
            else:
                index = index * 2 + ((u >> at) & 1)
                at -= 1
        return index

    def free(self, c, s):
        return sorted(self.orders[c][s + 1 :], reverse=True)

    def whole(self, c, s):
        part = self.buffer.at[c, pl.ds(self.offset(s), 1 << (self.nh - 1 - s))]
        return self.copy(part, part, self.send.at[c, s], self.recv.at[c, s], self.orders[c][s])

    def start(self, c, s):
        k, free = self.orders[c][s], self.free(c, s)
        for u in range(1 << len(free)):
            at = self.place(u, free, k, 1 - self.my[k])
            if s == 0:
                ref, row = self.sources[c]
                src = ref.at[at, pl.ds(row, CHUNK)]
            else:
                src = self.buffer.at[c, self.offset(s - 1) + at]
            self.copy(src, self.buffer.at[c, self.offset(s) + u], self.send.at[c, s], self.recv.at[c, s], k).start()

    def fetch(self, c):
        k, free = self.orders[c][0], self.free(c, 0)
        ref, row = self.sources[c]
        for u in range(1 << len(free)):
            at = self.place(u, free, k, self.my[k])
            pltpu.make_async_copy(ref.at[at, pl.ds(row, CHUNK)], self.kept.at[c, u], self.kept_sem.at[c]).start()

    def add(self, c, s):
        fetched = c < self.kept.shape[0]
        if s == 0 and fetched:
            pltpu.make_async_copy(self.kept.at[c], self.kept.at[c], self.kept_sem.at[c]).wait()
        self.whole(c, s).wait_recv()
        k, free = self.orders[c][s], self.free(c, s)
        for u in range(1 << len(free)):
            at = self.place(u, free, k, self.my[k])
            if s == 0 and fetched:
                mine = self.kept[c, u]
            elif s == 0:
                ref, row = self.sources[c]
                mine = ref[at, row : row + CHUNK, :]
            else:
                mine = self.buffer[c, self.offset(s - 1) + at]
            total = mine.astype(f32) + self.buffer[c, self.offset(s) + u].astype(f32)
            if s == self.nh - 1:
                self.out[c * CHUNK : (c + 1) * CHUNK, :] = total
            else:
                self.buffer[c, self.offset(s) + u] = total.astype(low_type)

    def step(self, c, s):
        if s > 0:
            self.add(c, s - 1)
        if s < self.nh:
            self.start(c, s)

    def drain(self):
        for c in range(len(self.sources)):
            for s in range(self.nh):
                self.whole(c, s).wait_send()


class Doubler:
    def __init__(self, reducer, value, sent, got, send, recv):
        self.reducer, self.value, self.sent, self.got, self.send, self.recv = reducer, value, sent, got, send, recv
        self.order = reducer.orders[0] + list(range(reducer.extra))

    def copy(self, s):
        return self.reducer.copy(self.sent, self.got.at[s], self.send.at[s], self.recv.at[s], self.order[s])

    def step(self, s):
        if s > 0:
            copy = self.copy(s - 1)
            copy.wait()
            self.value[...] = self.sent[...].astype(f32) + self.got[s - 1].astype(f32)
        if s < len(self.order):
            self.sent[...] = self.value[...].astype(self.sent.dtype)
            self.copy(s).start()


def back_kernel(
    dp_size, hidden, joined_grad, residual_grad, q_in, k_in, v_in, probs, conv_pad, taps, tap_mask, query_pre, key_conv, depth_low,
    conv_attn, units2, small2, query_w, key_w, value_w, point_w, conv_w, depth_w, kernel_w,
    grad_own, got_other, out, sum2, sum3,
    dk_acc, dv_acc, k_t, dq_low, kvc, key_conv_low, dg_pad, cg_pad, x_pad, mask_cols, dw_acc, dq_t, kernel_acc, bias_acc, moved_taps, part,
    sums, grad_other, units, small, buffer, sent2, got2, sent3, got3, extra_got,
    send, recv, send2, recv2, send3, recv3, other_sem, extra_sem, kept, kept_sem,
):
    reducer = Reducer(dp_size, (units2, units), kept, kept_sem, buffer, out, send, recv)
    nh, bits, extra = reducer.nh, reducer.bits, reducer.extra
    early, late = Doubler(reducer, sum2, sent2, got2, send2, recv2), Doubler(reducer, sum3, sent3, got3, send3, recv3)
    other_copy = reducer.copy(grad_other, got_other, other_sem.at[0], other_sem.at[1], 0)
    for c in range(5):
        reducer.fetch(c)
    reducer.enter()
    for c in range(5):
        reducer.step(c, 0)
    sum2[...] = small2[...]
    early.step(0)
    starts = (0, 0, 1, 1, 2)

    def advance(point):
        for c in range(5):
            s = point + 1 - starts[c]
            if 1 <= s <= nh:
                reducer.step(c, s)
        if 1 <= point + 1 <= bits:
            early.step(point + 1)

    def advance_at(i, half):
        for n in range(3):
            @pl.when(i == n)
            def _():
                advance(2 * n + half)

    b = lax.axis_index("branch")
    base = b * 512
    for ref in (dk_acc, dv_acc, dg_pad, cg_pad, dw_acc, kernel_acc, bias_acc, sums):
        ref[...] = jnp.zeros_like(ref)
    for c in range(D // 128):
        x_pad[c, 0:PAD, :] = jnp.zeros((PAD, 128), f32)
        x_pad[c, 1024 + PAD : 1024 + 2 * PAD, :] = jnp.zeros((PAD, 128), f32)

    def prepare(e, carry):
        rows = aligned(e * TILE, TILE)
        k_t[:, rows] = jnp.transpose(k_in[rows, :].astype(f32)).astype(low_type)
        x = hidden[aligned(base + e * TILE, TILE), :]
        place = pl.ds(pl.multiple_of(e * TILE + PAD, 8), TILE)
        for c in range(D // 128):
            x_pad[c, place, :] = x[:, c * 128 : c * 128 + 128].astype(f32)
        return carry

    lax.fori_loop(0, 4, prepare, 0)
    kernel_rows = mm(tap_permutation().astype(low_type), kernel_w[...]).astype(low_type)
    depth_weights = [depth_w[j : j + 1, :].astype(f32) for j in range(KERNEL)]
    head_rows = head_spread(0)[:8]
    moved = []
    for j in range(KERNEL):
        rows = taps[(8 - j) * 8 : (8 - j) * 8 + 8, :]
        rows = rows if j == 4 else pltpu.roll(rows, (4 - j) % 1024, 1)
        moved.append(rows * tap_mask[j * 8 : j * 8 + 8, :])
    moved_taps[...] = jnp.transpose(jnp.concatenate(moved, axis=0)).astype(low_type)

    def own(i, carry):
        e = b + i
        rows = aligned(i * TILE, TILE)
        ext = aligned(e * TILE, TILE)
        place = pl.ds(pl.multiple_of(e * TILE + PAD, 8), TILE)
        keys = aligned(lax.div(e, 2) * 512, 512)
        d_ctx = joined_grad[rows, 0:WIDTH]
        d_ctx_t = jnp.transpose(d_ctx.astype(f32)).astype(low_type)
        for p in range(HEADS // 2):
            lanes = slice(p * 128, p * 128 + 128)
            v_pair = v_in[keys, lanes]
            q_pair = q_in[rows, lanes]
            d_pair = d_ctx[:, lanes]
            scores, weights = [], []
            for odd in range(2):
                h = 2 * p + odd
                weight = probs[i * HEADS + h]
                prob_grad = mm(v_pair, half_rows(d_ctx_t[lanes], odd))
                wide = weight.astype(f32)
                term = wide * prob_grad
                score = (term - wide * jnp.sum(term, axis=0, keepdims=True)).astype(low_type)
                dq_t[h * HEAD_DIM : (h + 1) * HEAD_DIM, :] = mm(k_t[h * HEAD_DIM : (h + 1) * HEAD_DIM, keys], score)
                scores.append(score)
                weights.append(weight)
            q_both = jnp.concatenate([half_lanes(q_pair, 0), half_lanes(q_pair, 1)], axis=0)
            d_both = jnp.concatenate([half_lanes(d_pair, 0), half_lanes(d_pair, 1)], axis=0)
            dk_acc[keys, lanes] += mm(jnp.concatenate(scores, axis=1), q_both)
            dv_acc[keys, lanes] += mm(jnp.concatenate(weights, axis=1), d_both)
        advance_at(i, 0)
        query_low = (jnp.transpose(dq_t[...]) * 0.125).astype(low_type)

        grad = joined_grad[rows, WIDTH : 2 * WIDTH].astype(f32)
        for c in range(WIDTH // 128):
            cg_pad[c, place, :] = grad[:, c * 128 : c * 128 + 128]
        grads = []
        for j in range(KERNEL):
            pieces = [
                (grad[:, c * 128 : c * 128 + 128] * shifted(conv_pad, c, e * TILE, j, TILE)).astype(low_type)
                for c in range(WIDTH // 128)
            ]
            grads.append(mm_nt(head_rows, jnp.concatenate(pieces, axis=1)) * tap_mask[j * 8 : j * 8 + 8, ext])
        kept = taps[:, ext]
        level = functools.reduce(jnp.add, [grads[j] * kept[j * 8 : j * 8 + 8] for j in range(KERNEL)])
        logit = kept * jnp.concatenate([x - level for x in grads], axis=0)
        logit_low = logit.astype(low_type)
        logit_wide = logit_low.astype(f32)
        kernel_acc[...] += mm(logit_low, conv_attn[rows, :])
        bias_acc[...] += logit_wide[:, :128] + logit_wide[:, 128:]
        span = mm(jnp.transpose(logit_wide).astype(low_type), kernel_rows).astype(low_type).astype(f32)
        point_low = (span * query_pre[rows, :].astype(f32)).astype(low_type)
        query_conv = (span * key_conv[rows, :].astype(f32)).astype(low_type)
        key_conv_low[rows, :] = point_low
        sums[2] += fold_rows(point_low.astype(f32))
        both = query_low.astype(f32) + query_conv.astype(f32)
        sums[0] += fold_rows(both)
        dq_low[rows, :] = both.astype(low_type)
        d_depth = mm_nt(point_low, point_w[...])
        for c in range(D // 128):
            dg_pad[c, place, :] = d_depth[:, c * 128 : c * 128 + 128]
        mask_cols[...] = mm(jnp.transpose(tap_mask[:, ext]).astype(low_type), tap_spread())
        for c in range(D // 128):
            totals = [None] * KERNEL
            for lo in range(0, TILE, 64):
                grad_rows = dg_pad[c, pl.ds(e * TILE + (PAD + lo), 64), :]
                for j in range(KERNEL):
                    term = shifted(x_pad, c, e * TILE + lo, j, 64) * grad_rows
                    if j != KERNEL // 2:
                        term = term * mask_cols[lo : lo + 64, j * 128 : j * 128 + 128]
                    term = fold_rows(term)
                    totals[j] = term if lo == 0 else totals[j] + term
            for j in range(KERNEL):
                dw_acc[j, :, c * 128 : c * 128 + 128] += totals[j]
        advance_at(i, 1)
        return carry

    lax.fori_loop(0, 3, own, 0)

    def span_grads(e):
        ext = aligned(e * TILE, TILE)
        dv = dv_acc[ext, :].astype(low_type)
        dc = span_conv(cg_pad, moved_taps[ext, :], e * TILE).astype(low_type)
        kvc[ext, 0:WIDTH] = dk_acc[ext, :].astype(low_type)
        kvc[ext, WIDTH : 2 * WIDTH] = dv
        kvc[ext, 2 * WIDTH : 3 * WIDTH] = dc
        sums[1] += fold_rows(dv.astype(f32))
        sums[3] += fold_rows(dc.astype(f32))

    def input_part(e):
        ext = aligned(e * TILE, TILE)
        mask_cols[...] = mm(jnp.transpose(tap_mask[:, ext]).astype(low_type), tap_spread())

        def keep(c, lo, value):
            part[lo : lo + 64, c * 128 : c * 128 + 128] = value

        depth_conv(dg_pad, mask_cols, depth_weights, e * TILE, keep, True)
        pieces = [kvc[ext, k * WIDTH : (k + 1) * WIDTH] for k in range(3)]
        return part[...] + mm_nt(pieces[0], key_w[...]) + mm_nt(pieces[1], value_w[...]) + mm_nt(pieces[2], conv_w[...])

    def spans(i, carry):
        span_grads(i)
        return carry

    lax.fori_loop(0, 4, spans, 0)
    grad_other[...] = input_part(3 * (1 - b)).astype(low_type)
    other_copy.start()
    advance(6)

    depth_total = jnp.sum(dw_acc[...], axis=1)
    depth_t = jnp.transpose(jnp.concatenate([depth_total, jnp.zeros((128 - KERNEL, D), f32)], axis=0))
    for m in range(2):
        lanes = slice(m * 384, m * 384 + 384)
        group = slice(m * 16, m * 16 + 16)
        grad_kvc = mm_tn(hidden[aligned(base, 512), lanes], kvc[0:512, :]) + mm_tn(hidden[aligned(base + 512, 512), lanes], kvc[512:1024, :])
        grad_q = mm_tn(hidden[pl.ds(pl.multiple_of(b * 768, 256), 768), lanes], dq_low[...])
        grad_p = mm_tn(depth_low[:, lanes], key_conv_low[...])
        grad_d = jnp.concatenate([depth_t[lanes], jnp.zeros((384, 256), f32)], axis=1)
        pieces = [grad_q] + [grad_kvc[:, k * WIDTH : (k + 1) * WIDTH] for k in range(3)] + [grad_p, grad_d]
        pieces = [x.reshape(16, 24, 384) for x in pieces]
        for k in range(3):
            units[group, k * 48 : k * 48 + 48, :] = jnp.concatenate(pieces[2 * k : 2 * k + 2], axis=1).astype(low_type)
    small[...] = jnp.zeros_like(small)
    small[0:72, :] = kernel_acc[...]
    for k in range(4):
        small[72 + k : 73 + k, :] = jnp.sum(sums[k], axis=0, keepdims=True)
    column = jnp.concatenate([bias_acc[...], jnp.zeros((56, 128), f32)], axis=0)
    small[76:77, 0:128] = jnp.sum(jnp.transpose(column), axis=0, keepdims=True)
    for c in range(5, 8):
        reducer.step(c, 0)
    sum3[...] = small[...]
    late.step(0)

    def finish(i, carry):
        rows = aligned(i * TILE, TILE)
        grad_own[rows, :] = input_part(b + i) + mm_nt(dq_low[rows, :], query_w[...]) + residual_grad[rows, :]
        for n in range(3):
            @pl.when(i == n)
            def _():
                for c in range(5, 8):
                    reducer.step(c, n + 1)
                late.step(n + 1)
        return carry

    lax.fori_loop(0, 3, finish, 0)
    for s in range(4, nh + 1):
        for c in range(5, 8):
            reducer.step(c, s)
        late.step(s)
    for s in range(8, bits + 1):
        early.step(s)
    for s in range(nh + 1, bits + 1):
        late.step(s)
    for k in range(extra):
        copy = reducer.copy(out, extra_got.at[k], extra_sem.at[2 * k], extra_sem.at[2 * k + 1], k)
        copy.start()
        copy.wait()
        out[...] = out[...] + extra_got[k]
    reducer.drain()
    other_copy.wait()


def back_call(dp_size, hidden, joined_grad, residual_grad, saved, units2, small2, weights):
    shape = jax.ShapeDtypeStruct
    outs = (shape((768, D), f32), shape((256, D), low_type), shape((384, 384), f32), shape(small2.shape, f32), shape((96, 384), f32))
    operands = (hidden, joined_grad, residual_grad) + tuple(saved) + (units2, small2) + tuple(weights)
    ext = 1024 + 2 * PAD
    bits = int(math.log2(dp_size)) + 1
    extra = max(0, bits - 5)
    nh = bits - extra
    dma = pltpu.SemaphoreType.DMA
    return pl.pallas_call(
        functools.partial(back_kernel, dp_size), out_shape=outs, in_specs=[VM] * 14 + [pl.BlockSpec(memory_space=pl.ANY)] + [VM] * (len(operands) - 15), out_specs=(VM,) * len(outs),
        scratch_shapes=[
            pltpu.VMEM((1024, WIDTH), f32), pltpu.VMEM((1024, WIDTH), f32), pltpu.VMEM((WIDTH, 1024), low_type),
            pltpu.VMEM((768, WIDTH), low_type), pltpu.VMEM((1024, 3 * WIDTH), low_type), pltpu.VMEM((768, WIDTH), low_type),
            pltpu.VMEM((6, ext, 128), f32), pltpu.VMEM((3, ext, 128), f32), pltpu.VMEM((6, ext, 128), f32),
            pltpu.VMEM((TILE, KERNEL * 128), f32), pltpu.VMEM((KERNEL, 8, D), f32), pltpu.VMEM((WIDTH, TILE), f32),
            pltpu.VMEM((72, WIDTH), f32), pltpu.VMEM((72, 128), f32), pltpu.VMEM((1024, 72), low_type), pltpu.VMEM((TILE, D), f32),
            pltpu.VMEM((4, 8, WIDTH), f32),
            pltpu.VMEM((256, D), low_type), pltpu.VMEM((32, 144, 384), low_type), pltpu.VMEM((96, 384), f32),
            pltpu.VMEM((8, (1 << nh) - 1, CHUNK, 384), low_type),
            pltpu.VMEM(small2.shape, f32), pltpu.VMEM((bits,) + small2.shape, f32),
            pltpu.VMEM((96, 384), low_type), pltpu.VMEM((bits, 96, 384), low_type),
            pltpu.VMEM((max(extra, 1), 384 if extra else 8, 384), f32),
            dma((8, nh)), dma((8, nh)), dma((bits,)), dma((bits,)), dma((bits,)), dma((bits,)), dma((2,)), dma((max(2 * extra, 2),)),
            pltpu.VMEM((5, 1 << (nh - 1), CHUNK, 384), low_type), dma((5,)),
        ],
        compiler_params=pltpu.CompilerParams(collective_id=0, has_side_effects=True, vmem_limit_bytes=67_000_000),
        name="mix_backward_reduce",
    )(*operands)


def exact_columns(table, rows):
    return lax.dot_general(table, rows, (((0,), (0,)), ((), ())), precision=lax.Precision.HIGHEST, preferred_element_type=f32)


FINAL_SMALL = (
    ("query_b", 72, 384), ("value_b", 73, 384), ("point_b", 74, 384), ("conv_b", 75, 384), ("out_b", 96, 768), ("gain1", 98, 768),
    ("shift1", 100, 768), ("in_b", 102, 3072), ("ffo_b", 110, 768), ("gain2", 112, 768), ("shift2", 114, 768),
)


def final_kernel(
    grad_own, got, total, small2, small3,
    input_grad, query_w, key_w, value_w, depth_w, point_w, kernel_w, kernel_b, conv_w, out_w, in_w, ffo_w, *vectors,
):
    b = lax.axis_index("branch")
    input_grad[...] = grad_own[...]
    rows = aligned((1 - b) * 512, 256)
    input_grad[rows, :] = grad_own[rows, :] + got[...].astype(f32)
    for ref, row in ((query_w, 240), (key_w, 264), (value_w, 288), (conv_w, 312), (point_w, 336)):
        ref[...] = total[row : row + 24, :]
    ffo_w[0] = total[0:48, :]
    ffo_w[1] = total[48:96, :]
    out_w[:, 0:384] = total[192:216, :]
    out_w[:, 384:768] = total[216:240, :]
    in_w[0] = total[96:144, :]
    in_w[1] = total[144:192, :]
    depth = jnp.concatenate([total[360:384, 0:128], jnp.zeros((104, 128), f32)], axis=0)
    depth_w[...] = jnp.transpose(depth)[0:KERNEL, 0:24]
    table = tap_permutation()
    kernel_w[...] = exact_columns(table, small3[0:72, :])
    column = jnp.transpose(jnp.concatenate([small3[76:77, 0:128]] * 128, axis=0))[0:72, :]
    kernel_b[...] = jnp.sum(column[:, 0:54] * table, axis=0, keepdims=True).reshape(54)
    for ref, (_, row, size) in zip(vectors, FINAL_SMALL):
        small, row = (small3, row) if row < 96 else (small2, row - 96)
        ref[...] = jnp.concatenate([small[row + k : row + k + 1, :] for k in range(size // 384)], axis=1).reshape(size)


def final_call(*operands):
    shape = lambda *s: jax.ShapeDtypeStruct(s, f32)
    outs = (
        shape(768, D), shape(24, 384), shape(24, 384), shape(24, 384), shape(KERNEL, 24), shape(24, 384), shape(54, 384), shape(54),
        shape(24, 384), shape(24, 768), shape(2, 48, 384), shape(2, 48, 384),
    ) + tuple(shape(size) for _, _, size in FINAL_SMALL)
    return pl.pallas_call(
        final_kernel, out_shape=outs, in_specs=[VM] * 5, out_specs=(VM,) * len(outs),
        compiler_params=pltpu.CompilerParams(vmem_limit_bytes=32 << 20), name="finish",
    )(*operands)


def local(
    hidden, segment_ids, query_weight, query_bias, key_weight, value_weight, value_bias, depthwise_weight,
    pointwise_weight, pointwise_bias, kernel_weight, kernel_bias, conv_value_weight, conv_value_bias, output_weight,
    output_bias, norm1_gain, norm1_shift, ffn_in_weight, ffn_in_bias, ffn_out_weight, ffn_out_bias, norm2_gain,
    norm2_shift, cotangent,
):
    dp_size = lax.axis_size("dp")
    branch = lax.axis_index("branch")
    kernel_rows = jnp.transpose(kernel_weight)
    joined, *saved = mix_call(
        hidden, segment_ids, query_weight, key_weight, value_weight, pointwise_weight, conv_value_weight,
        depthwise_weight, kernel_rows, query_bias, value_bias, pointwise_bias, conv_value_bias, kernel_bias,
    )
    layer_out, residual_grad, joined_grad, units2, small2 = ffn_call(
        hidden, joined, cotangent, output_weight, ffn_in_weight, ffn_out_weight, output_bias, norm1_gain, norm1_shift,
        ffn_in_bias, ffn_out_bias, norm2_gain, norm2_shift,
    )
    grad_own, got, out_sum, sum2, sum3 = back_call(
        dp_size, hidden, joined_grad, residual_grad, saved, units2, small2,
        (query_weight, key_weight, value_weight, pointwise_weight, conv_value_weight, depthwise_weight, kernel_rows),
    )
    share = 2 * dp_size // 32
    if share == 1:
        (
            input_grad, query_w, key_w, value_w, depth_w, point_w, kernel_w, kernel_b, conv_w, out_w, in_w, ffo_w,
            query_b, value_b, point_b, conv_b, out_b, gain1, shift1, in_b, ffo_b, gain2, shift2,
        ) = final_call(grad_own, got, out_sum, sum2, sum3)
        return (
            layer_out, input_grad, query_w, query_b, key_w, value_w, value_b, depth_w, point_w, point_b, jnp.transpose(kernel_w),
            kernel_b, conv_w, conv_b, out_w, out_b, gain1, shift1, jnp.transpose(in_w, (0, 2, 1)), in_b, ffo_w, ffo_b, gain2, shift2,
        )
    small_sum = jnp.concatenate([sum3, sum2])
    start = (1 - branch) * 512
    block = lax.dynamic_slice_in_dim(grad_own, start, 256, 0) + got.astype(f32)
    input_grad = lax.dynamic_update_slice_in_dim(grad_own, block, start, 0)
    device = lax.axis_index("dp") * 2 + branch

    def piece(start, rows):
        n = rows // share
        return lax.dynamic_slice_in_dim(out_sum, start + lax.rem(device, share) * n, n, 0)

    def small(row, size):
        return small_sum[row : row + -(-size // 384)].reshape(-1)[:size]

    kern_w = jnp.transpose(small_sum[:72].reshape(9, 8, 384)[:, :6], (2, 1, 0)).reshape(384, 54)
    kern_b = jnp.transpose(small_sum[76, :72].reshape(9, 8)[:, :6]).reshape(54)
    in_g = jnp.stack([piece(96, 48), piece(144, 48)])
    return (
        layer_out,
        input_grad,
        piece(240, 24),
        small(72, 384),
        piece(264, 24),
        piece(288, 24),
        small(73, 384),
        jnp.transpose(piece(360, 24)[:, :KERNEL]),
        piece(336, 24),
        small(74, 384),
        kern_w,
        kern_b,
        piece(312, 24),
        small(75, 384),
        jnp.concatenate([piece(192, 24), piece(216, 24)], axis=1),
        small(96, 768),
        small(98, 768),
        small(100, 768),
        jnp.transpose(in_g, (0, 2, 1)),
        small(102, 3072),
        jnp.stack([piece(0, 48), piece(48, 48)]),
        small(110, 768),
        small(112, 768),
        small(114, 768),
    )


def solution(mesh):
    tokens, copied = P(("dp", "branch"), None), P()
    in_specs = (P("dp", None), P("dp", None)) + (copied,) * 22 + (tokens,)
    out_specs = (
        tokens, tokens, tokens, copied, tokens, tokens, copied, P(None, ("dp", "branch")), tokens, copied, copied, copied,
        tokens, copied, tokens, copied, copied, copied, P(None, None, ("dp", "branch")), copied,
        P(None, ("dp", "branch"), None), copied, copied, copied,
    )
    return jax.shard_map(local, mesh=mesh, in_specs=in_specs, out_specs=out_specs, check_vma=False)
```

```python
import functools
import math

import jax
import jax.numpy as jnp
from jax import lax
from jax.experimental import pallas as pl
from jax.experimental.pallas import tpu as pltpu
from jax.sharding import PartitionSpec as P

HEADS = 6
HEAD_DIM = 64
KERNEL = 9
WIDTH = HEADS * HEAD_DIM
D = 768
TILE = 256
PAD = 8
NEG = -1e30
norm_eps = 1e-12
low_type = jnp.bfloat16
f32 = jnp.float32

VEC_SIZES = (
    ("query_bias", 384), ("value_bias", 384), ("pointwise_bias", 384), ("conv_value_bias", 384),
    ("output_bias", 768), ("norm1_gain", 768), ("norm1_shift", 768), ("ffn_in_bias", 3072),
    ("ffn_out_bias", 768), ("norm2_gain", 768), ("norm2_shift", 768), ("kernel_bias", 128),
)
VEC_AT = {}
_at = 0
for _name, _size in VEC_SIZES:
    VEC_AT[_name] = (_at, _size)
    _at += _size
VEC_TOTAL = _at


def vec(vecs_ref, name):
    at, size = VEC_AT[name]
    return vecs_ref[0:1, at : at + size]


def load_vecs(vecs, names, refs):
    for name, ref in zip(names, refs):
        at, size = VEC_AT[name]
        if name == "kernel_bias":
            size = ref.shape[0]
        vecs[0:1, at : at + size] = ref[...].astype(f32).reshape(1, size)


MIX_VECS = ("query_bias", "value_bias", "pointwise_bias", "conv_value_bias", "kernel_bias")
FFN_VECS = ("output_bias", "norm1_gain", "norm1_shift", "ffn_in_bias", "ffn_out_bias", "norm2_gain", "norm2_shift")


def mm(a, b):
    return jnp.dot(a, b, preferred_element_type=f32)


def mm_nt(a, b):
    return lax.dot_general(a, b, (((1,), (1,)), ((), ())), preferred_element_type=f32)


def mm_tn(a, b):
    return lax.dot_general(a, b, (((0,), (0,)), ((), ())), preferred_element_type=f32)


def tap_permutation():
    row = lax.broadcasted_iota(jnp.int32, (72, 54), 0)
    col = lax.broadcasted_iota(jnp.int32, (72, 54), 1)
    head = lax.rem(row, 8)
    return jnp.where((head * 9 + lax.div(row, 8) == col) & (head < HEADS), 1.0, 0.0)


def head_spread(j):
    row = lax.broadcasted_iota(jnp.int32, (72, WIDTH), 0)
    col = lax.broadcasted_iota(jnp.int32, (72, WIDTH), 1)
    return jnp.where(row == j * 8 + lax.div(col, HEAD_DIM), 1.0, 0.0).astype(low_type)


def tap_spread():
    row = lax.broadcasted_iota(jnp.int32, (72, KERNEL * 128), 0)
    col = lax.broadcasted_iota(jnp.int32, (72, KERNEL * 128), 1)
    return jnp.where(row == lax.div(col, 128) * 8, 1.0, 0.0).astype(low_type)


def aligned(start, size):
    return pl.ds(pl.multiple_of(start, size), size)


def half_rows(block, odd):
    zero = jnp.zeros((HEAD_DIM, block.shape[1]), block.dtype)
    kept = block[HEAD_DIM:] if odd else block[:HEAD_DIM]
    return jnp.concatenate([zero, kept] if odd else [kept, zero], axis=0)


def half_lanes(block, odd):
    lane = lax.broadcasted_iota(jnp.int32, block.shape, 1)
    keep = (lane >= HEAD_DIM) if odd else (lane < HEAD_DIM)
    return jnp.where(keep, block, jnp.zeros_like(block))


def shifted(pad_ref, c, start, j, size):
    return pad_ref[c, pl.ds(start + (PAD - 4 + j), size), :]


def depth_conv(pad_ref, mask_ref, weight, start, out, flip):
    for lo in range(0, TILE, 64):
        for c in range(D // 128):
            total = None
            for j in range(KERNEL):
                w = weight[KERNEL - 1 - j if flip else j][:, c * 128 : c * 128 + 128]
                term = shifted(pad_ref, c, start + lo, j, 64) * w
                if j != KERNEL // 2:
                    term = term * mask_ref[lo : lo + 64, j * 128 : j * 128 + 128]
                total = term if total is None else total + term
            out(c, lo, total)


def span_conv(pad_ref, taps, start):
    totals = [None] * (WIDTH // 128)
    for j in range(KERNEL):
        spread = mm(taps, head_spread(j))
        for c in range(WIDTH // 128):
            term = spread[:, c * 128 : c * 128 + 128] * shifted(pad_ref, c, start, j, TILE)
            totals[c] = term if totals[c] is None else totals[c] + term
    return jnp.concatenate(totals, axis=1)


def taps_softmax(logits):
    parts = [logits[j * 8 : j * 8 + 8] for j in range(KERNEL)]
    peak = functools.reduce(jnp.maximum, parts)
    parts = [jnp.exp(x - peak) for x in parts]
    scale = 1.0 / functools.reduce(jnp.add, parts)
    return jnp.concatenate([x * scale for x in parts], axis=0)


def mix_kernel(
    hidden, segments, query_w, key_w, value_w, point_w, conv_w, depth_w, kernel_w,
    vec0, vec1, vec2, vec3, vec4, joined, q_out, k_out, v_out, probs, conv_pad, taps_out, tap_mask, query_pre, key_conv, depth_low, conv_attn,
    x_pad, v_t, ctx_t, bias, seg_rows, mask_cols, vecs,
):
    load_vecs(vecs, MIX_VECS, (vec0, vec1, vec2, vec3, vec4))
    b = lax.axis_index("branch")
    base = b * 512
    segs = segments[...].astype(f32)
    row0 = jnp.where(b == 0, segs[0:1], segs[1:2])
    row1 = jnp.where(b == 0, segs[1:2], segs[2:3])
    seg_rows[0:1, :] = row0
    seg_rows[1:2, :] = row1
    seg_t = jnp.transpose(jnp.concatenate([row0, row1] * 4, axis=0))
    both = jnp.concatenate([row0, row1 + 1024.0], axis=1)
    both = jnp.broadcast_to(both, (8, 1024))
    for j in range(KERNEL):
        moved = both if j == 4 else pltpu.roll(both, (4 - j) % 1024, 1)
        tap_mask[j * 8 : j * 8 + 8, :] = jnp.where(moved == both, 1.0, 0.0)
    for c in range(D // 128):
        x_pad[c, 0:PAD, :] = jnp.zeros((PAD, 128), f32)
        x_pad[c, 1024 + PAD : 1024 + 2 * PAD, :] = jnp.zeros((PAD, 128), f32)
    for c in range(WIDTH // 128):
        conv_pad[c, 0:PAD, :] = jnp.zeros((PAD, 128), f32)
        conv_pad[c, 1024 + PAD : 1024 + 2 * PAD, :] = jnp.zeros((PAD, 128), f32)
    taps_out[...] = jnp.zeros_like(taps_out)

    def project(e, carry):
        x = hidden[aligned(base + e * TILE, TILE), :]
        rows = aligned(e * TILE, TILE)
        k_out[rows, :] = mm(x, key_w[...]).astype(low_type)
        v = mm(x, value_w[...]) + vec(vecs, "value_bias")
        v_out[rows, :] = v.astype(low_type)
        v_t[:, rows] = jnp.transpose(v).astype(low_type)
        cv = mm(x, conv_w[...]) + vec(vecs, "conv_value_bias")
        place = pl.ds(pl.multiple_of(e * TILE + PAD, 8), TILE)
        for c in range(WIDTH // 128):
            conv_pad[c, place, :] = cv[:, c * 128 : c * 128 + 128]
        for c in range(D // 128):
            x_pad[c, place, :] = x[:, c * 128 : c * 128 + 128].astype(f32)
        return carry

    lax.fori_loop(0, 4, project, 0)
    kernel_rows = mm(tap_permutation().astype(low_type), kernel_w[...]).astype(low_type)
    kernel_bias = jnp.sum(tap_permutation() * vec(vecs, "kernel_bias")[:, :54], axis=1, keepdims=True)
    depth_weights = [depth_w[j : j + 1, :].astype(f32) for j in range(KERNEL)]

    def own(i, carry):
        e = b + i
        rows = aligned(i * TILE, TILE)
        ext = aligned(e * TILE, TILE)
        x = hidden[aligned(base + e * TILE, TILE), :]
        q_pre = mm(x, query_w[...]) + vec(vecs, "query_bias")
        query_pre[rows, :] = q_pre.astype(low_type)
        q = q_pre.astype(low_type).astype(f32) * 0.125
        q_out[rows, :] = q.astype(low_type)
        q_t = jnp.transpose(q).astype(low_type)
        row = lax.div(e, 2)
        keys = aligned(row * 512, 512)
        seg_q = jnp.where(row == 0, seg_rows[0:1, :], seg_rows[1:2, :])
        seg_q = jnp.where(lax.rem(e, 2) == 0, seg_q[:, :TILE], seg_q[:, TILE:])
        seg_k = jnp.where(row == 0, seg_t[:, 0:1], seg_t[:, 1:2])
        bias[...] = jnp.where(seg_k == seg_q, 0.0, NEG)
        for h in range(HEADS):
            p = h // 2
            k_pair = k_out[keys, p * 128 : p * 128 + 128]
            scores = mm(k_pair, half_rows(q_t[p * 128 : p * 128 + 128], h % 2)) + bias[...]
            peak = jnp.max(scores, axis=0, keepdims=True)
            weight = jnp.exp(scores - peak)
            weight = (weight * (1.0 / jnp.sum(weight, axis=0, keepdims=True))).astype(low_type)
            probs[i * HEADS + h] = weight
            ctx_t[h * HEAD_DIM : (h + 1) * HEAD_DIM, :] = mm(v_t[h * HEAD_DIM : (h + 1) * HEAD_DIM, keys], weight)
        joined[rows, 0:WIDTH] = jnp.transpose(ctx_t[...]).astype(low_type)

        masks = tap_mask[:, ext]
        mask_cols[...] = mm(jnp.transpose(masks).astype(low_type), tap_spread())

        def keep(c, lo, value):
            at = pl.ds(pl.multiple_of(i * TILE + lo, 64), 64)
            depth_low[at, c * 128 : c * 128 + 128] = value.astype(low_type)

        depth_conv(x_pad, mask_cols, depth_weights, e * TILE, keep, False)
        kc = mm(depth_low[rows, :], point_w[...]) + vec(vecs, "pointwise_bias")
        key_conv[rows, :] = kc.astype(low_type)
        attn = (kc * q_pre).astype(low_type)
        conv_attn[rows, :] = attn
        taps = taps_softmax(mm_nt(kernel_rows, attn) + kernel_bias)
        taps_out[:, ext] = taps
        spread = span_conv(conv_pad, jnp.transpose(taps * masks).astype(low_type), e * TILE)
        joined[rows, WIDTH : 2 * WIDTH] = spread.astype(low_type)
        return carry

    lax.fori_loop(0, 3, own, 0)


VM = pl.BlockSpec(memory_space=pltpu.VMEM)


def mix_call(*operands):
    shape = jax.ShapeDtypeStruct
    outs = (
        shape((768, 768), low_type), shape((768, WIDTH), low_type), shape((1024, WIDTH), low_type),
        shape((1024, WIDTH), low_type), shape((18, 512, TILE), low_type), shape((3, 1024 + 2 * PAD, 128), f32),
        shape((72, 1024), f32), shape((72, 1024), f32), shape((768, WIDTH), low_type), shape((768, WIDTH), low_type),
        shape((768, D), low_type), shape((768, WIDTH), low_type),
    )
    return pl.pallas_call(
        mix_kernel, out_shape=outs, in_specs=[VM] * len(operands), out_specs=(VM,) * len(outs),
        scratch_shapes=[
            pltpu.VMEM((6, 1024 + 2 * PAD, 128), f32), pltpu.VMEM((WIDTH, 1024), low_type),
            pltpu.VMEM((WIDTH, TILE), f32), pltpu.VMEM((512, TILE), f32), pltpu.VMEM((8, 512), f32),
            pltpu.VMEM((TILE, KERNEL * 128), f32), pltpu.VMEM((1, VEC_TOTAL), f32),
        ],
        compiler_params=pltpu.CompilerParams(vmem_limit_bytes=60 << 20),
        name="mix_forward",
    )(*operands)


SMALL2 = (("output_bias", 2), ("norm1_gain", 2), ("norm1_shift", 2), ("ffn_in_bias", 8), ("ffn_out_bias", 2), ("norm2_gain", 2), ("norm2_shift", 2))


def fold_rows(values):
    return jnp.sum(values.reshape(values.shape[0] // 8, 8, values.shape[1]), axis=0)


def normalize(values):
    centered = values - jnp.mean(values, axis=1, keepdims=True)
    scale = lax.rsqrt(jnp.mean(centered * centered, axis=1, keepdims=True) + norm_eps)
    return centered * scale, scale


def norm_back(grad, unit, scale, gain):
    e = grad * gain
    return (e - jnp.mean(e, axis=1, keepdims=True) - unit * jnp.mean(e * unit, axis=1, keepdims=True)) * scale


def write_small(small, row, total):
    line = jnp.sum(total, axis=0, keepdims=True)
    for k in range(line.shape[1] // 384):
        small[row + k : row + k + 1, :] = line[:, k * 384 : k * 384 + 384]


def ffn_kernel(
    hidden, joined, cotangent, out_w, in_w, ffo_w,
    vec0, vec1, vec2, vec3, vec4, vec5, vec6,
    layer_out, residual_grad, joined_grad, units, small,
    active, inner, normed_low, outer_low, attn_low, slope, total, unit1, sums, sums_in, vecs,
):
    load_vecs(vecs, FFN_VECS, (vec0, vec1, vec2, vec3, vec4, vec5, vec6))
    b = lax.axis_index("branch")
    sums[...] = jnp.zeros_like(sums)
    sums_in[...] = jnp.zeros_like(sums_in)

    def block(i, carry):
        rows = aligned(i * TILE, TILE)
        x = hidden[aligned(b * 768 + i * TILE, TILE), :].astype(f32)
        n1, scale1 = normalize(x + mm(joined[rows, :], out_w[...]) + vec(vecs, "output_bias"))
        unit1[...] = n1
        normed = n1 * vec(vecs, "norm1_gain") + vec(vecs, "norm1_shift")
        normed_low[rows, :] = normed.astype(low_type)
        total[...] = normed + vec(vecs, "ffn_out_bias")

        def forward(c, carry):
            g, part = lax.div(c, 2), lax.rem(c, 2)
            lanes = pl.ds(pl.multiple_of(g * 384, 128), 384)
            wide = pl.ds(pl.multiple_of(part * 768, 128), 768)
            here = pl.ds(pl.multiple_of(c * 768, 128), 768)
            at = pl.ds(pl.multiple_of(VEC_AT["ffn_in_bias"][0] + c * 768, 128), 768)
            z = mm(normed_low[rows, lanes], in_w[g, :, wide]) + vecs[0:1, at]
            phi = 0.5 + 0.5 * lax.erf(z * (0.5**0.5))
            act = (z * phi).astype(low_type)
            active[rows, here] = act
            slope[:, here] = phi + z * jnp.exp(-0.5 * z * z) * ((2.0 * math.pi) ** -0.5)
            total[:, lanes] += mm(act, ffo_w[g, pl.ds(pl.multiple_of(part * 768, 128), 768), :])
            return carry

        lax.fori_loop(0, 4, forward, 0)
        n2, scale2 = normalize(total[...])
        layer_out[rows, :] = (n2 * vec(vecs, "norm2_gain") + vec(vecs, "norm2_shift")).astype(low_type)
        grad = cotangent[rows, :].astype(f32)
        sums[5] += fold_rows(grad * n2)
        sums[6] += fold_rows(grad)
        sum_grad = norm_back(grad, n2, scale2, vec(vecs, "norm2_gain"))
        outer = sum_grad.astype(low_type)
        outer_low[rows, :] = outer
        sums[4] += fold_rows(outer.astype(f32))
        total[...] = sum_grad

        def backward(c, carry):
            g, part = lax.div(c, 2), lax.rem(c, 2)
            lanes = pl.ds(pl.multiple_of(g * 384, 128), 384)
            wide = pl.ds(pl.multiple_of(part * 768, 128), 768)
            here = pl.ds(pl.multiple_of(c * 768, 128), 768)
            grad_in = mm_nt(outer_low[rows, lanes], ffo_w[g, wide, :]) * slope[:, here]
            grad_low = grad_in.astype(low_type)
            inner[rows, here] = grad_low
            sums_in[:, here] += fold_rows(grad_low.astype(f32))
            total[:, lanes] += mm_nt(grad_low, in_w[g, :, wide])
            return carry

        lax.fori_loop(0, 4, backward, 0)
        normed_grad = total[...]
        n1 = unit1[...]
        sums[1] += fold_rows(normed_grad * n1)
        sums[2] += fold_rows(normed_grad)
        grad1 = norm_back(normed_grad, n1, scale1, vec(vecs, "norm1_gain"))
        residual_grad[rows, :] = grad1
        attn = grad1.astype(low_type)
        attn_low[rows, :] = attn
        sums[0] += fold_rows(attn.astype(f32))
        joined_grad[rows, :] = mm_nt(attn, out_w[...]).astype(low_type)
        return carry

    lax.fori_loop(0, 3, block, 0)

    for g in range(2):
        lanes = slice(g * 384, g * 384 + 384)

        def weights(m, carry, g=g, lanes=lanes):
            wide = pl.ds(pl.multiple_of(g * 1536 + m * 384, 128), 384)
            group = pl.ds(m * 8, 8)
            grad_out = mm_tn(active[:, wide], outer_low[:, lanes])
            units[group, g * 48 : g * 48 + 48, :] = grad_out.reshape(8, 48, 384).astype(low_type)
            grad_in = mm_tn(inner[:, wide], normed_low[:, lanes])
            units[group, 96 + g * 48 : 144 + g * 48, :] = grad_in.reshape(8, 48, 384).astype(low_type)
            return carry

        lax.fori_loop(0, 4, weights, 0)
    for m in range(2):
        grad_w = mm_tn(joined[:, m * 384 : m * 384 + 384], attn_low[...])
        halves = [grad_w[:, :384].reshape(16, 24, 384), grad_w[:, 384:].reshape(16, 24, 384)]
        units[m * 16 : m * 16 + 16, 192:240, :] = jnp.concatenate(halves, axis=1).astype(low_type)
    small[...] = jnp.zeros_like(small)
    row = 0
    for k, (name, count) in enumerate(SMALL2):
        if name == "ffn_in_bias":
            write_small(small, row, sums_in[...])
        else:
            write_small(small, row, sums[k])
        row += count


def ffn_call(*operands):
    shape = jax.ShapeDtypeStruct
    outs = (
        shape((768, D), low_type), shape((768, D), f32), shape((768, D), low_type),
        shape((32, 240, 384), low_type), shape((32, 384), f32),
    )
    return pl.pallas_call(
        ffn_kernel, out_shape=outs, in_specs=[VM] * len(operands), out_specs=(VM,) * len(outs),
        scratch_shapes=[
            pltpu.VMEM((768, 3072), low_type), pltpu.VMEM((768, 3072), low_type),
            pltpu.VMEM((768, D), low_type), pltpu.VMEM((768, D), low_type), pltpu.VMEM((768, D), low_type),
            pltpu.VMEM((TILE, 3072), f32), pltpu.VMEM((TILE, D), f32), pltpu.VMEM((TILE, D), f32),
            pltpu.VMEM((7, 8, D), f32), pltpu.VMEM((8, 3072), f32), pltpu.VMEM((1, VEC_TOTAL), f32),
        ],
        compiler_params=pltpu.CompilerParams(vmem_limit_bytes=60 << 20),
        name="ffn",
    )(*operands)


MESH = pl.DeviceIdType.MESH
CHUNK = 48


class Reducer:
    def __init__(self, dp_size, sources, kept, kept_sem, buffer, out, send, recv):
        self.bits = int(math.log2(dp_size)) + 1
        self.extra = max(0, self.bits - 5)
        self.nh = self.bits - self.extra
        self.dp = lax.axis_index("dp")
        self.br = lax.axis_index("branch")
        self.my = [self.br] + [lax.rem(lax.div(self.dp, 1 << (k - 1)), 2) for k in range(1, self.bits)]
        self.kept, self.kept_sem = kept, kept_sem
        self.buffer, self.out, self.send, self.recv = buffer, out, send, recv
        self.sources = [(ref, row) for ref in sources for row in range(0, ref.shape[1], CHUNK)]
        halving = list(range(self.extra, self.bits))
        first = [1] if 1 in halving else []
        r = [k for k in halving if k not in first]
        turns = [(0, 2, 1), (1, 2, 0), (0, 2, 1), (1, 2, 0), (2, 0, 1), (0, 2, 1), (1, 2, 0), (2, 1, 0)]
        self.orders = [first + [r[t] for t in turn] + r[3:] for turn in turns]

    def enter(self):
        barrier = pltpu.get_barrier_semaphore()
        for k in range(self.bits):
            pl.semaphore_signal(barrier, inc=1, device_id=self.partner(k), device_id_type=MESH)
        pl.semaphore_wait(barrier, self.bits)

    def partner(self, k):
        if k == 0:
            return (self.dp, 1 - self.br)
        return (self.dp + (1 << (k - 1)) * (1 - 2 * self.my[k]), self.br)

    def copy(self, src, dst, ssem, rsem, k):
        return pltpu.make_async_remote_copy(
            src_ref=src, dst_ref=dst, send_sem=ssem, recv_sem=rsem, device_id=self.partner(k), device_id_type=MESH
        )

    def offset(self, s):
        return sum(1 << (self.nh - 1 - t) for t in range(s))

    def place(self, u, free, fixed, value):
        index, at = 0, len(free) - 1
        for k in sorted(free + [fixed], reverse=True):
            if k == fixed:
                index = index * 2 + value
            else:
                index = index * 2 + ((u >> at) & 1)
                at -= 1
        return index

    def free(self, c, s):
        return sorted(self.orders[c][s + 1 :], reverse=True)

    def whole(self, c, s):
        part = self.buffer.at[c, pl.ds(self.offset(s), 1 << (self.nh - 1 - s))]
        return self.copy(part, part, self.send.at[c, s], self.recv.at[c, s], self.orders[c][s])

    def start(self, c, s):
        k, free = self.orders[c][s], self.free(c, s)
        for u in range(1 << len(free)):
            at = self.place(u, free, k, 1 - self.my[k])
            if s == 0:
                ref, row = self.sources[c]
                src = ref.at[at, pl.ds(row, CHUNK)]
            else:
                src = self.buffer.at[c, self.offset(s - 1) + at]
            self.copy(src, self.buffer.at[c, self.offset(s) + u], self.send.at[c, s], self.recv.at[c, s], k).start()

    def fetch(self, c):
        k, free = self.orders[c][0], self.free(c, 0)
        ref, row = self.sources[c]
        for u in range(1 << len(free)):
            at = self.place(u, free, k, self.my[k])
            pltpu.make_async_copy(ref.at[at, pl.ds(row, CHUNK)], self.kept.at[c, u], self.kept_sem.at[c]).start()

    def add(self, c, s):
        fetched = c < self.kept.shape[0]
        if s == 0 and fetched:
            pltpu.make_async_copy(self.kept.at[c], self.kept.at[c], self.kept_sem.at[c]).wait()
        self.whole(c, s).wait_recv()
        k, free = self.orders[c][s], self.free(c, s)
        for u in range(1 << len(free)):
            at = self.place(u, free, k, self.my[k])
            if s == 0 and fetched:
                mine = self.kept[c, u]
            elif s == 0:
                ref, row = self.sources[c]
                mine = ref[at, row : row + CHUNK, :]
            else:
                mine = self.buffer[c, self.offset(s - 1) + at]
            total = mine.astype(f32) + self.buffer[c, self.offset(s) + u].astype(f32)
            if s == self.nh - 1:
                self.out[c * CHUNK : (c + 1) * CHUNK, :] = total
            else:
                self.buffer[c, self.offset(s) + u] = total.astype(low_type)

    def step(self, c, s):
        if s > 0:
            self.add(c, s - 1)
        if s < self.nh:
            self.start(c, s)

    def drain(self):
        for c in range(len(self.sources)):
            for s in range(self.nh):
                self.whole(c, s).wait_send()


class Doubler:
    def __init__(self, reducer, value, sent, got, send, recv):
        self.reducer, self.value, self.sent, self.got, self.send, self.recv = reducer, value, sent, got, send, recv
        self.order = reducer.orders[0] + list(range(reducer.extra))

    def copy(self, s):
        return self.reducer.copy(self.sent, self.got.at[s], self.send.at[s], self.recv.at[s], self.order[s])

    def step(self, s):
        if s > 0:
            copy = self.copy(s - 1)
            copy.wait()
            self.value[...] = self.sent[...].astype(f32) + self.got[s - 1].astype(f32)
        if s < len(self.order):
            self.sent[...] = self.value[...].astype(self.sent.dtype)
            self.copy(s).start()


EARLY_STEPS = {
    (0, 1): [(0, 1), (1, 1)],
    (0, 2): [(2, 1), (3, 1)],
    (0, 3): [(4, 1)],
    (1, 1): [(0, 2), (1, 2)],
    (1, 3): [(2, 2), (3, 2), (4, 2)],
    (2, 2): [(0, 3), (1, 3), (4, 3)],
    (2, 3): [(0, 4), (1, 4), (4, 4)],
}


def back_kernel(
    dp_size, hidden, joined_grad, residual_grad, q_in, k_in, v_in, probs, conv_pad, taps, tap_mask, query_pre, key_conv, depth_low,
    conv_attn, units2, small2, query_w, key_w, value_w, point_w, conv_w, depth_w, kernel_w,
    grad_own, got_other, out, small_sum,
    dk_acc, dv_acc, k_t, dq_low, kvc, key_conv_low, dg_pad, cg_pad, x_pad, mask_cols, dw_acc, dq_t, kernel_acc, bias_acc, moved_taps, part,
    sums, grad_other, units, buffer, sent3, got3, extra_got,
    send, recv, send3, recv3, other_sem, extra_sem, kept, kept_sem,
):
    reducer = Reducer(dp_size, (units2, units), kept, kept_sem, buffer, out, send, recv)
    nh, bits, extra = reducer.nh, reducer.bits, reducer.extra
    late = Doubler(reducer, small_sum, sent3, got3, send3, recv3)
    other_copy = reducer.copy(grad_other, got_other, other_sem.at[0], other_sem.at[1], 0)
    for c in range(5):
        reducer.fetch(c)
    reducer.enter()
    for c in range(5):
        reducer.step(c, 0)
    def run(steps):
        for c, stage in steps:
            reducer.step(c, stage)

    def advance_at(i, spot):
        for (n, at), steps in EARLY_STEPS.items():
            if at == spot:
                @pl.when(i == n)
                def _(steps=steps):
                    run(steps)

    b = lax.axis_index("branch")
    base = b * 512
    for ref in (dk_acc, dv_acc, dg_pad, cg_pad, dw_acc, kernel_acc, bias_acc, sums):
        ref[...] = jnp.zeros_like(ref)
    for c in range(D // 128):
        x_pad[c, 0:PAD, :] = jnp.zeros((PAD, 128), f32)
        x_pad[c, 1024 + PAD : 1024 + 2 * PAD, :] = jnp.zeros((PAD, 128), f32)

    def prepare(e, carry):
        rows = aligned(e * TILE, TILE)
        k_t[:, rows] = jnp.transpose(k_in[rows, :].astype(f32)).astype(low_type)
        x = hidden[aligned(base + e * TILE, TILE), :]
        place = pl.ds(pl.multiple_of(e * TILE + PAD, 8), TILE)
        for c in range(D // 128):
            x_pad[c, place, :] = x[:, c * 128 : c * 128 + 128].astype(f32)
        return carry

    lax.fori_loop(0, 4, prepare, 0)
    kernel_rows = mm(tap_permutation().astype(low_type), kernel_w[...]).astype(low_type)
    depth_weights = [depth_w[j : j + 1, :].astype(f32) for j in range(KERNEL)]
    head_rows = head_spread(0)[:8]
    moved = []
    for j in range(KERNEL):
        rows = taps[(8 - j) * 8 : (8 - j) * 8 + 8, :]
        rows = rows if j == 4 else pltpu.roll(rows, (4 - j) % 1024, 1)
        moved.append(rows * tap_mask[j * 8 : j * 8 + 8, :])
    moved_taps[...] = jnp.transpose(jnp.concatenate(moved, axis=0)).astype(low_type)

    def own(i, carry):
        e = b + i
        rows = aligned(i * TILE, TILE)
        ext = aligned(e * TILE, TILE)
        place = pl.ds(pl.multiple_of(e * TILE + PAD, 8), TILE)
        keys = aligned(lax.div(e, 2) * 512, 512)
        d_ctx = joined_grad[rows, 0:WIDTH]
        d_ctx_t = jnp.transpose(d_ctx.astype(f32)).astype(low_type)
        for p in range(HEADS // 2):
            lanes = slice(p * 128, p * 128 + 128)
            v_pair = v_in[keys, lanes]
            q_pair = q_in[rows, lanes]
            d_pair = d_ctx[:, lanes]
            scores, weights = [], []
            for odd in range(2):
                h = 2 * p + odd
                weight = probs[i * HEADS + h]
                prob_grad = mm(v_pair, half_rows(d_ctx_t[lanes], odd))
                wide = weight.astype(f32)
                term = wide * prob_grad
                score = (term - wide * jnp.sum(term, axis=0, keepdims=True)).astype(low_type)
                dq_t[h * HEAD_DIM : (h + 1) * HEAD_DIM, :] = mm(k_t[h * HEAD_DIM : (h + 1) * HEAD_DIM, keys], score)
                scores.append(score)
                weights.append(weight)
            q_both = jnp.concatenate([half_lanes(q_pair, 0), half_lanes(q_pair, 1)], axis=0)
            d_both = jnp.concatenate([half_lanes(d_pair, 0), half_lanes(d_pair, 1)], axis=0)
            dk_acc[keys, lanes] += mm(jnp.concatenate(scores, axis=1), q_both)
            dv_acc[keys, lanes] += mm(jnp.concatenate(weights, axis=1), d_both)
            advance_at(i, p)
        query_low = (jnp.transpose(dq_t[...]) * 0.125).astype(low_type)

        grad = joined_grad[rows, WIDTH : 2 * WIDTH].astype(f32)
        for c in range(WIDTH // 128):
            cg_pad[c, place, :] = grad[:, c * 128 : c * 128 + 128]
        grads = []
        for j in range(KERNEL):
            pieces = [
                (grad[:, c * 128 : c * 128 + 128] * shifted(conv_pad, c, e * TILE, j, TILE)).astype(low_type)
                for c in range(WIDTH // 128)
            ]
            grads.append(mm_nt(head_rows, jnp.concatenate(pieces, axis=1)) * tap_mask[j * 8 : j * 8 + 8, ext])
        kept = taps[:, ext]
        level = functools.reduce(jnp.add, [grads[j] * kept[j * 8 : j * 8 + 8] for j in range(KERNEL)])
        logit = kept * jnp.concatenate([x - level for x in grads], axis=0)
        logit_low = logit.astype(low_type)
        logit_wide = logit_low.astype(f32)
        kernel_acc[...] += mm(logit_low, conv_attn[rows, :])
        bias_acc[...] += logit_wide[:, :128] + logit_wide[:, 128:]
        span = mm(jnp.transpose(logit_wide).astype(low_type), kernel_rows).astype(low_type).astype(f32)
        point_low = (span * query_pre[rows, :].astype(f32)).astype(low_type)
        query_conv = (span * key_conv[rows, :].astype(f32)).astype(low_type)
        key_conv_low[rows, :] = point_low
        sums[2] += fold_rows(point_low.astype(f32))
        both = query_low.astype(f32) + query_conv.astype(f32)
        sums[0] += fold_rows(both)
        dq_low[rows, :] = both.astype(low_type)
        d_depth = mm_nt(point_low, point_w[...])
        for c in range(D // 128):
            dg_pad[c, place, :] = d_depth[:, c * 128 : c * 128 + 128]
        mask_cols[...] = mm(jnp.transpose(tap_mask[:, ext]).astype(low_type), tap_spread())
        for c in range(D // 128):
            totals = [None] * KERNEL
            for lo in range(0, TILE, 64):
                grad_rows = dg_pad[c, pl.ds(e * TILE + (PAD + lo), 64), :]
                for j in range(KERNEL):
                    term = shifted(x_pad, c, e * TILE + lo, j, 64) * grad_rows
                    if j != KERNEL // 2:
                        term = term * mask_cols[lo : lo + 64, j * 128 : j * 128 + 128]
                    term = fold_rows(term)
                    totals[j] = term if lo == 0 else totals[j] + term
            for j in range(KERNEL):
                dw_acc[j, :, c * 128 : c * 128 + 128] += totals[j]
        advance_at(i, 3)
        return carry

    lax.fori_loop(0, 3, own, 0)

    def settle(e, carry):
        ext = aligned(e * TILE, TILE)
        dv = dv_acc[ext, :].astype(low_type)
        kvc[ext, 0:WIDTH] = dk_acc[ext, :].astype(low_type)
        kvc[ext, WIDTH : 2 * WIDTH] = dv
        sums[1] += fold_rows(dv.astype(f32))
        return carry

    def pack(k, first, second):
        for m in range(2):
            lanes = slice(m * 384, m * 384 + 384)
            pieces = [part_of(lanes).reshape(16, 24, 384) for part_of in (first, second)]
            units[m * 16 : m * 16 + 16, k * 48 : k * 48 + 48, :] = jnp.concatenate(pieces, axis=1).astype(low_type)

    def token_grad(k):
        return lambda lanes: mm_tn(hidden[aligned(base, 512), lanes], kvc[0:512, k * WIDTH : (k + 1) * WIDTH]) + mm_tn(
            hidden[aligned(base + 512, 512), lanes], kvc[512:1024, k * WIDTH : (k + 1) * WIDTH]
        )

    lax.fori_loop(0, 4, settle, 0)
    own_tokens = pl.ds(pl.multiple_of(b * 768, 256), 768)
    pack(0, lambda lanes: mm_tn(hidden[own_tokens, lanes], dq_low[...]), token_grad(0))
    run([(5, 0), (2, 3), (3, 3)])
    depth_total = jnp.sum(dw_acc[...], axis=1)
    depth_t = jnp.transpose(jnp.concatenate([depth_total, jnp.zeros((128 - KERNEL, D), f32)], axis=0))
    pack(
        2,
        lambda lanes: mm_tn(depth_low[:, lanes], key_conv_low[...]),
        lambda lanes: jnp.concatenate([depth_t[lanes], jnp.zeros((384, 256), f32)], axis=1),
    )
    run([(7, 0)])

    def spans(e, carry):
        ext = aligned(e * TILE, TILE)
        dc = span_conv(cg_pad, moved_taps[ext, :], e * TILE).astype(low_type)
        kvc[ext, 2 * WIDTH : 3 * WIDTH] = dc
        sums[3] += fold_rows(dc.astype(f32))
        return carry

    lax.fori_loop(0, 4, spans, 0)
    run([(2, 4), (3, 4), (0, 5), (1, 5), (4, 5)])
    small_sum[...] = jnp.zeros_like(small_sum)
    small_sum[0:72, :] = kernel_acc[...]
    for k in range(4):
        small_sum[72 + k : 73 + k, :] = jnp.sum(sums[k], axis=0, keepdims=True)
    column = jnp.concatenate([bias_acc[...], jnp.zeros((56, 128), f32)], axis=0)
    small_sum[76:77, 0:128] = jnp.sum(jnp.transpose(column), axis=0, keepdims=True)
    small_sum[80:104, :] = small2[0:24, :]
    late.step(0)
    run([(5, 1), (7, 1)])
    pack(1, token_grad(1), token_grad(2))
    run([(6, 0)])
    late.step(1)
    def input_part(e):
        ext = aligned(e * TILE, TILE)
        mask_cols[...] = mm(jnp.transpose(tap_mask[:, ext]).astype(low_type), tap_spread())

        def keep(c, lo, value):
            part[lo : lo + 64, c * 128 : c * 128 + 128] = value

        depth_conv(dg_pad, mask_cols, depth_weights, e * TILE, keep, True)
        pieces = [kvc[ext, k * WIDTH : (k + 1) * WIDTH] for k in range(3)]
        return part[...] + mm_nt(pieces[0], key_w[...]) + mm_nt(pieces[1], value_w[...]) + mm_nt(pieces[2], conv_w[...])

    grad_other[...] = input_part(3 * (1 - b)).astype(low_type)
    run([(6, 1), (2, 5), (3, 5)])
    other_copy.start()

    def finish(i, carry):
        rows = aligned(i * TILE, TILE)
        grad_own[rows, :] = input_part(b + i) + mm_nt(dq_low[rows, :], query_w[...]) + residual_grad[rows, :]
        return carry

    lax.fori_loop(0, 3, finish, 0)
    for stage in range(2, 6):
        late.step(stage)
        run([(c, stage) for c in (5, 7, 6)])
    for s in range(6, nh + 1):
        for c in range(8):
            reducer.step(c, s)
    for s in range(6, bits + 1):
        late.step(s)
    for k in range(extra):
        copy = reducer.copy(out, extra_got.at[k], extra_sem.at[2 * k], extra_sem.at[2 * k + 1], k)
        copy.start()
        copy.wait()
        out[...] = out[...] + extra_got[k]
    reducer.drain()
    other_copy.wait()


def back_call(dp_size, hidden, joined_grad, residual_grad, saved, units2, small2, weights):
    shape = jax.ShapeDtypeStruct
    outs = (shape((768, D), f32), shape((256, D), low_type), shape((384, 384), f32), shape((104, 384), f32))
    operands = (hidden, joined_grad, residual_grad) + tuple(saved) + (units2, small2) + tuple(weights)
    ext = 1024 + 2 * PAD
    bits = int(math.log2(dp_size)) + 1
    extra = max(0, bits - 5)
    nh = bits - extra
    dma = pltpu.SemaphoreType.DMA
    return pl.pallas_call(
        functools.partial(back_kernel, dp_size), out_shape=outs, in_specs=[VM] * 14 + [pl.BlockSpec(memory_space=pl.ANY)] + [VM] * (len(operands) - 15), out_specs=(VM,) * len(outs),
        scratch_shapes=[
            pltpu.VMEM((1024, WIDTH), f32), pltpu.VMEM((1024, WIDTH), f32), pltpu.VMEM((WIDTH, 1024), low_type),
            pltpu.VMEM((768, WIDTH), low_type), pltpu.VMEM((1024, 3 * WIDTH), low_type), pltpu.VMEM((768, WIDTH), low_type),
            pltpu.VMEM((6, ext, 128), f32), pltpu.VMEM((3, ext, 128), f32), pltpu.VMEM((6, ext, 128), f32),
            pltpu.VMEM((TILE, KERNEL * 128), f32), pltpu.VMEM((KERNEL, 8, D), f32), pltpu.VMEM((WIDTH, TILE), f32),
            pltpu.VMEM((72, WIDTH), f32), pltpu.VMEM((72, 128), f32), pltpu.VMEM((1024, 72), low_type), pltpu.VMEM((TILE, D), f32),
            pltpu.VMEM((4, 8, WIDTH), f32),
            pltpu.VMEM((256, D), low_type), pltpu.VMEM((32, 144, 384), low_type),
            pltpu.VMEM((8, (1 << nh) - 1, CHUNK, 384), low_type),
            pltpu.VMEM((104, 384), low_type), pltpu.VMEM((bits, 104, 384), low_type),
            pltpu.VMEM((max(extra, 1), 384 if extra else 8, 384), f32),
            dma((8, nh)), dma((8, nh)), dma((bits,)), dma((bits,)), dma((2,)), dma((max(2 * extra, 2),)),
            pltpu.VMEM((5, 1 << (nh - 1), CHUNK, 384), low_type), dma((5,)),
        ],
        compiler_params=pltpu.CompilerParams(collective_id=0, has_side_effects=True, vmem_limit_bytes=67_000_000),
        name="mix_backward_reduce",
    )(*operands)


def exact_columns(table, rows):
    return lax.dot_general(table, rows, (((0,), (0,)), ((), ())), precision=lax.Precision.HIGHEST, preferred_element_type=f32)


FINAL_SMALL = (
    ("query_b", 72, 384), ("value_b", 73, 384), ("point_b", 74, 384), ("conv_b", 75, 384), ("out_b", 80, 768), ("gain1", 82, 768),
    ("shift1", 84, 768), ("in_b", 86, 3072), ("ffo_b", 94, 768), ("gain2", 96, 768), ("shift2", 98, 768),
)


def final_kernel(
    grad_own, got, total, small,
    input_grad, query_w, key_w, value_w, depth_w, point_w, kernel_w, kernel_b, conv_w, out_w, in_w, ffo_w, *vectors,
):
    b = lax.axis_index("branch")
    input_grad[...] = grad_own[...]
    rows = aligned((1 - b) * 512, 256)
    input_grad[rows, :] = grad_own[rows, :] + got[...].astype(f32)
    for ref, row in ((query_w, 240), (key_w, 264), (value_w, 288), (conv_w, 312), (point_w, 336)):
        ref[...] = total[row : row + 24, :]
    ffo_w[0] = total[0:48, :]
    ffo_w[1] = total[48:96, :]
    out_w[:, 0:384] = total[192:216, :]
    out_w[:, 384:768] = total[216:240, :]
    in_w[0] = total[96:144, :]
    in_w[1] = total[144:192, :]
    depth = jnp.concatenate([total[360:384, 0:128], jnp.zeros((104, 128), f32)], axis=0)
    depth_w[...] = jnp.transpose(depth)[0:KERNEL, 0:24]
    table = tap_permutation()
    kernel_w[...] = exact_columns(table, small[0:72, :])
    column = jnp.transpose(jnp.concatenate([small[76:77, 0:128]] * 128, axis=0))[0:72, :]
    kernel_b[...] = jnp.sum(column[:, 0:54] * table, axis=0, keepdims=True).reshape(54)
    for ref, (_, row, size) in zip(vectors, FINAL_SMALL):
        ref[...] = jnp.concatenate([small[row + k : row + k + 1, :] for k in range(size // 384)], axis=1).reshape(size)


def final_call(*operands):
    shape = lambda *s: jax.ShapeDtypeStruct(s, f32)
    outs = (
        shape(768, D), shape(24, 384), shape(24, 384), shape(24, 384), shape(KERNEL, 24), shape(24, 384), shape(54, 384), shape(54),
        shape(24, 384), shape(24, 768), shape(2, 48, 384), shape(2, 48, 384),
    ) + tuple(shape(size) for _, _, size in FINAL_SMALL)
    return pl.pallas_call(
        final_kernel, out_shape=outs, in_specs=[VM] * 4, out_specs=(VM,) * len(outs),
        compiler_params=pltpu.CompilerParams(vmem_limit_bytes=32 << 20), name="finish",
    )(*operands)


def local(
    hidden, segment_ids, query_weight, query_bias, key_weight, value_weight, value_bias, depthwise_weight,
    pointwise_weight, pointwise_bias, kernel_weight, kernel_bias, conv_value_weight, conv_value_bias, output_weight,
    output_bias, norm1_gain, norm1_shift, ffn_in_weight, ffn_in_bias, ffn_out_weight, ffn_out_bias, norm2_gain,
    norm2_shift, cotangent,
):
    dp_size = lax.axis_size("dp")
    branch = lax.axis_index("branch")
    kernel_rows = jnp.transpose(kernel_weight)
    joined, *saved = mix_call(
        hidden, segment_ids, query_weight, key_weight, value_weight, pointwise_weight, conv_value_weight,
        depthwise_weight, kernel_rows, query_bias, value_bias, pointwise_bias, conv_value_bias, kernel_bias,
    )
    layer_out, residual_grad, joined_grad, units2, small2 = ffn_call(
        hidden, joined, cotangent, output_weight, ffn_in_weight, ffn_out_weight, output_bias, norm1_gain, norm1_shift,
        ffn_in_bias, ffn_out_bias, norm2_gain, norm2_shift,
    )
    grad_own, got, out_sum, small_sum = back_call(
        dp_size, hidden, joined_grad, residual_grad, saved, units2, small2,
        (query_weight, key_weight, value_weight, pointwise_weight, conv_value_weight, depthwise_weight, kernel_rows),
    )
    share = 2 * dp_size // 32
    if share == 1:
        (
            input_grad, query_w, key_w, value_w, depth_w, point_w, kernel_w, kernel_b, conv_w, out_w, in_w, ffo_w,
            query_b, value_b, point_b, conv_b, out_b, gain1, shift1, in_b, ffo_b, gain2, shift2,
        ) = final_call(grad_own, got, out_sum, small_sum)
        return (
            layer_out, input_grad, query_w, query_b, key_w, value_w, value_b, depth_w, point_w, point_b, jnp.transpose(kernel_w),
            kernel_b, conv_w, conv_b, out_w, out_b, gain1, shift1, jnp.transpose(in_w, (0, 2, 1)), in_b, ffo_w, ffo_b, gain2, shift2,
        )
    start = (1 - branch) * 512
    block = lax.dynamic_slice_in_dim(grad_own, start, 256, 0) + got.astype(f32)
    input_grad = lax.dynamic_update_slice_in_dim(grad_own, block, start, 0)
    device = lax.axis_index("dp") * 2 + branch

    def piece(start, rows):
        n = rows // share
        return lax.dynamic_slice_in_dim(out_sum, start + lax.rem(device, share) * n, n, 0)

    def small(row, size):
        return small_sum[row : row + -(-size // 384)].reshape(-1)[:size]

    kern_w = jnp.transpose(small_sum[:72].reshape(9, 8, 384)[:, :6], (2, 1, 0)).reshape(384, 54)
    kern_b = jnp.transpose(small_sum[76, :72].reshape(9, 8)[:, :6]).reshape(54)
    in_g = jnp.stack([piece(96, 48), piece(144, 48)])
    return (
        layer_out,
        input_grad,
        piece(240, 24),
        small(72, 384),
        piece(264, 24),
        piece(288, 24),
        small(73, 384),
        jnp.transpose(piece(360, 24)[:, :KERNEL]),
        piece(336, 24),
        small(74, 384),
        kern_w,
        kern_b,
        piece(312, 24),
        small(75, 384),
        jnp.concatenate([piece(192, 24), piece(216, 24)], axis=1),
        small(80, 768),
        small(82, 768),
        small(84, 768),
        jnp.transpose(in_g, (0, 2, 1)),
        small(86, 3072),
        jnp.stack([piece(0, 48), piece(48, 48)]),
        small(94, 768),
        small(96, 768),
        small(98, 768),
    )


def solution(mesh):
    tokens, copied = P(("dp", "branch"), None), P()
    in_specs = (P("dp", None), P("dp", None)) + (copied,) * 22 + (tokens,)
    out_specs = (
        tokens, tokens, tokens, copied, tokens, tokens, copied, P(None, ("dp", "branch")), tokens, copied, copied, copied,
        tokens, copied, tokens, copied, copied, copied, P(None, None, ("dp", "branch")), copied,
        P(None, ("dp", "branch"), None), copied, copied, copied,
    )
    return jax.shard_map(local, mesh=mesh, in_specs=in_specs, out_specs=out_specs, check_vma=False)
```

```python
import functools
import math

import jax
import jax.numpy as jnp
from jax import lax
from jax.experimental import pallas as pl
from jax.experimental.pallas import tpu as pltpu
from jax.sharding import PartitionSpec as P

HEADS = 6
HEAD_DIM = 64
KERNEL = 9
WIDTH = HEADS * HEAD_DIM
D = 768
TILE = 256
PAD = 8
NEG = -1e30
norm_eps = 1e-12
low_type = jnp.bfloat16
f32 = jnp.float32

VEC_SIZES = (
    ("query_bias", 384), ("value_bias", 384), ("pointwise_bias", 384), ("conv_value_bias", 384),
    ("output_bias", 768), ("norm1_gain", 768), ("norm1_shift", 768), ("ffn_in_bias", 3072),
    ("ffn_out_bias", 768), ("norm2_gain", 768), ("norm2_shift", 768), ("kernel_bias", 128),
)
VEC_AT = {}
_at = 0
for _name, _size in VEC_SIZES:
    VEC_AT[_name] = (_at, _size)
    _at += _size
VEC_TOTAL = _at


def vec(vecs_ref, name):
    at, size = VEC_AT[name]
    return vecs_ref[0:1, at : at + size]


def load_vecs(vecs, names, refs):
    for name, ref in zip(names, refs):
        at, size = VEC_AT[name]
        if name == "kernel_bias":
            size = ref.shape[0]
        vecs[0:1, at : at + size] = ref[...].astype(f32).reshape(1, size)


MIX_VECS = ("query_bias", "value_bias", "pointwise_bias", "conv_value_bias", "kernel_bias")
FFN_VECS = ("output_bias", "norm1_gain", "norm1_shift", "ffn_in_bias", "ffn_out_bias", "norm2_gain", "norm2_shift")


def mm(a, b):
    return jnp.dot(a, b, preferred_element_type=f32)


def mm_nt(a, b):
    return lax.dot_general(a, b, (((1,), (1,)), ((), ())), preferred_element_type=f32)


def mm_tn(a, b):
    return lax.dot_general(a, b, (((0,), (0,)), ((), ())), preferred_element_type=f32)


def tap_permutation():
    row = lax.broadcasted_iota(jnp.int32, (72, 54), 0)
    col = lax.broadcasted_iota(jnp.int32, (72, 54), 1)
    head = lax.rem(row, 8)
    return jnp.where((head * 9 + lax.div(row, 8) == col) & (head < HEADS), 1.0, 0.0)


def head_spread(j):
    row = lax.broadcasted_iota(jnp.int32, (72, WIDTH), 0)
    col = lax.broadcasted_iota(jnp.int32, (72, WIDTH), 1)
    return jnp.where(row == j * 8 + lax.div(col, HEAD_DIM), 1.0, 0.0).astype(low_type)


def tap_spread():
    row = lax.broadcasted_iota(jnp.int32, (72, KERNEL * 128), 0)
    col = lax.broadcasted_iota(jnp.int32, (72, KERNEL * 128), 1)
    return jnp.where(row == lax.div(col, 128) * 8, 1.0, 0.0).astype(low_type)


def aligned(start, size):
    return pl.ds(pl.multiple_of(start, size), size)


def half_rows(block, odd):
    zero = jnp.zeros((HEAD_DIM, block.shape[1]), block.dtype)
    kept = block[HEAD_DIM:] if odd else block[:HEAD_DIM]
    return jnp.concatenate([zero, kept] if odd else [kept, zero], axis=0)


def half_lanes(block, odd):
    lane = lax.broadcasted_iota(jnp.int32, block.shape, 1)
    keep = (lane >= HEAD_DIM) if odd else (lane < HEAD_DIM)
    return jnp.where(keep, block, jnp.zeros_like(block))


def shifted(pad_ref, c, start, j, size):
    return pad_ref[c, pl.ds(start + (PAD - 4 + j), size), :]


def depth_conv(pad_ref, mask_ref, weight, start, out, flip):
    for lo in range(0, TILE, 64):
        for c in range(D // 128):
            total = None
            for j in range(KERNEL):
                w = weight[KERNEL - 1 - j if flip else j][:, c * 128 : c * 128 + 128]
                term = shifted(pad_ref, c, start + lo, j, 64) * w
                if j != KERNEL // 2:
                    term = term * mask_ref[lo : lo + 64, j * 128 : j * 128 + 128]
                total = term if total is None else total + term
            out(c, lo, total)


def span_conv(pad_ref, taps, start):
    totals = [None] * (WIDTH // 128)
    for j in range(KERNEL):
        spread = mm(taps, head_spread(j))
        for c in range(WIDTH // 128):
            term = spread[:, c * 128 : c * 128 + 128] * shifted(pad_ref, c, start, j, TILE)
            totals[c] = term if totals[c] is None else totals[c] + term
    return jnp.concatenate(totals, axis=1)


def taps_softmax(logits):
    parts = [logits[j * 8 : j * 8 + 8] for j in range(KERNEL)]
    peak = functools.reduce(jnp.maximum, parts)
    parts = [jnp.exp(x - peak) for x in parts]
    scale = 1.0 / functools.reduce(jnp.add, parts)
    return jnp.concatenate([x * scale for x in parts], axis=0)


def mix_kernel(
    hidden, segments, query_w, key_w, value_w, point_w, conv_w, depth_w, kernel_w,
    vec0, vec1, vec2, vec3, vec4, joined, q_out, k_out, v_out, probs, conv_pad, taps_out, tap_mask, query_pre, key_conv, depth_low, conv_attn,
    x_pad, v_t, ctx_t, bias, seg_rows, mask_cols, vecs, probs_held, pad_held, out_sem,
):
    load_vecs(vecs, MIX_VECS, (vec0, vec1, vec2, vec3, vec4))
    b = lax.axis_index("branch")
    base = b * 512
    segs = segments[...].astype(f32)
    row0 = jnp.where(b == 0, segs[0:1], segs[1:2])
    row1 = jnp.where(b == 0, segs[1:2], segs[2:3])
    seg_rows[0:1, :] = row0
    seg_rows[1:2, :] = row1
    seg_t = jnp.transpose(jnp.concatenate([row0, row1] * 4, axis=0))
    both = jnp.concatenate([row0, row1 + 1024.0], axis=1)
    both = jnp.broadcast_to(both, (8, 1024))
    for j in range(KERNEL):
        moved = both if j == 4 else pltpu.roll(both, (4 - j) % 1024, 1)
        tap_mask[j * 8 : j * 8 + 8, :] = jnp.where(moved == both, 1.0, 0.0)
    for c in range(D // 128):
        x_pad[c, 0:PAD, :] = jnp.zeros((PAD, 128), f32)
        x_pad[c, 1024 + PAD : 1024 + 2 * PAD, :] = jnp.zeros((PAD, 128), f32)
    for c in range(WIDTH // 128):
        pad_held[c, 0:PAD, :] = jnp.zeros((PAD, 128), f32)
        pad_held[c, 1024 + PAD : 1024 + 2 * PAD, :] = jnp.zeros((PAD, 128), f32)
    taps_out[...] = jnp.zeros_like(taps_out)

    def project(e, carry):
        x = hidden[aligned(base + e * TILE, TILE), :]
        rows = aligned(e * TILE, TILE)
        k_out[rows, :] = mm(x, key_w[...]).astype(low_type)
        v = mm(x, value_w[...]) + vec(vecs, "value_bias")
        v_out[rows, :] = v.astype(low_type)
        v_t[:, rows] = jnp.transpose(v).astype(low_type)
        cv = mm(x, conv_w[...]) + vec(vecs, "conv_value_bias")
        place = pl.ds(pl.multiple_of(e * TILE + PAD, 8), TILE)
        for c in range(WIDTH // 128):
            pad_held[c, place, :] = cv[:, c * 128 : c * 128 + 128]
        for c in range(D // 128):
            x_pad[c, place, :] = x[:, c * 128 : c * 128 + 128].astype(f32)
        return carry

    lax.fori_loop(0, 4, project, 0, unroll=2)
    kernel_rows = mm(tap_permutation().astype(low_type), kernel_w[...]).astype(low_type)
    kernel_bias = jnp.sum(tap_permutation() * vec(vecs, "kernel_bias")[:, :54], axis=1, keepdims=True)
    depth_weights = [depth_w[j : j + 1, :].astype(f32) for j in range(KERNEL)]

    def probs_copy(i):
        heads = pl.ds(i * HEADS, HEADS)
        return pltpu.make_async_copy(probs_held.at[heads], probs.at[heads], out_sem.at[i])

    pad_copy = pltpu.make_async_copy(pad_held, conv_pad, out_sem.at[3])
    pad_copy.start()

    def own(i, carry):
        e = b + i
        rows = aligned(i * TILE, TILE)
        ext = aligned(e * TILE, TILE)
        x = hidden[aligned(base + e * TILE, TILE), :]
        q_pre = mm(x, query_w[...]) + vec(vecs, "query_bias")
        query_pre[rows, :] = q_pre.astype(low_type)
        q = q_pre.astype(low_type).astype(f32) * 0.125
        q_out[rows, :] = q.astype(low_type)
        q_t = jnp.transpose(q).astype(low_type)
        row = lax.div(e, 2)
        keys = aligned(row * 512, 512)
        seg_q = jnp.where(row == 0, seg_rows[0:1, :], seg_rows[1:2, :])
        seg_q = jnp.where(lax.rem(e, 2) == 0, seg_q[:, :TILE], seg_q[:, TILE:])
        seg_k = jnp.where(row == 0, seg_t[:, 0:1], seg_t[:, 1:2])
        bias[...] = jnp.where(seg_k == seg_q, 0.0, NEG)
        for h in range(HEADS):
            p = h // 2
            k_pair = k_out[keys, p * 128 : p * 128 + 128]
            scores = mm(k_pair, half_rows(q_t[p * 128 : p * 128 + 128], h % 2)) + bias[...]
            peak = jnp.max(scores, axis=0, keepdims=True)
            weight = jnp.exp(scores - peak)
            weight = (weight * (1.0 / jnp.sum(weight, axis=0, keepdims=True))).astype(low_type)
            probs_held[i * HEADS + h] = weight
            ctx_t[h * HEAD_DIM : (h + 1) * HEAD_DIM, :] = mm(v_t[h * HEAD_DIM : (h + 1) * HEAD_DIM, keys], weight)
        probs_copy(i).start()
        joined[rows, 0:WIDTH] = jnp.transpose(ctx_t[...]).astype(low_type)

        masks = tap_mask[:, ext]
        mask_cols[...] = mm(jnp.transpose(masks).astype(low_type), tap_spread())

        def keep(c, lo, value):
            at = pl.ds(pl.multiple_of(i * TILE + lo, 64), 64)
            depth_low[at, c * 128 : c * 128 + 128] = value.astype(low_type)

        depth_conv(x_pad, mask_cols, depth_weights, e * TILE, keep, False)
        kc = mm(depth_low[rows, :], point_w[...]) + vec(vecs, "pointwise_bias")
        key_conv[rows, :] = kc.astype(low_type)
        attn = (kc * q_pre).astype(low_type)
        conv_attn[rows, :] = attn
        taps = taps_softmax(mm_nt(kernel_rows, attn) + kernel_bias)
        taps_out[:, ext] = taps
        spread = span_conv(pad_held, jnp.transpose(taps * masks).astype(low_type), e * TILE)
        joined[rows, WIDTH : 2 * WIDTH] = spread.astype(low_type)
        return carry

    lax.fori_loop(0, 3, own, 0)
    for i in range(3):
        probs_copy(i).wait()
    pad_copy.wait()


VM = pl.BlockSpec(memory_space=pltpu.VMEM)
ANY = pl.BlockSpec(memory_space=pl.ANY)


def mix_call(*operands):
    shape = jax.ShapeDtypeStruct
    outs = (
        shape((768, 768), low_type), shape((768, WIDTH), low_type), shape((1024, WIDTH), low_type),
        shape((1024, WIDTH), low_type), shape((18, 512, TILE), low_type), shape((3, 1024 + 2 * PAD, 128), f32),
        shape((72, 1024), f32), shape((72, 1024), f32), shape((768, WIDTH), low_type), shape((768, WIDTH), low_type),
        shape((768, D), low_type), shape((768, WIDTH), low_type),
    )
    return pl.pallas_call(
        mix_kernel, out_shape=outs, in_specs=[VM] * len(operands), out_specs=(VM,) * 4 + (ANY,) * 2 + (VM,) * (len(outs) - 6),
        scratch_shapes=[
            pltpu.VMEM((6, 1024 + 2 * PAD, 128), f32), pltpu.VMEM((WIDTH, 1024), low_type),
            pltpu.VMEM((WIDTH, TILE), f32), pltpu.VMEM((512, TILE), f32), pltpu.VMEM((8, 512), f32),
            pltpu.VMEM((TILE, KERNEL * 128), f32), pltpu.VMEM((1, VEC_TOTAL), f32),
            pltpu.VMEM((18, 512, TILE), low_type), pltpu.VMEM((3, 1024 + 2 * PAD, 128), f32), pltpu.SemaphoreType.DMA((4,)),
        ],
        compiler_params=pltpu.CompilerParams(vmem_limit_bytes=60 << 20),
        name="mix_forward",
    )(*operands)


SMALL2 = (("output_bias", 2), ("norm1_gain", 2), ("norm1_shift", 2), ("ffn_in_bias", 8), ("ffn_out_bias", 2), ("norm2_gain", 2), ("norm2_shift", 2))


def fold_rows(values):
    return jnp.sum(values.reshape(values.shape[0] // 8, 8, values.shape[1]), axis=0)


def normalize(values):
    centered = values - jnp.mean(values, axis=1, keepdims=True)
    scale = lax.rsqrt(jnp.mean(centered * centered, axis=1, keepdims=True) + norm_eps)
    return centered * scale, scale


def norm_back(grad, unit, scale, gain):
    e = grad * gain
    return (e - jnp.mean(e, axis=1, keepdims=True) - unit * jnp.mean(e * unit, axis=1, keepdims=True)) * scale


def write_small(small, row, total):
    line = jnp.sum(total, axis=0, keepdims=True)
    for k in range(line.shape[1] // 384):
        small[row + k : row + k + 1, :] = line[:, k * 384 : k * 384 + 384]


def ffn_kernel(
    hidden, joined, cotangent, out_w, in_w, ffo_w,
    vec0, vec1, vec2, vec3, vec4, vec5, vec6,
    layer_out, residual_grad, joined_grad, units, small,
    active, inner, normed_low, outer_low, attn_low, slope, total, unit1, sums, sums_in, vecs,
):
    load_vecs(vecs, FFN_VECS, (vec0, vec1, vec2, vec3, vec4, vec5, vec6))
    b = lax.axis_index("branch")
    sums[...] = jnp.zeros_like(sums)
    sums_in[...] = jnp.zeros_like(sums_in)

    def block(i, carry):
        rows = aligned(i * TILE, TILE)
        x = hidden[aligned(b * 768 + i * TILE, TILE), :].astype(f32)
        n1, scale1 = normalize(x + mm(joined[rows, :], out_w[...]) + vec(vecs, "output_bias"))
        unit1[...] = n1
        normed = n1 * vec(vecs, "norm1_gain") + vec(vecs, "norm1_shift")
        normed_low[rows, :] = normed.astype(low_type)
        total[...] = normed + vec(vecs, "ffn_out_bias")

        def forward(c, carry):
            g, part = lax.div(c, 2), lax.rem(c, 2)
            lanes = pl.ds(pl.multiple_of(g * 384, 128), 384)
            wide = pl.ds(pl.multiple_of(part * 768, 128), 768)
            here = pl.ds(pl.multiple_of(c * 768, 128), 768)
            at = pl.ds(pl.multiple_of(VEC_AT["ffn_in_bias"][0] + c * 768, 128), 768)
            z = mm(normed_low[rows, lanes], in_w[g, :, wide]) + vecs[0:1, at]
            phi = 0.5 + 0.5 * lax.erf(z * (0.5**0.5))
            act = (z * phi).astype(low_type)
            active[rows, here] = act
            slope[:, here] = phi + z * jnp.exp(-0.5 * z * z) * ((2.0 * math.pi) ** -0.5)
            total[:, lanes] += mm(act, ffo_w[g, pl.ds(pl.multiple_of(part * 768, 128), 768), :])
            return carry

        lax.fori_loop(0, 4, forward, 0, unroll=True)
        n2, scale2 = normalize(total[...])
        layer_out[rows, :] = (n2 * vec(vecs, "norm2_gain") + vec(vecs, "norm2_shift")).astype(low_type)
        grad = cotangent[rows, :].astype(f32)
        sums[5] += fold_rows(grad * n2)
        sums[6] += fold_rows(grad)
        sum_grad = norm_back(grad, n2, scale2, vec(vecs, "norm2_gain"))
        outer = sum_grad.astype(low_type)
        outer_low[rows, :] = outer
        sums[4] += fold_rows(outer.astype(f32))
        total[...] = sum_grad

        def backward(c, carry):
            g, part = lax.div(c, 2), lax.rem(c, 2)
            lanes = pl.ds(pl.multiple_of(g * 384, 128), 384)
            wide = pl.ds(pl.multiple_of(part * 768, 128), 768)
            here = pl.ds(pl.multiple_of(c * 768, 128), 768)
            grad_in = mm_nt(outer_low[rows, lanes], ffo_w[g, wide, :]) * slope[:, here]
            grad_low = grad_in.astype(low_type)
            inner[rows, here] = grad_low
            sums_in[:, here] += fold_rows(grad_low.astype(f32))
            total[:, lanes] += mm_nt(grad_low, in_w[g, :, wide])
            return carry

        lax.fori_loop(0, 4, backward, 0, unroll=True)
        normed_grad = total[...]
        n1 = unit1[...]
        sums[1] += fold_rows(normed_grad * n1)
        sums[2] += fold_rows(normed_grad)
        grad1 = norm_back(normed_grad, n1, scale1, vec(vecs, "norm1_gain"))
        residual_grad[rows, :] = grad1
        attn = grad1.astype(low_type)
        attn_low[rows, :] = attn
        sums[0] += fold_rows(attn.astype(f32))
        joined_grad[rows, :] = mm_nt(attn, out_w[...]).astype(low_type)
        return carry

    lax.fori_loop(0, 3, block, 0)

    for g in range(2):
        lanes = slice(g * 384, g * 384 + 384)

        def weights(m, carry, g=g, lanes=lanes):
            wide = pl.ds(pl.multiple_of(g * 1536 + m * 384, 128), 384)
            group = pl.ds(m * 8, 8)
            grad_out = mm_tn(active[:, wide], outer_low[:, lanes])
            units[group, g * 48 : g * 48 + 48, :] = grad_out.reshape(8, 48, 384).astype(low_type)
            grad_in = mm_tn(inner[:, wide], normed_low[:, lanes])
            units[group, 96 + g * 48 : 144 + g * 48, :] = grad_in.reshape(8, 48, 384).astype(low_type)
            return carry

        lax.fori_loop(0, 4, weights, 0, unroll=2)
    for m in range(2):
        grad_w = mm_tn(joined[:, m * 384 : m * 384 + 384], attn_low[...])
        halves = [grad_w[:, :384].reshape(16, 24, 384), grad_w[:, 384:].reshape(16, 24, 384)]
        units[m * 16 : m * 16 + 16, 192:240, :] = jnp.concatenate(halves, axis=1).astype(low_type)
    small[...] = jnp.zeros_like(small)
    row = 0
    for k, (name, count) in enumerate(SMALL2):
        if name == "ffn_in_bias":
            write_small(small, row, sums_in[...])
        else:
            write_small(small, row, sums[k])
        row += count


def ffn_call(*operands):
    shape = jax.ShapeDtypeStruct
    outs = (
        shape((768, D), low_type), shape((768, D), f32), shape((768, D), low_type),
        shape((32, 240, 384), low_type), shape((32, 384), f32),
    )
    return pl.pallas_call(
        ffn_kernel, out_shape=outs, in_specs=[VM] * len(operands), out_specs=(VM,) * len(outs),
        scratch_shapes=[
            pltpu.VMEM((768, 3072), low_type), pltpu.VMEM((768, 3072), low_type),
            pltpu.VMEM((768, D), low_type), pltpu.VMEM((768, D), low_type), pltpu.VMEM((768, D), low_type),
            pltpu.VMEM((TILE, 3072), f32), pltpu.VMEM((TILE, D), f32), pltpu.VMEM((TILE, D), f32),
            pltpu.VMEM((7, 8, D), f32), pltpu.VMEM((8, 3072), f32), pltpu.VMEM((1, VEC_TOTAL), f32),
        ],
        compiler_params=pltpu.CompilerParams(vmem_limit_bytes=60 << 20),
        name="ffn",
    )(*operands)


MESH = pl.DeviceIdType.MESH
CHUNK = 48


class Reducer:
    def __init__(self, dp_size, sources, kept, kept_sem, buffer, out, send, recv):
        self.bits = int(math.log2(dp_size)) + 1
        self.extra = max(0, self.bits - 5)
        self.nh = self.bits - self.extra
        self.dp = lax.axis_index("dp")
        self.br = lax.axis_index("branch")
        self.my = [self.br] + [lax.rem(lax.div(self.dp, 1 << (k - 1)), 2) for k in range(1, self.bits)]
        self.kept, self.kept_sem = kept, kept_sem
        self.buffer, self.out, self.send, self.recv = buffer, out, send, recv
        self.sources = [(ref, row) for ref in sources for row in range(0, ref.shape[1], CHUNK)]
        halving = list(range(self.extra, self.bits))
        first = [1] if 1 in halving else []
        r = [k for k in halving if k not in first]
        turns = [(0, 2, 1), (1, 2, 0), (0, 2, 1), (1, 2, 0), (2, 0, 1), (0, 2, 1), (1, 2, 0), (2, 1, 0)]
        self.orders = [first + [r[t] for t in turn] + r[3:] for turn in turns]

    def enter(self):
        barrier = pltpu.get_barrier_semaphore()
        for k in range(self.bits):
            pl.semaphore_signal(barrier, inc=1, device_id=self.partner(k), device_id_type=MESH)
        pl.semaphore_wait(barrier, self.bits)

    def partner(self, k):
        if k == 0:
            return (self.dp, 1 - self.br)
        return (self.dp + (1 << (k - 1)) * (1 - 2 * self.my[k]), self.br)

    def copy(self, src, dst, ssem, rsem, k):
        return pltpu.make_async_remote_copy(
            src_ref=src, dst_ref=dst, send_sem=ssem, recv_sem=rsem, device_id=self.partner(k), device_id_type=MESH
        )

    def offset(self, s):
        return sum(1 << (self.nh - 1 - t) for t in range(s))

    def place(self, u, free, fixed, value):
        index, at = 0, len(free) - 1
        for k in sorted(free + [fixed], reverse=True):
            if k == fixed:
                index = index * 2 + value
            else:
                index = index * 2 + ((u >> at) & 1)
                at -= 1
        return index

    def free(self, c, s):
        return sorted(self.orders[c][s + 1 :], reverse=True)

    def whole(self, c, s):
        part = self.buffer.at[c, pl.ds(self.offset(s), 1 << (self.nh - 1 - s))]
        return self.copy(part, part, self.send.at[c, s], self.recv.at[c, s], self.orders[c][s])

    def start(self, c, s):
        k, free = self.orders[c][s], self.free(c, s)
        for u in range(1 << len(free)):
            at = self.place(u, free, k, 1 - self.my[k])
            if s == 0:
                ref, row = self.sources[c]
                src = ref.at[at, pl.ds(row, CHUNK)]
            else:
                src = self.buffer.at[c, self.offset(s - 1) + at]
            self.copy(src, self.buffer.at[c, self.offset(s) + u], self.send.at[c, s], self.recv.at[c, s], k).start()

    def fetch(self, c):
        k, free = self.orders[c][0], self.free(c, 0)
        ref, row = self.sources[c]
        for u in range(1 << len(free)):
            at = self.place(u, free, k, self.my[k])
            pltpu.make_async_copy(ref.at[at, pl.ds(row, CHUNK)], self.kept.at[c, u], self.kept_sem.at[c]).start()

    def add(self, c, s):
        fetched = c < self.kept.shape[0]
        if s == 0 and fetched:
            pltpu.make_async_copy(self.kept.at[c], self.kept.at[c], self.kept_sem.at[c]).wait()
        self.whole(c, s).wait_recv()
        k, free = self.orders[c][s], self.free(c, s)
        for u in range(1 << len(free)):
            at = self.place(u, free, k, self.my[k])
            if s == 0 and fetched:
                mine = self.kept[c, u]
            elif s == 0:
                ref, row = self.sources[c]
                mine = ref[at, row : row + CHUNK, :]
            else:
                mine = self.buffer[c, self.offset(s - 1) + at]
            theirs = self.buffer[c, self.offset(s) + u]
            if s == self.nh - 1:
                self.out[c * CHUNK : (c + 1) * CHUNK, :] = mine.astype(f32) + theirs.astype(f32)
            else:
                self.buffer[c, self.offset(s) + u] = mine + theirs

    def step(self, c, s):
        if s > 0:
            self.add(c, s - 1)
        if s < self.nh:
            self.start(c, s)

    def drain(self):
        for c in range(len(self.sources)):
            for s in range(self.nh):
                self.whole(c, s).wait_send()


class Doubler:
    def __init__(self, reducer, value, sent, got, send, recv):
        self.reducer, self.value, self.sent, self.got, self.send, self.recv = reducer, value, sent, got, send, recv
        self.order = reducer.orders[0] + list(range(reducer.extra))

    def copy(self, s):
        return self.reducer.copy(self.sent, self.got.at[s], self.send.at[s], self.recv.at[s], self.order[s])

    def step(self, s):
        if s > 0:
            copy = self.copy(s - 1)
            copy.wait()
            self.value[...] = self.sent[...].astype(f32) + self.got[s - 1].astype(f32)
        if s < len(self.order):
            self.sent[...] = self.value[...].astype(self.sent.dtype)
            self.copy(s).start()


EARLY_STEPS = {
    (0, 1): [(0, 1), (1, 1)],
    (0, 2): [(2, 1), (3, 1)],
    (0, 3): [(4, 1)],
    (1, 2): [(0, 2), (1, 2)],
    (2, 1): [(2, 2), (3, 2), (4, 2)],
    (2, 3): [(0, 3), (1, 3)],
}


def back_kernel(
    dp_size, hidden_far, joined_grad_far, residual_grad_far, q_in_far, k_in_far, v_in_far, probs_far, conv_pad_far, taps, tap_mask, query_pre_far, key_conv_far, depth_low_far,
    conv_attn_far, units2, small2, query_w_far, key_w_far, value_w_far, point_w_far, conv_w_far, depth_w, kernel_w,
    grad_own, got_other, out, small_sum,
    dk_acc, dv_acc, k_t, dq_low, kvc, key_conv_low, dg_pad, cg_pad, x_pad, mask_cols, dw_acc, dq_t, kernel_acc, bias_acc, moved_taps, part,
    sums, grad_other, units, buffer, sent3, got3, extra_got,
    send, recv, send3, recv3, other_sem, extra_sem, kept, kept_sem,
    hidden, joined_grad, residual_grad, q_in, k_in, v_in, probs, conv_pad, query_pre, key_conv, depth_low, conv_attn,
    query_w, key_w, value_w, point_w, conv_w, load_sem, probs_sem,
):
    order = (
        (hidden_far, hidden), (k_in_far, k_in), (joined_grad_far, joined_grad), (q_in_far, q_in), (v_in_far, v_in),
        (conv_pad_far, conv_pad), (conv_attn_far, conv_attn), (query_pre_far, query_pre), (key_conv_far, key_conv), (point_w_far, point_w),
        (depth_low_far, depth_low), (key_w_far, key_w), (value_w_far, value_w), (conv_w_far, conv_w), (query_w_far, query_w),
        (residual_grad_far, residual_grad),
    )
    loads = [pltpu.make_async_copy(away, near, load_sem.at[n]) for n, (away, near) in enumerate(order)]

    def probs_load(i):
        heads = pl.ds(i * HEADS, HEADS)
        return pltpu.make_async_copy(probs_far.at[heads], probs.at[heads], probs_sem.at[i])

    for load in loads[:5]:
        load.start()
    for i in range(3):
        probs_load(i).start()
    for load in loads[5:]:
        load.start()
    reducer = Reducer(dp_size, (units2, units), kept, kept_sem, buffer, out, send, recv)
    nh, bits, extra = reducer.nh, reducer.bits, reducer.extra
    late = Doubler(reducer, small_sum, sent3, got3, send3, recv3)
    other_copy = reducer.copy(grad_other, got_other, other_sem.at[0], other_sem.at[1], 0)
    for c in range(5):
        reducer.fetch(c)
    reducer.enter()
    for c in range(5):
        reducer.step(c, 0)
    def run(steps):
        for c, stage in steps:
            reducer.step(c, stage)

    def advance_at(i, spot):
        for (n, at), steps in EARLY_STEPS.items():
            if at == spot:
                @pl.when(i == n)
                def _(steps=steps):
                    run(steps)

    b = lax.axis_index("branch")
    base = b * 512
    for ref in (dk_acc, dv_acc, dg_pad, cg_pad, dw_acc, kernel_acc, bias_acc, sums):
        ref[...] = jnp.zeros_like(ref)
    for c in range(D // 128):
        x_pad[c, 0:PAD, :] = jnp.zeros((PAD, 128), f32)
        x_pad[c, 1024 + PAD : 1024 + 2 * PAD, :] = jnp.zeros((PAD, 128), f32)

    def prepare(e, carry):
        rows = aligned(e * TILE, TILE)
        k_t[:, rows] = jnp.transpose(k_in[rows, :].astype(f32)).astype(low_type)
        x = hidden[aligned(base + e * TILE, TILE), :]
        place = pl.ds(pl.multiple_of(e * TILE + PAD, 8), TILE)
        for c in range(D // 128):
            x_pad[c, place, :] = x[:, c * 128 : c * 128 + 128].astype(f32)
        return carry

    for load in loads[:2]:
        load.wait()
    lax.fori_loop(0, 4, prepare, 0)
    kernel_rows = mm(tap_permutation().astype(low_type), kernel_w[...]).astype(low_type)
    depth_weights = [depth_w[j : j + 1, :].astype(f32) for j in range(KERNEL)]
    head_rows = head_spread(0)[:8]
    moved = []
    for j in range(KERNEL):
        rows = taps[(8 - j) * 8 : (8 - j) * 8 + 8, :]
        rows = rows if j == 4 else pltpu.roll(rows, (4 - j) % 1024, 1)
        moved.append(rows * tap_mask[j * 8 : j * 8 + 8, :])
    moved_taps[...] = jnp.transpose(jnp.concatenate(moved, axis=0)).astype(low_type)

    def own(i, carry):
        e = b + i
        rows = aligned(i * TILE, TILE)
        ext = aligned(e * TILE, TILE)
        place = pl.ds(pl.multiple_of(e * TILE + PAD, 8), TILE)
        keys = aligned(lax.div(e, 2) * 512, 512)
        probs_load(i).wait()
        d_ctx = joined_grad[rows, 0:WIDTH]
        d_ctx_t = jnp.transpose(d_ctx.astype(f32)).astype(low_type)
        for p in range(HEADS // 2):
            lanes = slice(p * 128, p * 128 + 128)
            v_pair = v_in[keys, lanes]
            q_pair = q_in[rows, lanes]
            d_pair = d_ctx[:, lanes]
            scores, weights = [], []
            for odd in range(2):
                h = 2 * p + odd
                weight = probs[i * HEADS + h]
                prob_grad = mm(v_pair, half_rows(d_ctx_t[lanes], odd))
                wide = weight.astype(f32)
                term = wide * prob_grad
                score = (term - wide * jnp.sum(term, axis=0, keepdims=True)).astype(low_type)
                dq_t[h * HEAD_DIM : (h + 1) * HEAD_DIM, :] = mm(k_t[h * HEAD_DIM : (h + 1) * HEAD_DIM, keys], score)
                scores.append(score)
                weights.append(weight)
            q_both = jnp.concatenate([half_lanes(q_pair, 0), half_lanes(q_pair, 1)], axis=0)
            d_both = jnp.concatenate([half_lanes(d_pair, 0), half_lanes(d_pair, 1)], axis=0)
            dk_acc[keys, lanes] += mm(jnp.concatenate(scores, axis=1), q_both)
            dv_acc[keys, lanes] += mm(jnp.concatenate(weights, axis=1), d_both)
            advance_at(i, p)
        query_low = (jnp.transpose(dq_t[...]) * 0.125).astype(low_type)

        grad = joined_grad[rows, WIDTH : 2 * WIDTH].astype(f32)
        for c in range(WIDTH // 128):
            cg_pad[c, place, :] = grad[:, c * 128 : c * 128 + 128]
        grads = []
        for j in range(KERNEL):
            pieces = [
                (grad[:, c * 128 : c * 128 + 128] * shifted(conv_pad, c, e * TILE, j, TILE)).astype(low_type)
                for c in range(WIDTH // 128)
            ]
            grads.append(mm_nt(head_rows, jnp.concatenate(pieces, axis=1)) * tap_mask[j * 8 : j * 8 + 8, ext])
        kept = taps[:, ext]
        level = functools.reduce(jnp.add, [grads[j] * kept[j * 8 : j * 8 + 8] for j in range(KERNEL)])
        logit = kept * jnp.concatenate([x - level for x in grads], axis=0)
        logit_low = logit.astype(low_type)
        logit_wide = logit_low.astype(f32)
        kernel_acc[...] += mm(logit_low, conv_attn[rows, :])
        bias_acc[...] += logit_wide[:, :128] + logit_wide[:, 128:]
        span = mm(jnp.transpose(logit_wide).astype(low_type), kernel_rows).astype(low_type).astype(f32)
        point_low = (span * query_pre[rows, :].astype(f32)).astype(low_type)
        query_conv = (span * key_conv[rows, :].astype(f32)).astype(low_type)
        key_conv_low[rows, :] = point_low
        sums[2] += fold_rows(point_low.astype(f32))
        both = query_low.astype(f32) + query_conv.astype(f32)
        sums[0] += fold_rows(both)
        dq_low[rows, :] = both.astype(low_type)
        d_depth = mm_nt(point_low, point_w[...])
        for c in range(D // 128):
            dg_pad[c, place, :] = d_depth[:, c * 128 : c * 128 + 128]
        mask_cols[...] = mm(jnp.transpose(tap_mask[:, ext]).astype(low_type), tap_spread())
        for c in range(D // 128):
            totals = [None] * KERNEL
            for lo in range(0, TILE, 64):
                grad_rows = dg_pad[c, pl.ds(e * TILE + (PAD + lo), 64), :]
                for j in range(KERNEL):
                    term = shifted(x_pad, c, e * TILE + lo, j, 64) * grad_rows
                    if j != KERNEL // 2:
                        term = term * mask_cols[lo : lo + 64, j * 128 : j * 128 + 128]
                    term = fold_rows(term)
                    totals[j] = term if lo == 0 else totals[j] + term
            for j in range(KERNEL):
                dw_acc[j, :, c * 128 : c * 128 + 128] += totals[j]
        advance_at(i, 3)
        return carry

    for load in loads[2:10]:
        load.wait()
    lax.fori_loop(0, 3, own, 0)
    for load in loads[10:]:
        load.wait()

    def settle(e, carry):
        ext = aligned(e * TILE, TILE)
        dv = dv_acc[ext, :].astype(low_type)
        kvc[ext, 0:WIDTH] = dk_acc[ext, :].astype(low_type)
        kvc[ext, WIDTH : 2 * WIDTH] = dv
        sums[1] += fold_rows(dv.astype(f32))
        return carry

    def pack(k, first, second):
        for m in range(2):
            lanes = slice(m * 384, m * 384 + 384)
            pieces = [part_of(lanes).reshape(16, 24, 384) for part_of in (first, second)]
            units[m * 16 : m * 16 + 16, k * 48 : k * 48 + 48, :] = jnp.concatenate(pieces, axis=1).astype(low_type)

    def token_grad(k):
        return lambda lanes: mm_tn(hidden[aligned(base, 512), lanes], kvc[0:512, k * WIDTH : (k + 1) * WIDTH]) + mm_tn(
            hidden[aligned(base + 512, 512), lanes], kvc[512:1024, k * WIDTH : (k + 1) * WIDTH]
        )

    lax.fori_loop(0, 4, settle, 0)
    own_tokens = pl.ds(pl.multiple_of(b * 768, 256), 768)
    pack(0, lambda lanes: mm_tn(hidden[own_tokens, lanes], dq_low[...]), token_grad(0))
    run([(5, 0), (4, 3)])
    depth_total = jnp.sum(dw_acc[...], axis=1)
    depth_t = jnp.transpose(jnp.concatenate([depth_total, jnp.zeros((128 - KERNEL, D), f32)], axis=0))
    pack(
        2,
        lambda lanes: mm_tn(depth_low[:, lanes], key_conv_low[...]),
        lambda lanes: jnp.concatenate([depth_t[lanes], jnp.zeros((384, 256), f32)], axis=1),
    )
    run([(7, 0), (2, 3), (3, 3), (0, 4), (1, 4)])

    def spans(e, carry):
        ext = aligned(e * TILE, TILE)
        dc = span_conv(cg_pad, moved_taps[ext, :], e * TILE).astype(low_type)
        kvc[ext, 2 * WIDTH : 3 * WIDTH] = dc
        sums[3] += fold_rows(dc.astype(f32))
        return carry

    lax.fori_loop(0, 4, spans, 0, unroll=2)
    run([(4, 4), (2, 4), (3, 4)])
    small_sum[...] = jnp.zeros_like(small_sum)
    small_sum[0:72, :] = kernel_acc[...]
    for k in range(4):
        small_sum[72 + k : 73 + k, :] = jnp.sum(sums[k], axis=0, keepdims=True)
    column = jnp.concatenate([bias_acc[...], jnp.zeros((56, 128), f32)], axis=0)
    small_sum[76:77, 0:128] = jnp.sum(jnp.transpose(column), axis=0, keepdims=True)
    small_sum[80:104, :] = small2[0:24, :]
    late.step(0)
    run([(5, 1), (7, 1)])
    pack(1, token_grad(1), token_grad(2))
    run([(6, 0)])
    late.step(1)
    def input_part(e):
        ext = aligned(e * TILE, TILE)
        mask_cols[...] = mm(jnp.transpose(tap_mask[:, ext]).astype(low_type), tap_spread())

        def keep(c, lo, value):
            part[lo : lo + 64, c * 128 : c * 128 + 128] = value

        depth_conv(dg_pad, mask_cols, depth_weights, e * TILE, keep, True)
        pieces = [kvc[ext, k * WIDTH : (k + 1) * WIDTH] for k in range(3)]
        return part[...] + mm_nt(pieces[0], key_w[...]) + mm_nt(pieces[1], value_w[...]) + mm_nt(pieces[2], conv_w[...])

    grad_other[...] = input_part(3 * (1 - b)).astype(low_type)
    run([(6, 1), (0, 5), (1, 5), (4, 5), (2, 5), (3, 5)])
    other_copy.start()

    def finish(i, carry):
        rows = aligned(i * TILE, TILE)
        grad_own[rows, :] = input_part(b + i) + mm_nt(dq_low[rows, :], query_w[...]) + residual_grad[rows, :]
        return carry

    lax.fori_loop(0, 3, finish, 0)
    for stage in range(2, 6):
        late.step(stage)
        run([(c, stage) for c in (5, 7, 6)])
    for s in range(6, nh + 1):
        for c in range(8):
            reducer.step(c, s)
    for s in range(6, bits + 1):
        late.step(s)
    for k in range(extra):
        copy = reducer.copy(out, extra_got.at[k], extra_sem.at[2 * k], extra_sem.at[2 * k + 1], k)
        copy.start()
        copy.wait()
        out[...] = out[...] + extra_got[k]
    reducer.drain()
    other_copy.wait()


def back_call(dp_size, hidden, joined_grad, residual_grad, saved, units2, small2, weights):
    shape = jax.ShapeDtypeStruct
    outs = (shape((768, D), f32), shape((256, D), low_type), shape((384, 384), f32), shape((104, 384), f32))
    operands = (hidden, joined_grad, residual_grad) + tuple(saved) + (units2, small2) + tuple(weights)
    ext = 1024 + 2 * PAD
    bits = int(math.log2(dp_size)) + 1
    extra = max(0, bits - 5)
    nh = bits - extra
    dma = pltpu.SemaphoreType.DMA
    return pl.pallas_call(
        functools.partial(back_kernel, dp_size), out_shape=outs, in_specs=[ANY] * 8 + [VM] * 2 + [ANY] * 5 + [VM] + [ANY] * 5 + [VM] * 2, out_specs=(VM,) * len(outs),
        scratch_shapes=[
            pltpu.VMEM((1024, WIDTH), f32), pltpu.VMEM((1024, WIDTH), f32), pltpu.VMEM((WIDTH, 1024), low_type),
            pltpu.VMEM((768, WIDTH), low_type), pltpu.VMEM((1024, 3 * WIDTH), low_type), pltpu.VMEM((768, WIDTH), low_type),
            pltpu.VMEM((6, ext, 128), f32), pltpu.VMEM((3, ext, 128), f32), pltpu.VMEM((6, ext, 128), f32),
            pltpu.VMEM((TILE, KERNEL * 128), f32), pltpu.VMEM((KERNEL, 8, D), f32), pltpu.VMEM((WIDTH, TILE), f32),
            pltpu.VMEM((72, WIDTH), f32), pltpu.VMEM((72, 128), f32), pltpu.VMEM((1024, 72), low_type), pltpu.VMEM((TILE, D), f32),
            pltpu.VMEM((4, 8, WIDTH), f32),
            pltpu.VMEM((256, D), low_type), pltpu.VMEM((32, 144, 384), low_type),
            pltpu.VMEM((8, (1 << nh) - 1, CHUNK, 384), low_type),
            pltpu.VMEM((104, 384), low_type), pltpu.VMEM((bits, 104, 384), low_type),
            pltpu.VMEM((max(extra, 1), 384 if extra else 8, 384), f32),
            dma((8, nh)), dma((8, nh)), dma((bits,)), dma((bits,)), dma((2,)), dma((max(2 * extra, 2),)),
            pltpu.VMEM((5, 1 << (nh - 1), CHUNK, 384), low_type), dma((5,)),
        ] + [pltpu.VMEM(operands[n].shape, operands[n].dtype) for n in (0, 1, 2, 3, 4, 5, 6, 7, 10, 11, 12, 13, 16, 17, 18, 19, 20)] + [
            dma((16,)), dma((3,)),
        ],
        compiler_params=pltpu.CompilerParams(collective_id=0, has_side_effects=True, vmem_limit_bytes=67_000_000),
        name="mix_backward_reduce",
    )(*operands)


def exact_columns(table, rows):
    return lax.dot_general(table, rows, (((0,), (0,)), ((), ())), precision=lax.Precision.HIGHEST, preferred_element_type=f32)


FINAL_SMALL = (
    ("query_b", 72, 384), ("value_b", 73, 384), ("point_b", 74, 384), ("conv_b", 75, 384), ("out_b", 80, 768), ("gain1", 82, 768),
    ("shift1", 84, 768), ("in_b", 86, 3072), ("ffo_b", 94, 768), ("gain2", 96, 768), ("shift2", 98, 768),
)


def final_kernel(
    grad_own, got, total, small,
    input_grad, query_w, key_w, value_w, depth_w, point_w, kernel_w, kernel_b, conv_w, out_w, in_w, ffo_w, *vectors,
):
    b = lax.axis_index("branch")
    input_grad[...] = grad_own[...]
    rows = aligned((1 - b) * 512, 256)
    input_grad[rows, :] = grad_own[rows, :] + got[...].astype(f32)
    for ref, row in ((query_w, 240), (key_w, 264), (value_w, 288), (conv_w, 312), (point_w, 336)):
        ref[...] = total[row : row + 24, :]
    ffo_w[0] = total[0:48, :]
    ffo_w[1] = total[48:96, :]
    out_w[:, 0:384] = total[192:216, :]
    out_w[:, 384:768] = total[216:240, :]
    in_w[0] = total[96:144, :]
    in_w[1] = total[144:192, :]
    depth = jnp.concatenate([total[360:384, 0:128], jnp.zeros((104, 128), f32)], axis=0)
    depth_w[...] = jnp.transpose(depth)[0:KERNEL, 0:24]
    table = tap_permutation()
    kernel_w[...] = exact_columns(table, small[0:72, :])
    column = jnp.transpose(jnp.concatenate([small[76:77, 0:128]] * 128, axis=0))[0:72, :]
    kernel_b[...] = jnp.sum(column[:, 0:54] * table, axis=0, keepdims=True).reshape(54)
    for ref, (_, row, size) in zip(vectors, FINAL_SMALL):
        ref[...] = jnp.concatenate([small[row + k : row + k + 1, :] for k in range(size // 384)], axis=1).reshape(size)


def final_call(*operands):
    shape = lambda *s: jax.ShapeDtypeStruct(s, f32)
    outs = (
        shape(768, D), shape(24, 384), shape(24, 384), shape(24, 384), shape(KERNEL, 24), shape(24, 384), shape(54, 384), shape(54),
        shape(24, 384), shape(24, 768), shape(2, 48, 384), shape(2, 48, 384),
    ) + tuple(shape(size) for _, _, size in FINAL_SMALL)
    return pl.pallas_call(
        final_kernel, out_shape=outs, in_specs=[VM] * 4, out_specs=(VM,) * len(outs),
        compiler_params=pltpu.CompilerParams(vmem_limit_bytes=32 << 20), name="finish",
    )(*operands)


def local(
    hidden, segment_ids, query_weight, query_bias, key_weight, value_weight, value_bias, depthwise_weight,
    pointwise_weight, pointwise_bias, kernel_weight, kernel_bias, conv_value_weight, conv_value_bias, output_weight,
    output_bias, norm1_gain, norm1_shift, ffn_in_weight, ffn_in_bias, ffn_out_weight, ffn_out_bias, norm2_gain,
    norm2_shift, cotangent,
):
    dp_size = lax.axis_size("dp")
    branch = lax.axis_index("branch")
    kernel_rows = jnp.transpose(kernel_weight)
    joined, *saved = mix_call(
        hidden, segment_ids, query_weight, key_weight, value_weight, pointwise_weight, conv_value_weight,
        depthwise_weight, kernel_rows, query_bias, value_bias, pointwise_bias, conv_value_bias, kernel_bias,
    )
    layer_out, residual_grad, joined_grad, units2, small2 = ffn_call(
        hidden, joined, cotangent, output_weight, ffn_in_weight, ffn_out_weight, output_bias, norm1_gain, norm1_shift,
        ffn_in_bias, ffn_out_bias, norm2_gain, norm2_shift,
    )
    grad_own, got, out_sum, small_sum = back_call(
        dp_size, hidden, joined_grad, residual_grad, saved, units2, small2,
        (query_weight, key_weight, value_weight, pointwise_weight, conv_value_weight, depthwise_weight, kernel_rows),
    )
    share = 2 * dp_size // 32
    if share == 1:
        (
            input_grad, query_w, key_w, value_w, depth_w, point_w, kernel_w, kernel_b, conv_w, out_w, in_w, ffo_w,
            query_b, value_b, point_b, conv_b, out_b, gain1, shift1, in_b, ffo_b, gain2, shift2,
        ) = final_call(grad_own, got, out_sum, small_sum)
        return (
            layer_out, input_grad, query_w, query_b, key_w, value_w, value_b, depth_w, point_w, point_b, jnp.transpose(kernel_w),
            kernel_b, conv_w, conv_b, out_w, out_b, gain1, shift1, jnp.transpose(in_w, (0, 2, 1)), in_b, ffo_w, ffo_b, gain2, shift2,
        )
    start = (1 - branch) * 512
    block = lax.dynamic_slice_in_dim(grad_own, start, 256, 0) + got.astype(f32)
    input_grad = lax.dynamic_update_slice_in_dim(grad_own, block, start, 0)
    device = lax.axis_index("dp") * 2 + branch

    def piece(start, rows):
        n = rows // share
        return lax.dynamic_slice_in_dim(out_sum, start + lax.rem(device, share) * n, n, 0)

    def small(row, size):
        return small_sum[row : row + -(-size // 384)].reshape(-1)[:size]

    kern_w = jnp.transpose(small_sum[:72].reshape(9, 8, 384)[:, :6], (2, 1, 0)).reshape(384, 54)
    kern_b = jnp.transpose(small_sum[76, :72].reshape(9, 8)[:, :6]).reshape(54)
    in_g = jnp.stack([piece(96, 48), piece(144, 48)])
    return (
        layer_out,
        input_grad,
        piece(240, 24),
        small(72, 384),
        piece(264, 24),
        piece(288, 24),
        small(73, 384),
        jnp.transpose(piece(360, 24)[:, :KERNEL]),
        piece(336, 24),
        small(74, 384),
        kern_w,
        kern_b,
        piece(312, 24),
        small(75, 384),
        jnp.concatenate([piece(192, 24), piece(216, 24)], axis=1),
        small(80, 768),
        small(82, 768),
        small(84, 768),
        jnp.transpose(in_g, (0, 2, 1)),
        small(86, 3072),
        jnp.stack([piece(0, 48), piece(48, 48)]),
        small(94, 768),
        small(96, 768),
        small(98, 768),
    )


def solution(mesh):
    tokens, copied = P(("dp", "branch"), None), P()
    in_specs = (P("dp", None), P("dp", None)) + (copied,) * 22 + (tokens,)
    out_specs = (
        tokens, tokens, tokens, copied, tokens, tokens, copied, P(None, ("dp", "branch")), tokens, copied, copied, copied,
        tokens, copied, tokens, copied, copied, copied, P(None, None, ("dp", "branch")), copied,
        P(None, ("dp", "branch"), None), copied, copied, copied,
    )
    return jax.shard_map(local, mesh=mesh, in_specs=in_specs, out_specs=out_specs, check_vma=False)
```

```python
import functools
import math

import jax
import jax.numpy as jnp
from jax import lax
from jax.experimental import pallas as pl
from jax.experimental.pallas import tpu as pltpu
from jax.sharding import PartitionSpec as P

HEADS = 6
HEAD_DIM = 64
KERNEL = 9
WIDTH = HEADS * HEAD_DIM
D = 768
TILE = 256
PAD = 8
NEG = -1e30
norm_eps = 1e-12
low_type = jnp.bfloat16
f32 = jnp.float32

VEC_SIZES = (
    ("query_bias", 384), ("value_bias", 384), ("pointwise_bias", 384), ("conv_value_bias", 384),
    ("output_bias", 768), ("norm1_gain", 768), ("norm1_shift", 768), ("ffn_in_bias", 3072),
    ("ffn_out_bias", 768), ("norm2_gain", 768), ("norm2_shift", 768), ("kernel_bias", 128),
)
VEC_AT = {}
_at = 0
for _name, _size in VEC_SIZES:
    VEC_AT[_name] = (_at, _size)
    _at += _size
VEC_TOTAL = _at


def vec(vecs_ref, name):
    at, size = VEC_AT[name]
    return vecs_ref[0:1, at : at + size]


def load_vecs(vecs, names, refs):
    for name, ref in zip(names, refs):
        at, size = VEC_AT[name]
        if name == "kernel_bias":
            size = ref.shape[0]
        vecs[0:1, at : at + size] = ref[...].astype(f32).reshape(1, size)


MIX_VECS = ("query_bias", "value_bias", "pointwise_bias", "conv_value_bias", "kernel_bias")
FFN_VECS = ("output_bias", "norm1_gain", "norm1_shift", "ffn_in_bias", "ffn_out_bias", "norm2_gain", "norm2_shift")


def mm(a, b):
    return jnp.dot(a, b, preferred_element_type=f32)


def mm_nt(a, b):
    return lax.dot_general(a, b, (((1,), (1,)), ((), ())), preferred_element_type=f32)


def mm_tn(a, b):
    return lax.dot_general(a, b, (((0,), (0,)), ((), ())), preferred_element_type=f32)


def tap_permutation():
    row = lax.broadcasted_iota(jnp.int32, (72, 54), 0)
    col = lax.broadcasted_iota(jnp.int32, (72, 54), 1)
    head = lax.rem(row, 8)
    return jnp.where((head * 9 + lax.div(row, 8) == col) & (head < HEADS), 1.0, 0.0)


def head_spread(j):
    row = lax.broadcasted_iota(jnp.int32, (72, WIDTH), 0)
    col = lax.broadcasted_iota(jnp.int32, (72, WIDTH), 1)
    return jnp.where(row == j * 8 + lax.div(col, HEAD_DIM), 1.0, 0.0).astype(low_type)


def tap_spread():
    row = lax.broadcasted_iota(jnp.int32, (72, KERNEL * 128), 0)
    col = lax.broadcasted_iota(jnp.int32, (72, KERNEL * 128), 1)
    return jnp.where(row == lax.div(col, 128) * 8, 1.0, 0.0).astype(low_type)


def aligned(start, size):
    return pl.ds(pl.multiple_of(start, size), size)


def half_rows(block, odd):
    zero = jnp.zeros((HEAD_DIM, block.shape[1]), block.dtype)
    kept = block[HEAD_DIM:] if odd else block[:HEAD_DIM]
    return jnp.concatenate([zero, kept] if odd else [kept, zero], axis=0)


def half_lanes(block, odd):
    lane = lax.broadcasted_iota(jnp.int32, block.shape, 1)
    keep = (lane >= HEAD_DIM) if odd else (lane < HEAD_DIM)
    return jnp.where(keep, block, jnp.zeros_like(block))


def shifted(pad_ref, c, start, j, size):
    return pad_ref[c, pl.ds(start + (PAD - 4 + j), size), :]


def depth_conv(pad_ref, mask_ref, weight, start, out, flip):
    for lo in range(0, TILE, 64):
        for c in range(D // 128):
            total = None
            for j in range(KERNEL):
                w = weight[KERNEL - 1 - j if flip else j][:, c * 128 : c * 128 + 128]
                term = shifted(pad_ref, c, start + lo, j, 64) * w
                if j != KERNEL // 2:
                    term = term * mask_ref[lo : lo + 64, j * 128 : j * 128 + 128]
                total = term if total is None else total + term
            out(c, lo, total)


def span_conv(pad_ref, taps, start):
    totals = [None] * (WIDTH // 128)
    for j in range(KERNEL):
        spread = mm(taps, head_spread(j))
        for c in range(WIDTH // 128):
            term = spread[:, c * 128 : c * 128 + 128] * shifted(pad_ref, c, start, j, TILE)
            totals[c] = term if totals[c] is None else totals[c] + term
    return jnp.concatenate(totals, axis=1)


def taps_softmax(logits):
    parts = [logits[j * 8 : j * 8 + 8] for j in range(KERNEL)]
    peak = functools.reduce(jnp.maximum, parts)
    parts = [jnp.exp(x - peak) for x in parts]
    scale = 1.0 / functools.reduce(jnp.add, parts)
    return jnp.concatenate([x * scale for x in parts], axis=0)


def mix_kernel(
    hidden, segments, query_w, key_w, value_w, point_w, conv_w, depth_w, kernel_w,
    vec0, vec1, vec2, vec3, vec4, joined, q_out, k_out, v_out, probs, conv_pad, taps_out, tap_mask, query_pre, key_conv, depth_low, conv_attn,
    x_pad, v_t, ctx_t, bias, seg_rows, mask_cols, vecs, probs_held, pad_held, out_sem,
):
    load_vecs(vecs, MIX_VECS, (vec0, vec1, vec2, vec3, vec4))
    b = lax.axis_index("branch")
    base = b * 512
    segs = segments[...].astype(f32)
    row0 = jnp.where(b == 0, segs[0:1], segs[1:2])
    row1 = jnp.where(b == 0, segs[1:2], segs[2:3])
    seg_rows[0:1, :] = row0
    seg_rows[1:2, :] = row1
    seg_t = jnp.transpose(jnp.concatenate([row0, row1] * 4, axis=0))
    both = jnp.concatenate([row0, row1 + 1024.0], axis=1)
    both = jnp.broadcast_to(both, (8, 1024))
    for j in range(KERNEL):
        moved = both if j == 4 else pltpu.roll(both, (4 - j) % 1024, 1)
        tap_mask[j * 8 : j * 8 + 8, :] = jnp.where(moved == both, 1.0, 0.0)
    for c in range(D // 128):
        x_pad[c, 0:PAD, :] = jnp.zeros((PAD, 128), f32)
        x_pad[c, 1024 + PAD : 1024 + 2 * PAD, :] = jnp.zeros((PAD, 128), f32)
    for c in range(WIDTH // 128):
        pad_held[c, 0:PAD, :] = jnp.zeros((PAD, 128), f32)
        pad_held[c, 1024 + PAD : 1024 + 2 * PAD, :] = jnp.zeros((PAD, 128), f32)
    taps_out[...] = jnp.zeros_like(taps_out)

    def project(e, carry):
        x = hidden[aligned(base + e * TILE, TILE), :]
        rows = aligned(e * TILE, TILE)
        k_out[rows, :] = mm(x, key_w[...]).astype(low_type)
        v = mm(x, value_w[...]) + vec(vecs, "value_bias")
        v_out[rows, :] = v.astype(low_type)
        v_t[:, rows] = jnp.transpose(v).astype(low_type)
        cv = mm(x, conv_w[...]) + vec(vecs, "conv_value_bias")
        place = pl.ds(pl.multiple_of(e * TILE + PAD, 8), TILE)
        for c in range(WIDTH // 128):
            pad_held[c, place, :] = cv[:, c * 128 : c * 128 + 128]
        for c in range(D // 128):
            x_pad[c, place, :] = x[:, c * 128 : c * 128 + 128].astype(f32)
        return carry

    lax.fori_loop(0, 4, project, 0, unroll=2)
    kernel_rows = mm(tap_permutation().astype(low_type), kernel_w[...]).astype(low_type)
    kernel_bias = jnp.sum(tap_permutation() * vec(vecs, "kernel_bias")[:, :54], axis=1, keepdims=True)
    depth_weights = [depth_w[j : j + 1, :].astype(f32) for j in range(KERNEL)]

    def probs_copy(i):
        heads = pl.ds(i * HEADS, HEADS)
        return pltpu.make_async_copy(probs_held.at[heads], probs.at[heads], out_sem.at[i])

    pad_copy = pltpu.make_async_copy(pad_held, conv_pad, out_sem.at[3])
    pad_copy.start()

    def own(i, carry):
        e = b + i
        rows = aligned(i * TILE, TILE)
        ext = aligned(e * TILE, TILE)
        x = hidden[aligned(base + e * TILE, TILE), :]
        q_pre = mm(x, query_w[...]) + vec(vecs, "query_bias")
        query_pre[rows, :] = q_pre.astype(low_type)
        q = q_pre.astype(low_type).astype(f32) * 0.125
        q_out[rows, :] = q.astype(low_type)
        q_t = jnp.transpose(q).astype(low_type)
        row = lax.div(e, 2)
        keys = aligned(row * 512, 512)
        seg_q = jnp.where(row == 0, seg_rows[0:1, :], seg_rows[1:2, :])
        seg_q = jnp.where(lax.rem(e, 2) == 0, seg_q[:, :TILE], seg_q[:, TILE:])
        seg_k = jnp.where(row == 0, seg_t[:, 0:1], seg_t[:, 1:2])
        bias[...] = jnp.where(seg_k == seg_q, 0.0, NEG)
        for h in range(HEADS):
            p = h // 2
            k_pair = k_out[keys, p * 128 : p * 128 + 128]
            scores = mm(k_pair, half_rows(q_t[p * 128 : p * 128 + 128], h % 2)) + bias[...]
            peak = jnp.max(scores, axis=0, keepdims=True)
            weight = jnp.exp(scores - peak)
            weight = (weight * (1.0 / jnp.sum(weight, axis=0, keepdims=True))).astype(low_type)
            probs_held[i * HEADS + h] = weight
            ctx_t[h * HEAD_DIM : (h + 1) * HEAD_DIM, :] = mm(v_t[h * HEAD_DIM : (h + 1) * HEAD_DIM, keys], weight)
        probs_copy(i).start()
        joined[rows, 0:WIDTH] = jnp.transpose(ctx_t[...]).astype(low_type)

        masks = tap_mask[:, ext]
        mask_cols[...] = mm(jnp.transpose(masks).astype(low_type), tap_spread())

        def keep(c, lo, value):
            at = pl.ds(pl.multiple_of(i * TILE + lo, 64), 64)
            depth_low[at, c * 128 : c * 128 + 128] = value.astype(low_type)

        depth_conv(x_pad, mask_cols, depth_weights, e * TILE, keep, False)
        kc = mm(depth_low[rows, :], point_w[...]) + vec(vecs, "pointwise_bias")
        key_conv[rows, :] = kc.astype(low_type)
        attn = (kc * q_pre).astype(low_type)
        conv_attn[rows, :] = attn
        taps = taps_softmax(mm_nt(kernel_rows, attn) + kernel_bias)
        taps_out[:, ext] = taps
        spread = span_conv(pad_held, jnp.transpose(taps * masks).astype(low_type), e * TILE)
        joined[rows, WIDTH : 2 * WIDTH] = spread.astype(low_type)
        return carry

    lax.fori_loop(0, 3, own, 0)
    for i in range(3):
        probs_copy(i).wait()
    pad_copy.wait()


VM = pl.BlockSpec(memory_space=pltpu.VMEM)
ANY = pl.BlockSpec(memory_space=pl.ANY)


def mix_call(*operands):
    shape = jax.ShapeDtypeStruct
    outs = (
        shape((768, 768), low_type), shape((768, WIDTH), low_type), shape((1024, WIDTH), low_type),
        shape((1024, WIDTH), low_type), shape((18, 512, TILE), low_type), shape((3, 1024 + 2 * PAD, 128), f32),
        shape((72, 1024), f32), shape((72, 1024), f32), shape((768, WIDTH), low_type), shape((768, WIDTH), low_type),
        shape((768, D), low_type), shape((768, WIDTH), low_type),
    )
    return pl.pallas_call(
        mix_kernel, out_shape=outs, in_specs=[VM] * len(operands), out_specs=(VM,) * 4 + (ANY,) * 2 + (VM,) * (len(outs) - 6),
        scratch_shapes=[
            pltpu.VMEM((6, 1024 + 2 * PAD, 128), f32), pltpu.VMEM((WIDTH, 1024), low_type),
            pltpu.VMEM((WIDTH, TILE), f32), pltpu.VMEM((512, TILE), f32), pltpu.VMEM((8, 512), f32),
            pltpu.VMEM((TILE, KERNEL * 128), f32), pltpu.VMEM((1, VEC_TOTAL), f32),
            pltpu.VMEM((18, 512, TILE), low_type), pltpu.VMEM((3, 1024 + 2 * PAD, 128), f32), pltpu.SemaphoreType.DMA((4,)),
        ],
        compiler_params=pltpu.CompilerParams(vmem_limit_bytes=60 << 20),
        name="mix_forward",
    )(*operands)


SMALL2 = (("output_bias", 2), ("norm1_gain", 2), ("norm1_shift", 2), ("ffn_in_bias", 8), ("ffn_out_bias", 2), ("norm2_gain", 2), ("norm2_shift", 2))


def fold_rows(values):
    return jnp.sum(values.reshape(values.shape[0] // 8, 8, values.shape[1]), axis=0)


def normalize(values):
    centered = values - jnp.mean(values, axis=1, keepdims=True)
    scale = lax.rsqrt(jnp.mean(centered * centered, axis=1, keepdims=True) + norm_eps)
    return centered * scale, scale


def norm_back(grad, unit, scale, gain):
    e = grad * gain
    return (e - jnp.mean(e, axis=1, keepdims=True) - unit * jnp.mean(e * unit, axis=1, keepdims=True)) * scale


def write_small(small, row, total):
    line = jnp.sum(total, axis=0, keepdims=True)
    for k in range(line.shape[1] // 384):
        small[row + k : row + k + 1, :] = line[:, k * 384 : k * 384 + 384]


def ffn_kernel(
    hidden, joined, cotangent, out_w, in_w, ffo_w,
    vec0, vec1, vec2, vec3, vec4, vec5, vec6,
    layer_out, residual_grad, joined_grad, units, small,
    active, inner, normed_low, outer_low, attn_low, slope, total, unit1, sums, sums_in, vecs,
):
    load_vecs(vecs, FFN_VECS, (vec0, vec1, vec2, vec3, vec4, vec5, vec6))
    b = lax.axis_index("branch")
    sums[...] = jnp.zeros_like(sums)
    sums_in[...] = jnp.zeros_like(sums_in)

    def block(i, carry):
        rows = aligned(i * TILE, TILE)
        x = hidden[aligned(b * 768 + i * TILE, TILE), :].astype(f32)
        n1, scale1 = normalize(x + mm(joined[rows, :], out_w[...]) + vec(vecs, "output_bias"))
        unit1[...] = n1
        normed = n1 * vec(vecs, "norm1_gain") + vec(vecs, "norm1_shift")
        normed_low[rows, :] = normed.astype(low_type)
        total[...] = normed + vec(vecs, "ffn_out_bias")

        def forward(c, carry):
            g, part = lax.div(c, 2), lax.rem(c, 2)
            lanes = pl.ds(pl.multiple_of(g * 384, 128), 384)
            wide = pl.ds(pl.multiple_of(part * 768, 128), 768)
            here = pl.ds(pl.multiple_of(c * 768, 128), 768)
            at = pl.ds(pl.multiple_of(VEC_AT["ffn_in_bias"][0] + c * 768, 128), 768)
            z = mm(normed_low[rows, lanes], in_w[g, :, wide]) + vecs[0:1, at]
            phi = 0.5 + 0.5 * lax.erf(z * (0.5**0.5))
            act = (z * phi).astype(low_type)
            active[rows, here] = act
            slope[:, here] = phi + z * jnp.exp(-0.5 * z * z) * ((2.0 * math.pi) ** -0.5)
            total[:, lanes] += mm(act, ffo_w[g, pl.ds(pl.multiple_of(part * 768, 128), 768), :])
            return carry

        lax.fori_loop(0, 4, forward, 0, unroll=True)
        n2, scale2 = normalize(total[...])
        layer_out[rows, :] = (n2 * vec(vecs, "norm2_gain") + vec(vecs, "norm2_shift")).astype(low_type)
        grad = cotangent[rows, :].astype(f32)
        sums[5] += fold_rows(grad * n2)
        sums[6] += fold_rows(grad)
        sum_grad = norm_back(grad, n2, scale2, vec(vecs, "norm2_gain"))
        outer = sum_grad.astype(low_type)
        outer_low[rows, :] = outer
        sums[4] += fold_rows(outer.astype(f32))
        total[...] = sum_grad

        def backward(c, carry):
            g, part = lax.div(c, 2), lax.rem(c, 2)
            lanes = pl.ds(pl.multiple_of(g * 384, 128), 384)
            wide = pl.ds(pl.multiple_of(part * 768, 128), 768)
            here = pl.ds(pl.multiple_of(c * 768, 128), 768)
            grad_in = mm_nt(outer_low[rows, lanes], ffo_w[g, wide, :]) * slope[:, here]
            grad_low = grad_in.astype(low_type)
            inner[rows, here] = grad_low
            sums_in[:, here] += fold_rows(grad_low.astype(f32))
            total[:, lanes] += mm_nt(grad_low, in_w[g, :, wide])
            return carry

        lax.fori_loop(0, 4, backward, 0, unroll=True)
        normed_grad = total[...]
        n1 = unit1[...]
        sums[1] += fold_rows(normed_grad * n1)
        sums[2] += fold_rows(normed_grad)
        grad1 = norm_back(normed_grad, n1, scale1, vec(vecs, "norm1_gain"))
        residual_grad[rows, :] = grad1
        attn = grad1.astype(low_type)
        attn_low[rows, :] = attn
        sums[0] += fold_rows(attn.astype(f32))
        joined_grad[rows, :] = mm_nt(attn, out_w[...]).astype(low_type)
        return carry

    lax.fori_loop(0, 3, block, 0)

    for g in range(2):
        lanes = slice(g * 384, g * 384 + 384)

        def weights(m, carry, g=g, lanes=lanes):
            wide = pl.ds(pl.multiple_of(g * 1536 + m * 384, 128), 384)
            group = pl.ds(m * 8, 8)
            grad_out = mm_tn(active[:, wide], outer_low[:, lanes])
            units[group, g * 48 : g * 48 + 48, :] = grad_out.reshape(8, 48, 384).astype(low_type)
            grad_in = mm_tn(inner[:, wide], normed_low[:, lanes])
            units[group, 96 + g * 48 : 144 + g * 48, :] = grad_in.reshape(8, 48, 384).astype(low_type)
            return carry

        lax.fori_loop(0, 4, weights, 0, unroll=2)
    for m in range(2):
        grad_w = mm_tn(joined[:, m * 384 : m * 384 + 384], attn_low[...])
        halves = [grad_w[:, :384].reshape(16, 24, 384), grad_w[:, 384:].reshape(16, 24, 384)]
        units[m * 16 : m * 16 + 16, 192:240, :] = jnp.concatenate(halves, axis=1).astype(low_type)
    small[...] = jnp.zeros_like(small)
    row = 0
    for k, (name, count) in enumerate(SMALL2):
        if name == "ffn_in_bias":
            write_small(small, row, sums_in[...])
        else:
            write_small(small, row, sums[k])
        row += count


def ffn_call(*operands):
    shape = jax.ShapeDtypeStruct
    outs = (
        shape((768, D), low_type), shape((768, D), f32), shape((768, D), low_type),
        shape((32, 240, 384), low_type), shape((32, 384), f32),
    )
    return pl.pallas_call(
        ffn_kernel, out_shape=outs, in_specs=[VM] * len(operands), out_specs=(VM,) * len(outs),
        scratch_shapes=[
            pltpu.VMEM((768, 3072), low_type), pltpu.VMEM((768, 3072), low_type),
            pltpu.VMEM((768, D), low_type), pltpu.VMEM((768, D), low_type), pltpu.VMEM((768, D), low_type),
            pltpu.VMEM((TILE, 3072), f32), pltpu.VMEM((TILE, D), f32), pltpu.VMEM((TILE, D), f32),
            pltpu.VMEM((7, 8, D), f32), pltpu.VMEM((8, 3072), f32), pltpu.VMEM((1, VEC_TOTAL), f32),
        ],
        compiler_params=pltpu.CompilerParams(vmem_limit_bytes=60 << 20),
        name="ffn",
    )(*operands)


MESH = pl.DeviceIdType.MESH
CHUNK = 48


class Reducer:
    def __init__(self, dp_size, sources, kept, kept_sem, buffer, out, send, recv):
        self.bits = int(math.log2(dp_size)) + 1
        self.extra = max(0, self.bits - 5)
        self.nh = self.bits - self.extra
        self.dp = lax.axis_index("dp")
        self.br = lax.axis_index("branch")
        self.my = [self.br] + [lax.rem(lax.div(self.dp, 1 << (k - 1)), 2) for k in range(1, self.bits)]
        self.kept, self.kept_sem = kept, kept_sem
        self.buffer, self.out, self.send, self.recv = buffer, out, send, recv
        self.sources = [(ref, row) for ref in sources for row in range(0, ref.shape[1], CHUNK)]
        halving = list(range(self.extra, self.bits))
        first = [1] if 1 in halving else []
        r = [k for k in halving if k not in first]
        turns = [(0, 2, 1), (1, 2, 0), (0, 2, 1), (1, 2, 0), (2, 0, 1), (0, 2, 1), (1, 2, 0), (2, 1, 0)]
        self.orders = [first + [r[t] for t in turn] + r[3:] for turn in turns]

    def enter(self):
        barrier = pltpu.get_barrier_semaphore()
        for k in range(self.bits):
            pl.semaphore_signal(barrier, inc=1, device_id=self.partner(k), device_id_type=MESH)
        pl.semaphore_wait(barrier, self.bits)

    def partner(self, k):
        if k == 0:
            return (self.dp, 1 - self.br)
        return (self.dp + (1 << (k - 1)) * (1 - 2 * self.my[k]), self.br)

    def copy(self, src, dst, ssem, rsem, k):
        return pltpu.make_async_remote_copy(
            src_ref=src, dst_ref=dst, send_sem=ssem, recv_sem=rsem, device_id=self.partner(k), device_id_type=MESH
        )

    def offset(self, s):
        return sum(1 << (self.nh - 1 - t) for t in range(s))

    def place(self, u, free, fixed, value):
        index, at = 0, len(free) - 1
        for k in sorted(free + [fixed], reverse=True):
            if k == fixed:
                index = index * 2 + value
            else:
                index = index * 2 + ((u >> at) & 1)
                at -= 1
        return index

    def free(self, c, s):
        return sorted(self.orders[c][s + 1 :], reverse=True)

    def whole(self, c, s):
        part = self.buffer.at[c, pl.ds(self.offset(s), 1 << (self.nh - 1 - s))]
        return self.copy(part, part, self.send.at[c, s], self.recv.at[c, s], self.orders[c][s])

    def start(self, c, s):
        k, free = self.orders[c][s], self.free(c, s)
        for u in range(1 << len(free)):
            at = self.place(u, free, k, 1 - self.my[k])
            if s == 0:
                ref, row = self.sources[c]
                src = ref.at[at, pl.ds(row, CHUNK)]
            else:
                src = self.buffer.at[c, self.offset(s - 1) + at]
            self.copy(src, self.buffer.at[c, self.offset(s) + u], self.send.at[c, s], self.recv.at[c, s], k).start()

    def fetch(self, c):
        k, free = self.orders[c][0], self.free(c, 0)
        ref, row = self.sources[c]
        for u in range(1 << len(free)):
            at = self.place(u, free, k, self.my[k])
            pltpu.make_async_copy(ref.at[at, pl.ds(row, CHUNK)], self.kept.at[c, u], self.kept_sem.at[c]).start()

    def add(self, c, s):
        fetched = c < self.kept.shape[0]
        if s == 0 and fetched:
            pltpu.make_async_copy(self.kept.at[c], self.kept.at[c], self.kept_sem.at[c]).wait()
        self.whole(c, s).wait_recv()
        k, free = self.orders[c][s], self.free(c, s)
        for u in range(1 << len(free)):
            at = self.place(u, free, k, self.my[k])
            if s == 0 and fetched:
                mine = self.kept[c, u]
            elif s == 0:
                ref, row = self.sources[c]
                mine = ref[at, row : row + CHUNK, :]
            else:
                mine = self.buffer[c, self.offset(s - 1) + at]
            theirs = self.buffer[c, self.offset(s) + u]
            if s == self.nh - 1:
                self.out[c * CHUNK : (c + 1) * CHUNK, :] = mine.astype(f32) + theirs.astype(f32)
            else:
                self.buffer[c, self.offset(s) + u] = mine + theirs

    def step(self, c, s):
        if s > 0:
            self.add(c, s - 1)
        if s < self.nh:
            self.start(c, s)

    def drain(self):
        for c in range(len(self.sources)):
            for s in range(self.nh):
                self.whole(c, s).wait_send()


class Doubler:
    def __init__(self, reducer, value, sent, got, send, recv):
        self.reducer, self.value, self.sent, self.got, self.send, self.recv = reducer, value, sent, got, send, recv
        self.order = reducer.orders[0] + list(range(reducer.extra))

    def copy(self, s):
        return self.reducer.copy(self.sent, self.got.at[s], self.send.at[s], self.recv.at[s], self.order[s])

    def step(self, s):
        if s > 0:
            copy = self.copy(s - 1)
            copy.wait()
            self.value[...] = self.sent[...].astype(f32) + self.got[s - 1].astype(f32)
        if s < len(self.order):
            self.sent[...] = self.value[...].astype(self.sent.dtype)
            self.copy(s).start()


EARLY_STEPS = {
    (0, 1): [(0, 1), (1, 1)],
    (0, 2): [(2, 1), (3, 1)],
    (0, 3): [(4, 1)],
    (1, 2): [(0, 2), (1, 2)],
    (2, 1): [(2, 2), (3, 2), (4, 2)],
    (2, 3): [(0, 3), (1, 3)],
}


def back_kernel(
    dp_size, hidden_far, joined_grad_far, residual_grad_far, q_in_far, k_in_far, v_in_far, probs_far, conv_pad_far, taps, tap_mask, query_pre_far, key_conv_far, depth_low_far,
    conv_attn_far, units2, small2, query_w_far, key_w_far, value_w_far, point_w_far, conv_w_far, depth_w, kernel_w,
    grad_own, got_other, out, small_sum,
    dk_acc, dv_acc, k_t, dq_low, kvc, key_conv_low, dg_pad, cg_pad, x_pad, mask_cols, dw_acc, dq_t, kernel_acc, bias_acc, moved_taps, part,
    sums, grad_other, units, buffer, sent3, got3, extra_got,
    send, recv, send3, recv3, other_sem, extra_sem, kept, kept_sem,
    hidden, joined_grad, residual_grad, q_in, k_in, v_in, probs, conv_pad, query_pre, key_conv, depth_low, conv_attn,
    query_w, key_w, value_w, point_w, conv_w, load_sem, probs_sem,
):
    order = (
        (hidden_far, hidden), (k_in_far, k_in), (joined_grad_far, joined_grad), (q_in_far, q_in), (v_in_far, v_in),
        (conv_pad_far, conv_pad), (conv_attn_far, conv_attn), (query_pre_far, query_pre), (key_conv_far, key_conv), (point_w_far, point_w),
        (depth_low_far, depth_low), (key_w_far, key_w), (value_w_far, value_w), (conv_w_far, conv_w), (query_w_far, query_w),
        (residual_grad_far, residual_grad),
    )
    loads = [pltpu.make_async_copy(away, near, load_sem.at[n]) for n, (away, near) in enumerate(order)]

    def probs_load(i):
        heads = pl.ds(i * HEADS, HEADS)
        return pltpu.make_async_copy(probs_far.at[heads], probs.at[heads], probs_sem.at[i])

    for load in loads[:5]:
        load.start()
    for i in range(3):
        probs_load(i).start()
    for load in loads[5:]:
        load.start()
    reducer = Reducer(dp_size, (units2, units), kept, kept_sem, buffer, out, send, recv)
    nh, bits, extra = reducer.nh, reducer.bits, reducer.extra
    late = Doubler(reducer, small_sum, sent3, got3, send3, recv3)
    other_copy = reducer.copy(grad_other, got_other, other_sem.at[0], other_sem.at[1], 0)
    for c in range(5):
        reducer.fetch(c)
    reducer.enter()
    for c in range(5):
        reducer.step(c, 0)
    def run(steps):
        for c, stage in steps:
            reducer.step(c, stage)

    def advance_at(i, spot):
        for (n, at), steps in EARLY_STEPS.items():
            if at == spot:
                @pl.when(i == n)
                def _(steps=steps):
                    run(steps)

    b = lax.axis_index("branch")
    base = b * 512
    for ref in (dk_acc, dv_acc, dg_pad, cg_pad, dw_acc, kernel_acc, bias_acc, sums):
        ref[...] = jnp.zeros_like(ref)
    for c in range(D // 128):
        x_pad[c, 0:PAD, :] = jnp.zeros((PAD, 128), f32)
        x_pad[c, 1024 + PAD : 1024 + 2 * PAD, :] = jnp.zeros((PAD, 128), f32)

    def prepare(e, carry):
        rows = aligned(e * TILE, TILE)
        k_t[:, rows] = jnp.transpose(k_in[rows, :].astype(f32)).astype(low_type)
        x = hidden[aligned(base + e * TILE, TILE), :]
        place = pl.ds(pl.multiple_of(e * TILE + PAD, 8), TILE)
        for c in range(D // 128):
            x_pad[c, place, :] = x[:, c * 128 : c * 128 + 128].astype(f32)
        return carry

    for load in loads[:2]:
        load.wait()
    lax.fori_loop(0, 4, prepare, 0)
    kernel_rows = mm(tap_permutation().astype(low_type), kernel_w[...]).astype(low_type)
    depth_weights = [depth_w[j : j + 1, :].astype(f32) for j in range(KERNEL)]
    head_rows = head_spread(0)[:8]
    moved = []
    for j in range(KERNEL):
        rows = taps[(8 - j) * 8 : (8 - j) * 8 + 8, :]
        rows = rows if j == 4 else pltpu.roll(rows, (4 - j) % 1024, 1)
        moved.append(rows * tap_mask[j * 8 : j * 8 + 8, :])
    moved_taps[...] = jnp.transpose(jnp.concatenate(moved, axis=0)).astype(low_type)

    def own(i, carry):
        e = b + i
        rows = aligned(i * TILE, TILE)
        ext = aligned(e * TILE, TILE)
        place = pl.ds(pl.multiple_of(e * TILE + PAD, 8), TILE)
        keys = aligned(lax.div(e, 2) * 512, 512)
        probs_load(i).wait()
        d_ctx = joined_grad[rows, 0:WIDTH]
        d_ctx_t = jnp.transpose(d_ctx.astype(f32)).astype(low_type)
        for p in range(HEADS // 2):
            lanes = slice(p * 128, p * 128 + 128)
            v_pair = v_in[keys, lanes]
            q_pair = q_in[rows, lanes]
            d_pair = d_ctx[:, lanes]
            scores, weights = [], []
            for odd in range(2):
                h = 2 * p + odd
                weight = probs[i * HEADS + h]
                prob_grad = mm(v_pair, half_rows(d_ctx_t[lanes], odd))
                wide = weight.astype(f32)
                term = wide * prob_grad
                score = (term - wide * jnp.sum(term, axis=0, keepdims=True)).astype(low_type)
                dq_t[h * HEAD_DIM : (h + 1) * HEAD_DIM, :] = mm(k_t[h * HEAD_DIM : (h + 1) * HEAD_DIM, keys], score)
                scores.append(score)
                weights.append(weight)
            q_both = jnp.concatenate([half_lanes(q_pair, 0), half_lanes(q_pair, 1)], axis=0)
            d_both = jnp.concatenate([half_lanes(d_pair, 0), half_lanes(d_pair, 1)], axis=0)
            dk_acc[keys, lanes] += mm(jnp.concatenate(scores, axis=1), q_both)
            dv_acc[keys, lanes] += mm(jnp.concatenate(weights, axis=1), d_both)
            advance_at(i, p)
        query_low = (jnp.transpose(dq_t[...]) * 0.125).astype(low_type)

        grad = joined_grad[rows, WIDTH : 2 * WIDTH].astype(f32)
        for c in range(WIDTH // 128):
            cg_pad[c, place, :] = grad[:, c * 128 : c * 128 + 128]
        grads = []
        for j in range(KERNEL):
            pieces = [
                (grad[:, c * 128 : c * 128 + 128] * shifted(conv_pad, c, e * TILE, j, TILE)).astype(low_type)
                for c in range(WIDTH // 128)
            ]
            grads.append(mm_nt(head_rows, jnp.concatenate(pieces, axis=1)) * tap_mask[j * 8 : j * 8 + 8, ext])
        kept = taps[:, ext]
        level = functools.reduce(jnp.add, [grads[j] * kept[j * 8 : j * 8 + 8] for j in range(KERNEL)])
        logit = kept * jnp.concatenate([x - level for x in grads], axis=0)
        logit_low = logit.astype(low_type)
        logit_wide = logit_low.astype(f32)
        kernel_acc[...] += mm(logit_low, conv_attn[rows, :])
        bias_acc[...] += logit_wide[:, :128] + logit_wide[:, 128:]
        span = mm(jnp.transpose(logit_wide).astype(low_type), kernel_rows).astype(low_type).astype(f32)
        point_low = (span * query_pre[rows, :].astype(f32)).astype(low_type)
        query_conv = (span * key_conv[rows, :].astype(f32)).astype(low_type)
        key_conv_low[rows, :] = point_low
        sums[2] += fold_rows(point_low.astype(f32))
        both = query_low.astype(f32) + query_conv.astype(f32)
        sums[0] += fold_rows(both)
        dq_low[rows, :] = both.astype(low_type)
        d_depth = mm_nt(point_low, point_w[...])
        for c in range(D // 128):
            dg_pad[c, place, :] = d_depth[:, c * 128 : c * 128 + 128]
        mask_cols[...] = mm(jnp.transpose(tap_mask[:, ext]).astype(low_type), tap_spread())
        for c in range(D // 128):
            totals = [None] * KERNEL
            for lo in range(0, TILE, 64):
                grad_rows = dg_pad[c, pl.ds(e * TILE + (PAD + lo), 64), :]
                for j in range(KERNEL):
                    term = shifted(x_pad, c, e * TILE + lo, j, 64) * grad_rows
                    if j != KERNEL // 2:
                        term = term * mask_cols[lo : lo + 64, j * 128 : j * 128 + 128]
                    term = fold_rows(term)
                    totals[j] = term if lo == 0 else totals[j] + term
            for j in range(KERNEL):
                dw_acc[j, :, c * 128 : c * 128 + 128] += totals[j]
        advance_at(i, 3)
        return carry

    for load in loads[2:10]:
        load.wait()
    lax.fori_loop(0, 3, own, 0)
    for load in loads[10:]:
        load.wait()

    def settle(e, carry):
        ext = aligned(e * TILE, TILE)
        dv = dv_acc[ext, :].astype(low_type)
        kvc[ext, 0:WIDTH] = dk_acc[ext, :].astype(low_type)
        kvc[ext, WIDTH : 2 * WIDTH] = dv
        sums[1] += fold_rows(dv.astype(f32))
        return carry

    def pack(k, first, second):
        for m in range(2):
            lanes = slice(m * 384, m * 384 + 384)
            pieces = [part_of(lanes).reshape(16, 24, 384) for part_of in (first, second)]
            units[m * 16 : m * 16 + 16, k * 48 : k * 48 + 48, :] = jnp.concatenate(pieces, axis=1).astype(low_type)

    def token_grad(k):
        return lambda lanes: mm_tn(hidden[aligned(base, 512), lanes], kvc[0:512, k * WIDTH : (k + 1) * WIDTH]) + mm_tn(
            hidden[aligned(base + 512, 512), lanes], kvc[512:1024, k * WIDTH : (k + 1) * WIDTH]
        )

    lax.fori_loop(0, 4, settle, 0)
    own_tokens = pl.ds(pl.multiple_of(b * 768, 256), 768)
    pack(0, lambda lanes: mm_tn(hidden[own_tokens, lanes], dq_low[...]), token_grad(0))
    run([(5, 0), (4, 3)])
    depth_total = jnp.sum(dw_acc[...], axis=1)
    depth_t = jnp.transpose(jnp.concatenate([depth_total, jnp.zeros((128 - KERNEL, D), f32)], axis=0))
    pack(
        2,
        lambda lanes: mm_tn(depth_low[:, lanes], key_conv_low[...]),
        lambda lanes: jnp.concatenate([depth_t[lanes], jnp.zeros((384, 256), f32)], axis=1),
    )
    run([(7, 0), (2, 3), (3, 3), (0, 4), (1, 4)])

    def spans(e, carry):
        ext = aligned(e * TILE, TILE)
        dc = span_conv(cg_pad, moved_taps[ext, :], e * TILE).astype(low_type)
        kvc[ext, 2 * WIDTH : 3 * WIDTH] = dc
        sums[3] += fold_rows(dc.astype(f32))
        return carry

    lax.fori_loop(0, 4, spans, 0, unroll=2)
    run([(4, 4), (2, 4), (3, 4)])
    small_sum[...] = jnp.zeros_like(small_sum)
    small_sum[0:72, :] = kernel_acc[...]
    for k in range(4):
        small_sum[72 + k : 73 + k, :] = jnp.sum(sums[k], axis=0, keepdims=True)
    column = jnp.concatenate([bias_acc[...], jnp.zeros((56, 128), f32)], axis=0)
    small_sum[76:77, 0:128] = jnp.sum(jnp.transpose(column), axis=0, keepdims=True)
    small_sum[80:104, :] = small2[0:24, :]
    late.step(0)
    run([(5, 1), (7, 1)])
    pack(1, token_grad(1), token_grad(2))
    run([(6, 0)])
    late.step(1)
    def input_part(e):
        ext = aligned(e * TILE, TILE)
        mask_cols[...] = mm(jnp.transpose(tap_mask[:, ext]).astype(low_type), tap_spread())

        def keep(c, lo, value):
            part[lo : lo + 64, c * 128 : c * 128 + 128] = value

        depth_conv(dg_pad, mask_cols, depth_weights, e * TILE, keep, True)
        pieces = [kvc[ext, k * WIDTH : (k + 1) * WIDTH] for k in range(3)]
        return part[...] + mm_nt(pieces[0], key_w[...]) + mm_nt(pieces[1], value_w[...]) + mm_nt(pieces[2], conv_w[...])

    grad_other[...] = input_part(3 * (1 - b)).astype(low_type)
    run([(6, 1), (0, 5), (1, 5), (4, 5), (2, 5), (3, 5)])
    other_copy.start()

    def finish(i, carry):
        rows = aligned(i * TILE, TILE)
        @pl.when(i == 2)
        def _():
            late.step(2)
            run([(c, 2) for c in (5, 7, 6)])

        grad_own[rows, :] = input_part(b + i) + mm_nt(dq_low[rows, :], query_w[...]) + residual_grad[rows, :]
        return carry

    lax.fori_loop(0, 3, finish, 0)
    for stage in range(3, 6):
        late.step(stage)
        run([(c, stage) for c in (5, 7, 6)])
    for s in range(6, nh + 1):
        for c in range(8):
            reducer.step(c, s)
    for s in range(6, bits + 1):
        late.step(s)
    for k in range(extra):
        copy = reducer.copy(out, extra_got.at[k], extra_sem.at[2 * k], extra_sem.at[2 * k + 1], k)
        copy.start()
        copy.wait()
        out[...] = out[...] + extra_got[k]
    reducer.drain()
    other_copy.wait()


def back_call(dp_size, hidden, joined_grad, residual_grad, saved, units2, small2, weights):
    shape = jax.ShapeDtypeStruct
    outs = (shape((768, D), f32), shape((256, D), low_type), shape((384, 384), f32), shape((104, 384), f32))
    operands = (hidden, joined_grad, residual_grad) + tuple(saved) + (units2, small2) + tuple(weights)
    ext = 1024 + 2 * PAD
    bits = int(math.log2(dp_size)) + 1
    extra = max(0, bits - 5)
    nh = bits - extra
    dma = pltpu.SemaphoreType.DMA
    return pl.pallas_call(
        functools.partial(back_kernel, dp_size), out_shape=outs, in_specs=[ANY] * 8 + [VM] * 2 + [ANY] * 5 + [VM] + [ANY] * 5 + [VM] * 2, out_specs=(VM,) * len(outs),
        scratch_shapes=[
            pltpu.VMEM((1024, WIDTH), f32), pltpu.VMEM((1024, WIDTH), f32), pltpu.VMEM((WIDTH, 1024), low_type),
            pltpu.VMEM((768, WIDTH), low_type), pltpu.VMEM((1024, 3 * WIDTH), low_type), pltpu.VMEM((768, WIDTH), low_type),
            pltpu.VMEM((6, ext, 128), f32), pltpu.VMEM((3, ext, 128), f32), pltpu.VMEM((6, ext, 128), f32),
            pltpu.VMEM((TILE, KERNEL * 128), f32), pltpu.VMEM((KERNEL, 8, D), f32), pltpu.VMEM((WIDTH, TILE), f32),
            pltpu.VMEM((72, WIDTH), f32), pltpu.VMEM((72, 128), f32), pltpu.VMEM((1024, 72), low_type), pltpu.VMEM((TILE, D), f32),
            pltpu.VMEM((4, 8, WIDTH), f32),
            pltpu.VMEM((256, D), low_type), pltpu.VMEM((32, 144, 384), low_type),
            pltpu.VMEM((8, (1 << nh) - 1, CHUNK, 384), low_type),
            pltpu.VMEM((104, 384), low_type), pltpu.VMEM((bits, 104, 384), low_type),
            pltpu.VMEM((max(extra, 1), 384 if extra else 8, 384), f32),
            dma((8, nh)), dma((8, nh)), dma((bits,)), dma((bits,)), dma((2,)), dma((max(2 * extra, 2),)),
            pltpu.VMEM((5, 1 << (nh - 1), CHUNK, 384), low_type), dma((5,)),
        ] + [pltpu.VMEM(operands[n].shape, operands[n].dtype) for n in (0, 1, 2, 3, 4, 5, 6, 7, 10, 11, 12, 13, 16, 17, 18, 19, 20)] + [
            dma((16,)), dma((3,)),
        ],
        compiler_params=pltpu.CompilerParams(collective_id=0, has_side_effects=True, vmem_limit_bytes=67_000_000),
        name="mix_backward_reduce",
    )(*operands)


def exact_columns(table, rows):
    return lax.dot_general(table, rows, (((0,), (0,)), ((), ())), precision=lax.Precision.HIGHEST, preferred_element_type=f32)


FINAL_SMALL = (
    ("query_b", 72, 384), ("value_b", 73, 384), ("point_b", 74, 384), ("conv_b", 75, 384), ("out_b", 80, 768), ("gain1", 82, 768),
    ("shift1", 84, 768), ("in_b", 86, 3072), ("ffo_b", 94, 768), ("gain2", 96, 768), ("shift2", 98, 768),
)


def final_kernel(
    grad_own, got, total, small,
    input_grad, query_w, key_w, value_w, depth_w, point_w, kernel_w, kernel_b, conv_w, out_w, in_w, ffo_w, *vectors,
):
    b = lax.axis_index("branch")
    input_grad[...] = grad_own[...]
    rows = aligned((1 - b) * 512, 256)
    input_grad[rows, :] = grad_own[rows, :] + got[...].astype(f32)
    for ref, row in ((query_w, 240), (key_w, 264), (value_w, 288), (conv_w, 312), (point_w, 336)):
        ref[...] = total[row : row + 24, :]
    ffo_w[0] = total[0:48, :]
    ffo_w[1] = total[48:96, :]
    out_w[:, 0:384] = total[192:216, :]
    out_w[:, 384:768] = total[216:240, :]
    in_w[0] = total[96:144, :]
    in_w[1] = total[144:192, :]
    depth = jnp.concatenate([total[360:384, 0:128], jnp.zeros((104, 128), f32)], axis=0)
    depth_w[...] = jnp.transpose(depth)[0:KERNEL, 0:24]
    table = tap_permutation()
    kernel_w[...] = exact_columns(table, small[0:72, :])
    column = jnp.transpose(jnp.concatenate([small[76:77, 0:128]] * 128, axis=0))[0:72, :]
    kernel_b[...] = jnp.sum(column[:, 0:54] * table, axis=0, keepdims=True).reshape(54)
    for ref, (_, row, size) in zip(vectors, FINAL_SMALL):
        ref[...] = jnp.concatenate([small[row + k : row + k + 1, :] for k in range(size // 384)], axis=1).reshape(size)


def final_call(*operands):
    shape = lambda *s: jax.ShapeDtypeStruct(s, f32)
    outs = (
        shape(768, D), shape(24, 384), shape(24, 384), shape(24, 384), shape(KERNEL, 24), shape(24, 384), shape(54, 384), shape(54),
        shape(24, 384), shape(24, 768), shape(2, 48, 384), shape(2, 48, 384),
    ) + tuple(shape(size) for _, _, size in FINAL_SMALL)
    return pl.pallas_call(
        final_kernel, out_shape=outs, in_specs=[VM] * 4, out_specs=(VM,) * len(outs),
        compiler_params=pltpu.CompilerParams(vmem_limit_bytes=32 << 20), name="finish",
    )(*operands)


def local(
    hidden, segment_ids, query_weight, query_bias, key_weight, value_weight, value_bias, depthwise_weight,
    pointwise_weight, pointwise_bias, kernel_weight, kernel_bias, conv_value_weight, conv_value_bias, output_weight,
    output_bias, norm1_gain, norm1_shift, ffn_in_weight, ffn_in_bias, ffn_out_weight, ffn_out_bias, norm2_gain,
    norm2_shift, cotangent,
):
    dp_size = lax.axis_size("dp")
    branch = lax.axis_index("branch")
    kernel_rows = jnp.transpose(kernel_weight)
    joined, *saved = mix_call(
        hidden, segment_ids, query_weight, key_weight, value_weight, pointwise_weight, conv_value_weight,
        depthwise_weight, kernel_rows, query_bias, value_bias, pointwise_bias, conv_value_bias, kernel_bias,
    )
    layer_out, residual_grad, joined_grad, units2, small2 = ffn_call(
        hidden, joined, cotangent, output_weight, ffn_in_weight, ffn_out_weight, output_bias, norm1_gain, norm1_shift,
        ffn_in_bias, ffn_out_bias, norm2_gain, norm2_shift,
    )
    grad_own, got, out_sum, small_sum = back_call(
        dp_size, hidden, joined_grad, residual_grad, saved, units2, small2,
        (query_weight, key_weight, value_weight, pointwise_weight, conv_value_weight, depthwise_weight, kernel_rows),
    )
    share = 2 * dp_size // 32
    if share == 1:
        (
            input_grad, query_w, key_w, value_w, depth_w, point_w, kernel_w, kernel_b, conv_w, out_w, in_w, ffo_w,
            query_b, value_b, point_b, conv_b, out_b, gain1, shift1, in_b, ffo_b, gain2, shift2,
        ) = final_call(grad_own, got, out_sum, small_sum)
        return (
            layer_out, input_grad, query_w, query_b, key_w, value_w, value_b, depth_w, point_w, point_b, jnp.transpose(kernel_w),
            kernel_b, conv_w, conv_b, out_w, out_b, gain1, shift1, jnp.transpose(in_w, (0, 2, 1)), in_b, ffo_w, ffo_b, gain2, shift2,
        )
    start = (1 - branch) * 512
    block = lax.dynamic_slice_in_dim(grad_own, start, 256, 0) + got.astype(f32)
    input_grad = lax.dynamic_update_slice_in_dim(grad_own, block, start, 0)
    device = lax.axis_index("dp") * 2 + branch

    def piece(start, rows):
        n = rows // share
        return lax.dynamic_slice_in_dim(out_sum, start + lax.rem(device, share) * n, n, 0)

    def small(row, size):
        return small_sum[row : row + -(-size // 384)].reshape(-1)[:size]

    kern_w = jnp.transpose(small_sum[:72].reshape(9, 8, 384)[:, :6], (2, 1, 0)).reshape(384, 54)
    kern_b = jnp.transpose(small_sum[76, :72].reshape(9, 8)[:, :6]).reshape(54)
    in_g = jnp.stack([piece(96, 48), piece(144, 48)])
    return (
        layer_out,
        input_grad,
        piece(240, 24),
        small(72, 384),
        piece(264, 24),
        piece(288, 24),
        small(73, 384),
        jnp.transpose(piece(360, 24)[:, :KERNEL]),
        piece(336, 24),
        small(74, 384),
        kern_w,
        kern_b,
        piece(312, 24),
        small(75, 384),
        jnp.concatenate([piece(192, 24), piece(216, 24)], axis=1),
        small(80, 768),
        small(82, 768),
        small(84, 768),
        jnp.transpose(in_g, (0, 2, 1)),
        small(86, 3072),
        jnp.stack([piece(0, 48), piece(48, 48)]),
        small(94, 768),
        small(96, 768),
        small(98, 768),
    )


def solution(mesh):
    tokens, copied = P(("dp", "branch"), None), P()
    in_specs = (P("dp", None), P("dp", None)) + (copied,) * 22 + (tokens,)
    out_specs = (
        tokens, tokens, tokens, copied, tokens, tokens, copied, P(None, ("dp", "branch")), tokens, copied, copied, copied,
        tokens, copied, tokens, copied, copied, copied, P(None, None, ("dp", "branch")), copied,
        P(None, ("dp", "branch"), None), copied, copied, copied,
    )
    return jax.shard_map(local, mesh=mesh, in_specs=in_specs, out_specs=out_specs, check_vma=False)
```
